32 devices in a mesh: segment: 2 (over x), blk: 4 (over z), mp: 4 (over y, core).
Axes of the slice: x: 2, y: 2, z: 4, core: 2. Of those that a mesh axis runs over, the one named last changes fastest.
Arguments:
- segment_in: bfloat16 [2, 1024, 4096], P('segment', 'blk'), may hold values from -7.5 to 7.5
- norm_gains: float32 [2, 4096], P('segment'), may hold values from 0.25 to 1.75
- projections: bfloat16 [2, 4096, 2, 2048], P('segment', None, None, 'mp'), may hold values from -2 to 2
- live_counts: int32 [2, 4], P(None, 'blk'), may hold values from 1 to 256, 768 in all within a row
- cotangent: bfloat16 [1024, 4096], P('blk', 'mp'), may hold values from -6 to 6
Outputs:
- segment_out: bfloat16 [2, 1024, 4096], P('segment', 'blk', 'mp')
- state_grads: bfloat16 [2, 1024, 4096], P('segment', 'blk', 'mp')
The draws below stay inside these ranges and needn't reach their ends.
Inputs may be any that keep to these rules, and one draw needn't show every extreme that they name: `live_counts`: each row sums to 768; every entry is at least 1; each row has an entry equal to 256.
All inputs are finite; a program needn't handle non-finite values. No bound on the sum of `live_counts` on one device may be relied on, other than what follows from the above.
Results may differ from the reference program's by a relative error of at most 0.015.
Values may be sent and summed in bfloat16 or wider, within the bound.
No kernel may reach another device: no remote copies, remote signals or barrier semaphores. Data moves between devices by JAX's collectives and lax.ppermute only.
A program may use at most 128 MiB of HBM per device.

```python
import math
import jax
import jax.numpy as jnp
import numpy as np
from jax import lax

D = 4096
H = 32
DH = 64
B = 256
WIN = 4
C = 2048
ROWS = 1024
N_BLK = 4
N_MP = 4


def draw_segment_in(key, part):
    base = jax.random.fold_in(key, 7002)
    noise_key = jax.random.fold_in(base, 0)
    noise = jnp.clip(jax.random.normal(noise_key, (2, ROWS, D), jnp.float32), -6.0, 6.0)
    return noise.astype(jnp.bfloat16)


def draw_projections(key, part):
    base = jax.random.fold_in(key, 7003)
    weights = jnp.clip(jax.random.normal(base, (2, D, 2, C), jnp.float32), -6.0, 6.0) / jnp.sqrt(jnp.float32(D))
    return weights.astype(jnp.bfloat16)


def steps_of(own_key, extent, cuts, smallest, top_value):
    def one(axis_at, shards_of):
        steps = jax.random.uniform(jax.random.fold_in(jax.random.fold_in(own_key, 6), axis_at), (shards_of,), jnp.float32, smallest / len(cuts), top_value / len(cuts))
        return jnp.repeat(jnp.exp(steps), extent[axis_at] // shards_of).reshape((-1,) + (1,) * (len(extent) - axis_at - 1))

    loudness = one(*cuts[0])
    for cut in cuts[1:]:
        loudness = loudness * one(*cut)
    return loudness


def length_profile(amount, total, most, skew):
    portions = [(1 << 20) // math.isqrt(grade ** skew) + 1 for grade in range(2, amount + 1)]
    rest, counts = total - most - (amount - 1), [1] * (amount - 1)
    while rest > 0:
        free = [i for i in range(amount - 1) if counts[i] < most]
        mass, budget = sum([portions[i] for i in free]), rest
        for i in free:
            extra = min(most - counts[i], max(1, budget * portions[i] // mass), rest)
            counts[i] = counts[i] + extra
            rest = rest - extra
    return np.array([most] + counts)


def ragged(stream_key, amount, total, bound, slope):
    if amount == 2:
        one = jax.random.randint(stream_key, (), max(1, total - bound), min(bound, total - 1) + 1)
        return jnp.stack([one, total - one])
    sizes = jnp.asarray(length_profile(amount, total, bound, slope), jnp.int32)
    couples = (amount - 1) // 2
    source_of, receiver = sizes[1:1 + 2 * couples:2], sizes[2:2 + 2 * couples:2]
    room = jnp.minimum(source_of - 1, bound - receiver)
    passed = jax.random.randint(jax.random.fold_in(stream_key, 1), (couples,), 0, 1 << 20) % (room + 1)
    sizes = sizes.at[1:1 + 2 * couples:2].set(source_of - passed).at[2:2 + 2 * couples:2].set(receiver + passed)
    return sizes[jax.random.permutation(jax.random.fold_in(stream_key, 2), amount)]


def centred(stream_key, dims, scale, bound, cuts=(), held_as=jnp.bfloat16):
    array = jax.random.normal(stream_key, dims, jnp.float32) * scale
    if len(cuts) > 0:
        array = steps_of(stream_key, dims, cuts, -0.22, 0.18) * array
    return jnp.clip(array, min=-bound, max=bound).astype(held_as)


def setup_inputs(seed: int = 0) -> dict:
    seeds = jax.random.split(jax.random.key(seed), 6)
    segment_in = draw_segment_in(jax.random.fold_in(seeds[5], 71), 0)
    norm_gains = jnp.clip(1.0 + 0.15 * jax.random.normal(seeds[1], (2, D), jnp.float32), 0.25, 1.75)
    projections = draw_projections(jax.random.fold_in(seeds[5], 71), 0)
    live_counts = jax.vmap(lambda own: ragged(own, N_BLK, N_BLK * B * 3 // 4, B, 0))(jax.random.split(seeds[3], 2)).reshape((2, N_BLK)).astype(jnp.int32)
    cotangent = centred(seeds[4], (ROWS, D), 1.0, 6.0, ((0, 4), (1, 4)))
    return dict(segment_in=segment_in, norm_gains=norm_gains, projections=projections, live_counts=live_counts, cotangent=cotangent)


EPSILON = 1e-06
SCALE = 0.125
NEGATIVE = -1e+30

def normalize(states, gain_row):
    widened = states.astype(jnp.float32)
    spread = jnp.sqrt(lax.optimization_barrier(jnp.mean(widened * widened, axis=-1, keepdims=True)) + EPSILON)
    return ((widened / spread * gain_row).astype(jnp.bfloat16), spread)

def grouped_product(pairs):
    group_width = pairs[0][0].shape[1] // N_MP
    total = jnp.zeros((pairs[0][0].shape[0], pairs[0][1].shape[0]), jnp.float32)
    for group in range(N_MP):
        lower = group * group_width
        upper = lower + group_width
        partial_value = jnp.zeros_like(total)
        for left, right in pairs:
            partial_value = partial_value + jnp.dot(left[:, lower:upper], right[:, lower:upper].T, preferred_element_type=jnp.float32)
        rounded = lax.optimization_barrier(partial_value.astype(jnp.bfloat16))
        total = total + rounded.astype(jnp.float32)
    return total

def norm_backward(states, gain_row, spread, grad_normed):
    widened = states.astype(jnp.float32)
    row_term = lax.optimization_barrier(jnp.sum(grad_normed * gain_row * widened, axis=-1, keepdims=True))
    result = gain_row * grad_normed / spread - widened * row_term / (D * spread ** 3)
    return result.astype(jnp.bfloat16)

def reference(segment_in, norm_gains, projections, live_counts, cotangent):
    normed_doc, spread_doc = normalize(segment_in[0], norm_gains[0])
    normed_sum, spread_sum = normalize(segment_in[1], norm_gains[1])
    w_key = projections[0, :, 0, :]
    w_value = projections[0, :, 1, :]
    w_query = projections[1, :, 0, :]
    w_out = projections[1, :, 1, :]
    keys = jnp.dot(normed_doc, w_key, preferred_element_type=jnp.float32).astype(jnp.bfloat16)
    values = jnp.dot(normed_doc, w_value, preferred_element_type=jnp.float32).astype(jnp.bfloat16)
    queries = jnp.dot(normed_sum, w_query, preferred_element_type=jnp.float32).astype(jnp.bfloat16)
    position = jnp.arange(B, dtype=jnp.int32)
    doc_live = position[None, :] < live_counts[0][:, None]
    sum_live = position[None, :] < live_counts[1][:, None]
    grad_out = jnp.dot(cotangent, w_out, preferred_element_type=jnp.float32).astype(jnp.bfloat16)
    grad_out = jnp.where(sum_live.reshape(-1)[:, None], grad_out, jnp.zeros_like(grad_out))
    key_blocks = keys.reshape(N_BLK, B, H, DH)
    value_blocks = values.reshape(N_BLK, B, H, DH)
    query_blocks = queries.reshape(N_BLK, B, H, DH)
    grad_blocks = grad_out.reshape(N_BLK, B, H, DH)

    def block_step(carry, block):
        key_acc, value_acc = carry
        raw_order = block - jnp.arange(WIN, dtype=jnp.int32)
        present = raw_order >= 0
        order = jnp.maximum(raw_order, 0).astype(jnp.int32)
        win_keys = key_blocks[order].reshape(WIN * B, H, DH).astype(jnp.float32)
        win_values = value_blocks[order].reshape(WIN * B, H, DH).astype(jnp.float32)
        live = (doc_live[order] & present[:, None]).reshape(-1)
        query_rows = query_blocks[block].astype(jnp.float32)
        scores = jnp.einsum('qhd,khd->hqk', query_rows, win_keys) * SCALE
        scores = jnp.where(live[None, None, :], scores, NEGATIVE)
        row_max = lax.optimization_barrier(jnp.max(scores, axis=-1, keepdims=True))
        expo = jnp.exp(scores - row_max)
        probs = expo / lax.optimization_barrier(jnp.sum(expo, axis=-1, keepdims=True))
        probs_low = probs.astype(jnp.bfloat16).astype(jnp.float32)
        attended = jnp.einsum('hqk,khd->qhd', probs_low, win_values).astype(jnp.bfloat16)
        query_live = sum_live[block]
        attended = jnp.where(query_live[:, None, None], attended, jnp.zeros_like(attended))
        grad_rows = grad_blocks[block].astype(jnp.float32)
        grad_probs = jnp.einsum('qhd,khd->hqk', grad_rows, win_values)
        row_delta = lax.optimization_barrier(jnp.sum(probs * grad_probs, axis=-1, keepdims=True))
        grad_scores = (probs * (grad_probs - row_delta)).astype(jnp.bfloat16).astype(jnp.float32)
        grad_queries = (SCALE * jnp.einsum('hqk,khd->qhd', grad_scores, win_keys)).astype(jnp.bfloat16)
        key_part = (SCALE * jnp.einsum('hqk,qhd->khd', grad_scores, query_rows)).reshape(WIN, B, H, DH)
        value_part = jnp.einsum('hqk,qhd->khd', probs_low, grad_rows).reshape(WIN, B, H, DH)
        key_acc = key_acc.at[order].add(key_part)
        value_acc = value_acc.at[order].add(value_part)
        return ((key_acc, value_acc), (attended, grad_queries))
    empty = jnp.zeros((N_BLK, B, H, DH), jnp.float32)
    (key_acc, value_acc), (attended, grad_queries) = lax.scan(block_step, (empty, empty), jnp.arange(N_BLK, dtype=jnp.int32))
    attended = attended.reshape(ROWS, H * DH)
    grad_queries = grad_queries.reshape(ROWS, H * DH)
    grad_keys = key_acc.reshape(ROWS, H * DH).astype(jnp.bfloat16)
    grad_values = value_acc.reshape(ROWS, H * DH).astype(jnp.bfloat16)
    layer_out = grouped_product([(attended, w_out)]).astype(jnp.bfloat16)
    grad_doc = grouped_product([(grad_keys, w_key), (grad_values, w_value)])
    grad_sum = grouped_product([(grad_queries, w_query)])
    segment_out = jnp.stack([normed_doc, layer_out])
    state_grads = jnp.stack([norm_backward(segment_in[0], norm_gains[0], spread_doc, grad_doc), norm_backward(segment_in[1], norm_gains[1], spread_sum, grad_sum)])
    return (segment_out, state_grads)
```

```python
import functools

import jax
import jax.numpy as jnp
from jax import lax
from jax.experimental import pallas as pl
from jax.experimental.pallas import tpu as pltpu
from jax.sharding import PartitionSpec as P

DH = 64
WIN = 4


EPSILON = 1e-06
SCALE = 0.125
NEGATIVE = -1e30
LANES = 128
TAIL = 16
AXES = ("segment", "blk", "mp")

F32 = jnp.float32
BF16 = jnp.bfloat16


def from_behind(x, axis, by):
    size = lax.axis_size(axis)
    pairs = [(i, i + by) for i in range(size) if 0 <= i + by < size]
    return lax.ppermute(x, axis, pairs)


def normalize(states, gain_row):
    widened = states.astype(jnp.float32)
    spread = jnp.sqrt(jnp.mean(widened * widened, axis=-1, keepdims=True) + EPSILON)
    return ((widened / spread * gain_row).astype(jnp.bfloat16), spread)


def right_product(left, right):
    return lax.dot_general(
        left, right, (((1,), (1,)), ((), ())), preferred_element_type=jnp.float32
    )


def per_device_windows(segment_in, norm_gains, projections, live_counts, cotangent):
    segment_pos = lax.axis_index("segment")
    model_index = lax.axis_index("mp")
    states = segment_in[0]
    gain_row = norm_gains[0]
    row_count, full_width = states.shape
    feature_width = cotangent.shape[1]
    w_primary = projections[0, :, 0, :]
    w_secondary = projections[0, :, 1, :]
    group_width = w_primary.shape[1]
    group_heads = group_width // DH
    normed, spread = normalize(states, gain_row)
    primary = jnp.dot(normed, w_primary, preferred_element_type=jnp.float32).astype(jnp.bfloat16)
    secondary = lax.cond(
        segment_pos == 0,
        lambda: jnp.dot(normed, w_secondary, preferred_element_type=jnp.float32).astype(
            jnp.bfloat16
        ),
        lambda: jnp.zeros_like(primary),
    )
    doc_keys, doc_values = from_behind((primary, secondary), "segment", 1)
    own_block = (doc_keys, doc_values, live_counts[0])
    window = [own_block]
    moving = own_block
    for offset in range(1, WIN):
        moving = from_behind((moving[0], moving[1], moving[2]), "blk", 1)
        window.append(moving)
    position = jnp.arange(row_count, dtype=jnp.int32)
    all_keys = jnp.concatenate([piece[0] for piece in window], 0).reshape(
        WIN * row_count, group_heads, DH
    )
    all_values = jnp.concatenate([piece[1] for piece in window], 0).reshape(
        WIN * row_count, group_heads, DH
    )
    key_live = jnp.concatenate([position < piece[2][0] for piece in window], 0)
    query_live = position < live_counts[1][0]
    query_heads = primary.reshape(row_count, group_heads, DH)
    scores = (
        jnp.einsum("qhd,khd->hqk", query_heads, all_keys, preferred_element_type=jnp.float32)
        * SCALE
    )
    scores = jnp.where(key_live[None, None, :], scores, NEGATIVE)
    row_max = jnp.max(scores, axis=-1, keepdims=True)
    expo = jnp.exp(scores - row_max)
    row_total = jnp.sum(expo, axis=-1, keepdims=True)
    softmax_out = expo / row_total
    weights_low = softmax_out.astype(jnp.bfloat16)
    attended = jnp.einsum(
        "hqk,khd->qhd", weights_low, all_values, preferred_element_type=jnp.float32
    ).astype(jnp.bfloat16)
    attended = jnp.where(query_live[:, None, None], attended, jnp.zeros_like(attended)).reshape(
        row_count, group_width
    )
    projected = lax.cond(
        segment_pos == 1,
        lambda: right_product(attended, w_secondary),
        lambda: jnp.zeros((row_count, full_width), jnp.float32),
    )
    layer_out = lax.psum_scatter(
        projected.astype(jnp.bfloat16), "mp", scatter_dimension=1, tiled=True
    )
    own_normed = lax.dynamic_slice_in_dim(normed, model_index * feature_width, feature_width, 1)
    segment_out = jnp.where(segment_pos == 0, own_normed, layer_out)[None]
    grad_out = jnp.dot(
        lax.all_gather(cotangent, "mp", axis=1, tiled=True),
        w_secondary,
        preferred_element_type=jnp.float32,
    )
    grad_out = grad_out.astype(jnp.bfloat16)
    grad_out = jnp.where(query_live[:, None], grad_out, jnp.zeros_like(grad_out))
    grad_heads = grad_out.reshape(row_count, group_heads, DH)
    grad_probs = jnp.einsum(
        "qhd,khd->hqk", grad_heads, all_values, preferred_element_type=jnp.float32
    )
    row_delta = jnp.sum(softmax_out * grad_probs, axis=-1, keepdims=True)
    grad_scores = (softmax_out * (grad_probs - row_delta)).astype(jnp.bfloat16)
    grad_queries = (
        (
            SCALE
            * jnp.einsum("hqk,khd->qhd", grad_scores, all_keys, preferred_element_type=jnp.float32)
        )
        .astype(jnp.bfloat16)
        .reshape(row_count, group_width)
    )
    key_parts = (
        SCALE
        * jnp.einsum("hqk,qhd->khd", grad_scores, query_heads, preferred_element_type=jnp.float32)
    ).reshape(WIN, row_count, group_width)
    value_parts = jnp.einsum(
        "hqk,qhd->khd", weights_low, grad_heads, preferred_element_type=jnp.float32
    ).reshape(WIN, row_count, group_width)
    key_total = key_parts[WIN - 1]
    value_total = value_parts[WIN - 1]
    for offset in range(WIN - 2, -1, -1):
        arrived = (
            from_behind(key_total.astype(jnp.bfloat16), "blk", -1).astype(key_total.dtype),
            from_behind(value_total.astype(jnp.bfloat16), "blk", -1).astype(value_total.dtype),
        )
        key_total = arrived[0] + key_parts[offset]
        value_total = arrived[1] + value_parts[offset]
    grad_keys = key_total.astype(jnp.bfloat16)
    grad_values = value_total.astype(jnp.bfloat16)
    back_keys, back_values = from_behind((grad_keys, grad_values), "segment", -1)
    partial_grad = lax.cond(
        segment_pos == 0,
        lambda: right_product(back_keys, w_primary) + right_product(back_values, w_secondary),
        lambda: right_product(grad_queries, w_primary),
    )
    widened = states.astype(jnp.float32)
    summed = lax.psum_scatter(
        partial_grad.astype(jnp.bfloat16), "mp", scatter_dimension=1, tiled=True
    ).astype(jnp.float32)
    own_states = lax.dynamic_slice_in_dim(widened, model_index * feature_width, feature_width, 1)
    own_gain = lax.dynamic_slice_in_dim(gain_row, model_index * feature_width, feature_width, 0)
    row_term = lax.psum(jnp.sum(summed * own_gain * own_states, axis=-1, keepdims=True), "mp")
    input_grad = (
        own_gain * summed / spread - own_states * row_term / (full_width * spread**3)
    ).astype(jnp.bfloat16)
    return (segment_out, input_grad[None])


def full_spec(shape):
    return pl.BlockSpec(shape, lambda *_: (0,) * len(shape))


def low_half(shape):
    return lax.broadcasted_iota(jnp.int32, shape, 1) < DH


def enter_kernel(info, states, gain, w, wp, ws, own, spread, prim, sec, normed, mix, pacc, sacc):
    step = pl.program_id(0)
    rows, width = states.shape
    depth = wp.shape[0]
    tiles = wp.shape[1] // LANES
    pack = 2 * tiles
    group = 2 * LANES // pack
    out_width = own.shape[1]

    @pl.when(step == 0)
    def _():
        here = lax.broadcasted_iota(jnp.int32, mix.shape, 0)
        there = lax.broadcasted_iota(jnp.int32, mix.shape, 1)
        source = pack * lax.rem(here, group) + lax.div(here, group)
        mix[...] = jnp.where(there == source, 1.0, 0.0).astype(BF16)
        pacc[...] = jnp.zeros_like(pacc)
        sacc[...] = jnp.zeros_like(sacc)
        chunk = 16

        def norm_rows(at, _):
            line = pl.ds(pl.multiple_of(at * chunk, chunk), chunk)
            wide = states[line, :].astype(F32)
            mean = jnp.sum(wide * wide, axis=1, keepdims=True) * (1.0 / width)
            root = jnp.sqrt(mean + EPSILON)
            normed[line, :] = (wide * (1.0 / root) * gain[...]).astype(BF16)
            spread[line, :] = jnp.broadcast_to(root, (chunk, LANES))
            return 0

        lax.fori_loop(0, rows // chunk, norm_rows, 0)
        own[...] = normed[:, pl.ds(pl.multiple_of(info[1] * out_width, out_width), out_width)]

    for pair in range(depth // (2 * group)):
        base = pair * 4 * LANES
        left = w[base : base + 2 * LANES, :]
        right = w[base + 2 * LANES : base + 4 * LANES, :]
        both = jnp.concatenate([left, right], axis=1)
        sorted_rows = jnp.dot(mix[...], both, preferred_element_type=F32).astype(BF16)
        for slot in range(pack):
            target = (wp, ws)[slot % 2]
            tile = slice(slot // 2 * LANES, (slot // 2 + 1) * LANES)
            part = sorted_rows[slot * group : (slot + 1) * group, :]
            first = 2 * pair * group
            target[first : first + group, tile] = part[:, :LANES]
            target[first + group : first + 2 * group, tile] = part[:, LANES:]
    piece = normed[:, pl.ds(pl.multiple_of(step * depth, depth), depth)]
    pacc[...] += jnp.dot(piece, wp[...], preferred_element_type=F32)

    @pl.when(info[2] == 0)
    def _():
        sacc[...] += jnp.dot(piece, ws[...], preferred_element_type=F32)

    @pl.when(step == pl.num_programs(0) - 1)
    def _():
        prim[...] = pacc[...].astype(BF16)
        sec[...] = sacc[...].astype(BF16)


def pack_kernel(heads, info, prim, sec, c0, c1, c2, c3, ws, *rest):
    outs, (second, acc, parts) = rest[:heads], rest[heads:]
    step = pl.program_id(0)
    rows = prim.shape[0]

    @pl.when(info[2] == 1)
    def _():
        for at, cot in enumerate((c0, c1, c2, c3)):

            @pl.when(step == at)
            def _():
                term = jnp.dot(cot[...], ws[...], preferred_element_type=F32)
                if at == 0:
                    acc[...] = term
                else:
                    acc[...] += term

    @pl.when(step == pl.num_programs(0) - 1)
    def _():
        @pl.when(info[2] == 0)
        def _():
            second[...] = sec[...]

        @pl.when(info[2] == 1)
        def _():
            line = lax.broadcasted_iota(jnp.int32, acc.shape, 0)
            second[...] = jnp.where(line < info[4], acc[...], 0.0).astype(BF16)

        count = info[3].astype(F32)
        tail = jnp.full((TAIL, LANES), 1.0, F32) * count
        for head in range(heads):
            cols = slice(head * DH, (head + 1) * DH)
            parts[head, :rows, :] = jnp.concatenate([prim[:, cols], second[:, cols]], axis=1)
            parts[head, rows:, :] = tail.astype(BF16)
        for k, out in enumerate(outs):
            out[...] = parts[jnp.bitwise_xor(info[0], k)]


def attend_kernel(heads, info, *rest):
    ins, outs = rest[:heads], rest[heads : 2 * heads]
    parts, back, grads = rest[2 * heads :]
    rows = outs[0].shape[0]
    blocks = heads // 2
    for k, piece in enumerate(ins):
        parts[jnp.bitwise_xor(info[0], k)] = piece[...]
    low = low_half((rows, LANES))
    zero = jnp.zeros((rows, LANES), BF16)
    position = lax.broadcasted_iota(jnp.int32, (1, rows), 1).astype(F32)
    tall_low = lax.broadcasted_iota(jnp.int32, (LANES, rows), 0) < DH
    keys, values, live = [], [], []
    for j in range(blocks):
        pair = parts[j, :rows, :]
        keys.append(jnp.where(low, pair * BF16(SCALE), zero))
        values.append(jnp.where(low, zero, pair))
        count = parts[j, rows : rows + 1, :].astype(F32)
        live.append(position < jnp.concatenate([count] * (rows // LANES), axis=1))
    for i in range(blocks):
        both = parts[blocks + i, :rows, :]
        query = jnp.where(low, both * BF16(SCALE), zero)
        grad = jnp.where(low, zero, both)
        left = jnp.concatenate([query, grad], axis=0)
        scores, grad_probs = [], []
        for j in range(i + 1):
            product = right_product(left, parts[j, :rows, :])
            scores.append(jnp.where(live[j], product[:rows], NEGATIVE))
            grad_probs.append(product[rows:])
        top = functools.reduce(jnp.maximum, scores)
        top = jnp.max(top, axis=1, keepdims=True)
        expo = [jnp.exp(s - top) for s in scores]
        total = jnp.sum(functools.reduce(jnp.add, expo), axis=1, keepdims=True)
        share = 1.0 / total
        probs = [e * share for e in expo]
        delta = functools.reduce(jnp.add, [p * g for p, g in zip(probs, grad_probs)])
        delta = jnp.sum(delta, axis=1, keepdims=True)
        flipped = both.astype(F32).T
        flip_query = jnp.where(tall_low, flipped * SCALE, 0.0).astype(BF16)
        flip_grad = jnp.where(tall_low, 0.0, flipped).astype(BF16)
        outgoing = jnp.zeros((rows, LANES), F32)
        for j in range(i + 1):
            probs_low = probs[j].astype(BF16)
            grad_scores = (probs[j] * (grad_probs[j] - delta)).astype(BF16)
            outgoing += jnp.dot(grad_scores, keys[j], preferred_element_type=F32)
            outgoing += jnp.dot(probs_low, values[j], preferred_element_type=F32)
            tall = jnp.dot(flip_query, grad_scores, preferred_element_type=F32)
            tall += jnp.dot(flip_grad, probs_low, preferred_element_type=F32)
            if i == j:
                grads[j] = tall
            else:
                grads[j] += tall
        back[blocks + i] = outgoing.astype(BF16)
    for j in range(blocks):
        back[j] = grads[j].T.astype(BF16)
    for k, out in enumerate(outs):
        out[...] = back[jnp.bitwise_xor(info[0], k)]


def gather_heads(heads, info, ins, parts, lp, ls):
    for k, piece in enumerate(ins):
        parts[jnp.bitwise_xor(info[0], k)] = piece[...]
    for head in range(heads):
        cols = slice(head * DH, (head + 1) * DH)
        lp[:, cols] = parts[head, :, :DH]
        ls[:, cols] = parts[head, :, DH:]

    @pl.when(info[2] == 1)
    def _():
        line = lax.broadcasted_iota(jnp.int32, ls.shape, 0)
        ls[...] = jnp.where(line < info[4], ls[...].astype(F32), 0.0).astype(BF16)


def project_block(info, wp, ws, lp, ls, out, out2):
    first = right_product(lp[...], wp[...])
    second = right_product(ls[...], ws[...])
    rows = first.shape[0]

    @pl.when(info[2] == 0)
    def _():
        out[0, :rows, :] = (first + second).astype(BF16)

    @pl.when(info[2] == 1)
    def _():
        out[0, :rows, :] = first.astype(BF16)
        out2[0] = second.astype(BF16)


def split_rows(column):
    row = jnp.broadcast_to(column, (column.shape[0], LANES)).T[:TAIL, :]
    high = row.astype(BF16).astype(F32)
    line = lax.broadcasted_iota(jnp.int32, row.shape, 0)
    return jnp.where(line == 0, high, row - high).astype(BF16)


def send_kernel(heads, info, prim, sec, spread, wp, ws, *rest):
    ins, (out, out2, lp_out, ls_out), (parts, tail) = rest[:heads], rest[heads : heads + 4], rest[heads + 4 :]
    rows = prim.shape[0]

    @pl.when(pl.program_id(0) == 0)
    def _():
        gather_heads(heads, info, ins, parts, lp_out, ls_out)
        term = lp_out[...].astype(F32) * prim[...].astype(F32)
        other = ls_out[...].astype(F32) * sec[...].astype(F32)
        term = term + jnp.where(info[2] == 0, other, 0.0)
        column = jnp.sum(term, axis=1, keepdims=True) * spread[:, :1]
        tail[...] = jnp.zeros_like(tail)
        tail[:, :rows] = split_rows(column)

    project_block(info, wp, ws, lp_out, ls_out, out, out2)
    out[0, rows:, :] = tail[...]


def keep_kernel(info, lp, ls, wp, ws, out, out2):
    project_block(info, wp, ws, lp, ls, out, out2)


def fold_kernel(info, keep, got, sent, keep2, got2, out, out2):
    rows = keep.shape[1]
    out[:rows, :] = (keep[0].astype(F32) + got[0, :rows, :].astype(F32)).astype(BF16)
    mine = sent[0].astype(F32)
    theirs = got[0, rows:, :].astype(F32)
    total = mine[0:1] + mine[1:2] + theirs[0:1] + theirs[1:2]
    total = jnp.broadcast_to(total, mine.shape)
    high = total.astype(BF16).astype(F32)
    line = lax.broadcasted_iota(jnp.int32, mine.shape, 0)
    out[rows:, :] = jnp.where(line == 0, high, total - high).astype(BF16)

    @pl.when(info[2] == 1)
    def _():
        out2[...] = (keep2[0].astype(F32) + got2[0].astype(F32)).astype(BF16)


def leave_kernel(info, full_width, keep, got, half, far, keep2, got2, far2, states, gain, spread, own, out, grad):
    rows = keep.shape[1]
    total = keep[0].astype(F32) + got[0].astype(F32) + far[:rows, :].astype(F32)
    ends = half[...].astype(F32) + far[rows:, :].astype(F32)
    row = jnp.broadcast_to(ends[0:1, :rows] + ends[1:2, :rows], (LANES, rows))
    term = row.T[:, :1]
    root = spread[:, :1]
    scaled = term / (full_width * root * root * root)
    wide = states[...].astype(F32)
    grad[...] = (gain[...] * total * (1.0 / root) - wide * scaled).astype(BF16)

    @pl.when(info[2] == 0)
    def _():
        out[...] = own[...]

    @pl.when(info[2] == 1)
    def _():
        layer = keep2[0].astype(F32) + got2[0].astype(F32) + far2[...].astype(F32)
        out[...] = layer.astype(BF16)


def call(body, grid, ins, in_specs, outs, out_specs, scratch=(), name=None):
    return pl.pallas_call(
        body,
        grid_spec=pltpu.PrefetchScalarGridSpec(
            num_scalar_prefetch=1,
            grid=grid,
            in_specs=in_specs,
            out_specs=out_specs,
            scratch_shapes=list(scratch),
        ),
        out_shape=[jax.ShapeDtypeStruct(s, d) for s, d in outs],
        compiler_params=pltpu.CompilerParams(vmem_limit_bytes=56 << 20),
        name=name,
    )(*ins)


def per_device_heads(sizes, segment_in, norm_gains, projections, live_counts, cotangent):
    n_seg, n_blk, n_mp = sizes
    heads = n_seg * n_blk
    seg = lax.axis_index("segment")
    model = lax.axis_index("mp")
    entry = seg * n_blk + lax.axis_index("blk")
    states = segment_in[0]
    rows, width = states.shape
    feats = cotangent.shape[1]
    group = projections.shape[3]
    where = lax.iota(jnp.int32, 8)
    info = jnp.where(where == 0, entry, jnp.where(where == 1, model, seg))
    info = jnp.where(where == 3, live_counts[0, 0], info)
    info = jnp.where(where == 4, live_counts[1, 0], info)

    def swap(x, over_heads, over_mp, least=0):
        pairs = [
            (e * n_mp + m, (e ^ over_heads) * n_mp + (m ^ over_mp))
            for e in range(least * n_blk, heads)
            for m in range(n_mp)
        ]
        return lax.ppermute(x, AXES, pairs)

    far_cot = swap(cotangent, 0, 2)
    near_cot = swap(cotangent, 0, 1)
    tiles = group // LANES
    mixed = projections.reshape(width, 2, tiles, LANES).transpose(0, 2, 1, 3)
    mixed = mixed.reshape(width * 2 * tiles, LANES)
    depth = 512
    wp, ws, own, spread, prim, sec = call(
        enter_kernel,
        (width // depth,),
        (info, states, norm_gains, mixed),
        [
            full_spec((rows, width)),
            full_spec((1, width)),
            pl.BlockSpec((depth * 2 * tiles, LANES), lambda i, _: (i, 0)),
        ],
        [
            ((width, group), BF16),
            ((width, group), BF16),
            ((rows, feats), BF16),
            ((rows, LANES), F32),
            ((rows, group), BF16),
            ((rows, group), BF16),
        ],
        [
            pl.BlockSpec((depth, group), lambda i, _: (i, 0)),
            pl.BlockSpec((depth, group), lambda i, _: (i, 0)),
            full_spec((rows, feats)),
            full_spec((rows, LANES)),
            full_spec((rows, group)),
            full_spec((rows, group)),
        ],
        [
            pltpu.VMEM((rows, width), BF16),
            pltpu.VMEM((2 * LANES, 2 * LANES), BF16),
            pltpu.VMEM((rows, group), F32),
            pltpu.VMEM((rows, group), F32),
        ],
        "enter",
    )
    cross_cot = swap(far_cot, 0, 1)
    pieces = call(
        functools.partial(pack_kernel, heads),
        (n_mp,),
        (info, prim, sec, cotangent, near_cot, far_cot, cross_cot, ws),
        [full_spec((rows, group))] * 2
        + [full_spec((rows, feats))] * 4
        + [pl.BlockSpec((feats, group), lambda i, info: (jnp.bitwise_xor(info[1], i), 0))],
        [((rows + TAIL, LANES), BF16)] * heads,
        [full_spec((rows + TAIL, LANES))] * heads,
        [
            pltpu.VMEM((rows, group), BF16),
            pltpu.VMEM((rows, group), F32),
            pltpu.VMEM((heads, rows + TAIL, LANES), BF16),
        ],
        "pack",
    )
    pieces = [pieces[0]] + [swap(pieces[k], k, 0) for k in range(1, heads)]
    pieces = call(
        functools.partial(attend_kernel, heads),
        (1,),
        (info, *pieces),
        [full_spec((rows + TAIL, LANES))] * heads,
        [((rows, LANES), BF16)] * heads,
        [full_spec((rows, LANES))] * heads,
        [
            pltpu.VMEM((heads, rows + TAIL, LANES), BF16),
            pltpu.VMEM((heads, rows, LANES), BF16),
            pltpu.VMEM((n_blk, LANES, rows), F32),
        ],
        "attend",
    )
    pieces = [pieces[0]] + [swap(pieces[k], k, 0) for k in range(1, heads)]

    def weight_spec(first, second):
        return pl.BlockSpec(
            (feats, group),
            lambda i, info: (jnp.bitwise_xor(info[1], jnp.where(i == 0, first, second)), 0),
        )

    sent, sent2, lp, ls = call(
        functools.partial(send_kernel, heads),
        (2,),
        (info, prim, sec, spread, wp, ws, *pieces),
        [full_spec((rows, group))] * 2
        + [full_spec((rows, LANES))]
        + [weight_spec(3, 1)] * 2
        + [full_spec((rows, LANES))] * heads,
        [
            ((2, rows + TAIL, feats), BF16),
            ((2, rows, feats), BF16),
            ((rows, group), BF16),
            ((rows, group), BF16),
        ],
        [
            pl.BlockSpec((1, rows + TAIL, feats), lambda i, _: (i, 0, 0)),
            pl.BlockSpec((1, rows, feats), lambda i, _: (i, 0, 0)),
            full_spec((rows, group)),
            full_spec((rows, group)),
        ],
        [pltpu.VMEM((heads, rows, LANES), BF16), pltpu.VMEM((TAIL, feats), BF16)],
        "send",
    )
    got = swap(sent, 0, 1)
    got2 = swap(sent2, 0, 1, 1)
    keep, keep2 = call(
        keep_kernel,
        (2,),
        (info, lp, ls, wp, ws),
        [full_spec((rows, group))] * 2 + [weight_spec(2, 0)] * 2,
        [((2, rows, feats), BF16)] * 2,
        [pl.BlockSpec((1, rows, feats), lambda i, _: (i, 0, 0))] * 2,
        (),
        "keep",
    )

    def block(at, length=rows, start=0):
        return pl.BlockSpec((1, length, feats), lambda i, _: (at, start, 0))

    fold, fold2 = call(
        fold_kernel,
        (1,),
        (info, keep, got, sent, keep2, got2),
        [block(0), block(0, rows + TAIL), block(0, TAIL, rows // TAIL), block(0), block(0)],
        [((rows + TAIL, feats), BF16), ((rows, feats), BF16)],
        [full_spec((rows + TAIL, feats)), full_spec((rows, feats))],
        (),
        "fold",
    )
    far = swap(fold, 0, 2)
    far2 = swap(fold2, 0, 2, 1)
    out, grad = call(
        lambda info, *refs: leave_kernel(info, width, *refs),
        (1,),
        (info, keep, got, fold, far, keep2, got2, far2, states, norm_gains, spread, own),
        [
            block(1),
            block(1),
            pl.BlockSpec((TAIL, feats), lambda i, _: (rows // TAIL, 0)),
            full_spec((rows + TAIL, feats)),
            block(1),
            block(1),
            full_spec((rows, feats)),
            pl.BlockSpec((rows, feats), lambda i, info: (0, info[1])),
            pl.BlockSpec((1, feats), lambda i, info: (0, info[1])),
            full_spec((rows, LANES)),
            full_spec((rows, feats)),
        ],
        [((rows, feats), BF16)] * 2,
        [full_spec((rows, feats))] * 2,
        (),
        "leave",
    )
    return (out[None], grad[None])


def solution(mesh):
    sizes = tuple(mesh.shape[axis] for axis in AXES)
    n_seg, n_blk, n_mp = sizes

    def body(segment_in, norm_gains, projections, live_counts, cotangent):
        heads = projections.shape[3] // DH
        rows = segment_in.shape[1]
        power = heads & (heads - 1) == 0
        fits = n_seg == 2 and n_seg * n_blk == heads and power and n_blk <= WIN
        if fits and n_mp == 4 and rows % LANES == 0 and projections.shape[3] == 4 * LANES:
            form = functools.partial(per_device_heads, sizes)
        else:
            form = per_device_windows
        return form(segment_in, norm_gains, projections, live_counts, cotangent)

    in_specs = (
        P("segment", "blk", None),
        P("segment", None),
        P("segment", None, None, "mp"),
        P(None, "blk"),
        P("blk", "mp"),
    )
    out_specs = (P("segment", "blk", "mp"), P("segment", "blk", "mp"))
    return jax.shard_map(body, mesh=mesh, in_specs=in_specs, out_specs=out_specs, check_vma=False)
```

```python
import functools

import jax
import jax.numpy as jnp
from jax import lax
from jax.experimental import pallas as pl
from jax.experimental.pallas import tpu as pltpu
from jax.sharding import PartitionSpec as P

DH = 64
WIN = 4


EPSILON = 1e-06
SCALE = 0.125
NEGATIVE = -1e30
LANES = 128
TAIL = 16
AXES = ("segment", "blk", "mp")

F32 = jnp.float32
BF16 = jnp.bfloat16


def from_behind(x, axis, by):
    size = lax.axis_size(axis)
    pairs = [(i, i + by) for i in range(size) if 0 <= i + by < size]
    return lax.ppermute(x, axis, pairs)


def normalize(states, gain_row):
    widened = states.astype(jnp.float32)
    spread = jnp.sqrt(jnp.mean(widened * widened, axis=-1, keepdims=True) + EPSILON)
    return ((widened / spread * gain_row).astype(jnp.bfloat16), spread)


def right_product(left, right):
    return lax.dot_general(
        left, right, (((1,), (1,)), ((), ())), preferred_element_type=jnp.float32
    )


def per_device_windows(segment_in, norm_gains, projections, live_counts, cotangent):
    segment_pos = lax.axis_index("segment")
    model_index = lax.axis_index("mp")
    states = segment_in[0]
    gain_row = norm_gains[0]
    row_count, full_width = states.shape
    feature_width = cotangent.shape[1]
    w_primary = projections[0, :, 0, :]
    w_secondary = projections[0, :, 1, :]
    group_width = w_primary.shape[1]
    group_heads = group_width // DH
    normed, spread = normalize(states, gain_row)
    primary = jnp.dot(normed, w_primary, preferred_element_type=jnp.float32).astype(jnp.bfloat16)
    secondary = lax.cond(
        segment_pos == 0,
        lambda: jnp.dot(normed, w_secondary, preferred_element_type=jnp.float32).astype(
            jnp.bfloat16
        ),
        lambda: jnp.zeros_like(primary),
    )
    doc_keys, doc_values = from_behind((primary, secondary), "segment", 1)
    own_block = (doc_keys, doc_values, live_counts[0])
    window = [own_block]
    moving = own_block
    for offset in range(1, WIN):
        moving = from_behind((moving[0], moving[1], moving[2]), "blk", 1)
        window.append(moving)
    position = jnp.arange(row_count, dtype=jnp.int32)
    all_keys = jnp.concatenate([piece[0] for piece in window], 0).reshape(
        WIN * row_count, group_heads, DH
    )
    all_values = jnp.concatenate([piece[1] for piece in window], 0).reshape(
        WIN * row_count, group_heads, DH
    )
    key_live = jnp.concatenate([position < piece[2][0] for piece in window], 0)
    query_live = position < live_counts[1][0]
    query_heads = primary.reshape(row_count, group_heads, DH)
    scores = (
        jnp.einsum("qhd,khd->hqk", query_heads, all_keys, preferred_element_type=jnp.float32)
        * SCALE
    )
    scores = jnp.where(key_live[None, None, :], scores, NEGATIVE)
    row_max = jnp.max(scores, axis=-1, keepdims=True)
    expo = jnp.exp(scores - row_max)
    row_total = jnp.sum(expo, axis=-1, keepdims=True)
    softmax_out = expo / row_total
    weights_low = softmax_out.astype(jnp.bfloat16)
    attended = jnp.einsum(
        "hqk,khd->qhd", weights_low, all_values, preferred_element_type=jnp.float32
    ).astype(jnp.bfloat16)
    attended = jnp.where(query_live[:, None, None], attended, jnp.zeros_like(attended)).reshape(
        row_count, group_width
    )
    projected = lax.cond(
        segment_pos == 1,
        lambda: right_product(attended, w_secondary),
        lambda: jnp.zeros((row_count, full_width), jnp.float32),
    )
    layer_out = lax.psum_scatter(
        projected.astype(jnp.bfloat16), "mp", scatter_dimension=1, tiled=True
    )
    own_normed = lax.dynamic_slice_in_dim(normed, model_index * feature_width, feature_width, 1)
    segment_out = jnp.where(segment_pos == 0, own_normed, layer_out)[None]
    grad_out = jnp.dot(
        lax.all_gather(cotangent, "mp", axis=1, tiled=True),
        w_secondary,
        preferred_element_type=jnp.float32,
    )
    grad_out = grad_out.astype(jnp.bfloat16)
    grad_out = jnp.where(query_live[:, None], grad_out, jnp.zeros_like(grad_out))
    grad_heads = grad_out.reshape(row_count, group_heads, DH)
    grad_probs = jnp.einsum(
        "qhd,khd->hqk", grad_heads, all_values, preferred_element_type=jnp.float32
    )
    row_delta = jnp.sum(softmax_out * grad_probs, axis=-1, keepdims=True)
    grad_scores = (softmax_out * (grad_probs - row_delta)).astype(jnp.bfloat16)
    grad_queries = (
        (
            SCALE
            * jnp.einsum("hqk,khd->qhd", grad_scores, all_keys, preferred_element_type=jnp.float32)
        )
        .astype(jnp.bfloat16)
        .reshape(row_count, group_width)
    )
    key_parts = (
        SCALE
        * jnp.einsum("hqk,qhd->khd", grad_scores, query_heads, preferred_element_type=jnp.float32)
    ).reshape(WIN, row_count, group_width)
    value_parts = jnp.einsum(
        "hqk,qhd->khd", weights_low, grad_heads, preferred_element_type=jnp.float32
    ).reshape(WIN, row_count, group_width)
    key_total = key_parts[WIN - 1]
    value_total = value_parts[WIN - 1]
    for offset in range(WIN - 2, -1, -1):
        arrived = (
            from_behind(key_total.astype(jnp.bfloat16), "blk", -1).astype(key_total.dtype),
            from_behind(value_total.astype(jnp.bfloat16), "blk", -1).astype(value_total.dtype),
        )
        key_total = arrived[0] + key_parts[offset]
        value_total = arrived[1] + value_parts[offset]
    grad_keys = key_total.astype(jnp.bfloat16)
    grad_values = value_total.astype(jnp.bfloat16)
    back_keys, back_values = from_behind((grad_keys, grad_values), "segment", -1)
    partial_grad = lax.cond(
        segment_pos == 0,
        lambda: right_product(back_keys, w_primary) + right_product(back_values, w_secondary),
        lambda: right_product(grad_queries, w_primary),
    )
    widened = states.astype(jnp.float32)
    summed = lax.psum_scatter(
        partial_grad.astype(jnp.bfloat16), "mp", scatter_dimension=1, tiled=True
    ).astype(jnp.float32)
    own_states = lax.dynamic_slice_in_dim(widened, model_index * feature_width, feature_width, 1)
    own_gain = lax.dynamic_slice_in_dim(gain_row, model_index * feature_width, feature_width, 0)
    row_term = lax.psum(jnp.sum(summed * own_gain * own_states, axis=-1, keepdims=True), "mp")
    input_grad = (
        own_gain * summed / spread - own_states * row_term / (full_width * spread**3)
    ).astype(jnp.bfloat16)
    return (segment_out, input_grad[None])


def place(sizes):
    seg = lax.axis_index("segment")
    return seg, seg * sizes[1] + lax.axis_index("blk"), lax.axis_index("mp")


def swap_halves(x):
    return jnp.concatenate([x[:, DH:], x[:, :DH]], axis=1)


def fold_half(low, high):
    return jnp.concatenate([low, high], axis=1)


def enter_kernel(sizes, chunks, states, gain, w, counts, *rest):
    heads = sizes[0] * sizes[1]
    wp, ws, own, spread, prim, sec = rest[:6]
    pairs, queries = rest[6 : 6 + heads], rest[6 + heads : 6 + 2 * heads]
    xbuf, gbuf, wbuf, normed, pacc, sacc, sems, ready = rest[6 + 2 * heads :]
    seg, entry, model = place(sizes)
    rows, width = xbuf.shape
    out_width = own.shape[1]
    depth = width // chunks
    tiles = wp.shape[1] // LANES
    pack = 2 * tiles
    group = 2 * LANES // pack
    lines = depth * pack
    first_copies = [
        pltpu.make_async_copy(states, xbuf, ready.at[0]),
        pltpu.make_async_copy(gain, gbuf, ready.at[1]),
    ]
    copies = [
        pltpu.make_async_copy(
            w.at[pl.ds(c * lines, lines), :], wbuf.at[pl.ds(c * lines, lines), :], sems.at[c]
        )
        for c in range(chunks)
    ]
    for copy in first_copies + copies:
        copy.start()
    here = lax.broadcasted_iota(jnp.int32, (2 * LANES, 2 * LANES), 0)
    there = lax.broadcasted_iota(jnp.int32, (2 * LANES, 2 * LANES), 1)
    source = pack * lax.rem(here, group) + lax.div(here, group)
    mix = jnp.where(there == source, 1.0, 0.0).astype(BF16)
    for copy in first_copies:
        copy.wait()
    part_rows = 32

    def norm_rows(at, _):
        line = pl.ds(pl.multiple_of(at * part_rows, part_rows), part_rows)
        wide = xbuf[line, :].astype(F32)
        mean = jnp.sum(wide * wide, axis=1, keepdims=True) * (1.0 / width)
        root = jnp.sqrt(mean + EPSILON)
        normed[line, :] = (wide * (1.0 / root) * gbuf[...]).astype(BF16)
        spread[line, :] = jnp.broadcast_to(root, (part_rows, LANES))
        return 0

    lax.fori_loop(0, rows // part_rows, norm_rows, 0)
    for c in range(chunks):
        copies[c].wait()
        for pair in range(depth // (2 * group)):
            base = c * lines + pair * 4 * LANES
            left = wbuf[base : base + 2 * LANES, :]
            right = wbuf[base + 2 * LANES : base + 4 * LANES, :]
            both = jnp.concatenate([left, right], axis=1)
            ordered = jnp.dot(mix, both, preferred_element_type=F32).astype(BF16)
            first = c * depth + 2 * pair * group
            for slot in range(pack):
                target = (wp, ws)[slot % 2]
                tile = slice(slot // 2 * LANES, (slot // 2 + 1) * LANES)
                part = ordered[slot * group : (slot + 1) * group, :]
                target[first : first + group, tile] = part[:, :LANES]
                target[first + group : first + 2 * group, tile] = part[:, LANES:]
        span = slice(c * depth, (c + 1) * depth)
        piece = normed[:, span]
        term = jnp.dot(piece, wp[span, :], preferred_element_type=F32)
        if c == 0:
            pacc[...] = term
        else:
            pacc[...] += term

        @pl.when(seg == 0)
        def _():
            other = jnp.dot(normed[:, span], ws[span, :], preferred_element_type=F32)
            if c == 0:
                sacc[...] = other
            else:
                sacc[...] += other

    prim[...] = pacc[...].astype(BF16)

    @pl.when(seg == 0)
    def _():
        sec[...] = sacc[...].astype(BF16)
        tail = jnp.full((TAIL, LANES), 1.0, F32) * counts[0, 0].astype(F32)
        for head in range(heads):
            cols = slice(head * DH, (head + 1) * DH)
            pair = fold_half(prim[:, cols], sec[:, cols])
            for k, out in enumerate(pairs):

                @pl.when(jnp.bitwise_xor(entry, k) == head)
                def _():
                    out[:rows, :] = pair
                    out[rows:, :] = tail.astype(BF16)

    @pl.when(seg == 1)
    def _():
        for head in range(heads):
            cols = slice(head * DH, (head + 1) * DH)
            half = fold_half(prim[: rows // 2, cols], prim[rows // 2 :, cols])
            for k, out in enumerate(queries):

                @pl.when(jnp.bitwise_xor(entry, k) == head)
                def _():
                    out[...] = half

    own[...] = normed[:, pl.ds(pl.multiple_of(model * out_width, out_width), out_width)]


def pack_kernel(sizes, counts, c0, c1, c2, c3, ws, *rest):
    heads = sizes[0] * sizes[1]
    outs, (acc,) = rest[:heads], rest[heads:]
    seg, entry, model = place(sizes)
    rows, feats = c0.shape

    @pl.when(seg == 1)
    def _():
        for at, cot in enumerate((c0, c1, c2, c3)):
            start = pl.multiple_of(jnp.bitwise_xor(model, at) * feats, feats)
            term = jnp.dot(cot[...], ws[pl.ds(start, feats), :], preferred_element_type=F32)
            if at == 0:
                acc[...] = term
            else:
                acc[...] += term
        line = lax.broadcasted_iota(jnp.int32, acc.shape, 0)
        second = jnp.where(line < counts[0, 1], acc[...], 0.0).astype(BF16)
        for head in range(heads):
            cols = slice(head * DH, (head + 1) * DH)
            half = fold_half(second[: rows // 2, cols], second[rows // 2 :, cols])
            for k, out in enumerate(outs):

                @pl.when(jnp.bitwise_xor(entry, k) == head)
                def _():
                    out[...] = half


def collect(entry, pieces, target, first, last):
    for k, piece in enumerate(pieces):
        sender = jnp.bitwise_xor(entry, k)

        @pl.when(jnp.logical_and(sender >= first, sender < last))
        def _():
            target[sender - first] = piece[...]


def live_keys(piece, rows):
    position = lax.broadcasted_iota(jnp.int32, (1, rows), 1).astype(F32)
    count = piece[rows : rows + 1, :].astype(F32)
    return position < jnp.concatenate([count] * (rows // LANES), axis=1)


def forward_kernel(sizes, *rest):
    heads = sizes[0] * sizes[1]
    blocks = sizes[1]
    pair_in, query_in = rest[:heads], rest[heads : 2 * heads]
    outs = rest[2 * heads : 3 * heads]
    pairs, queries, probs, back = rest[3 * heads :]
    seg, entry, model = place(sizes)
    rows = 2 * outs[0].shape[0]
    collect(entry, pair_in, pairs, 0, blocks)
    collect(entry, query_in, queries, blocks, heads)
    low = lax.broadcasted_iota(jnp.int32, (rows, LANES), 1) < DH
    zero = jnp.zeros((rows, LANES), BF16)
    live = [live_keys(pairs[j], rows) for j in range(blocks)]
    for i in range(blocks):
        half = queries[i]
        query = jnp.concatenate([half, swap_halves(half)], axis=0)
        query = jnp.where(low, query * BF16(SCALE), zero)
        scores = []
        for j in range(i + 1):
            product = right_product(query, pairs[j, :rows, :])
            scores.append(jnp.where(live[j], product, NEGATIVE))
        top = jnp.max(functools.reduce(jnp.maximum, scores), axis=1, keepdims=True)
        expo = [jnp.exp(s - top) for s in scores]
        total = jnp.sum(functools.reduce(jnp.add, expo), axis=1, keepdims=True)
        share = 1.0 / total
        out = jnp.zeros((rows, LANES), F32)
        for j in range(i + 1):
            prob = expo[j] * share
            probs[i * (i + 1) // 2 + j] = prob
            out += jnp.dot(prob.astype(BF16), pairs[j, :rows, :], preferred_element_type=F32)
        out = out.astype(BF16)
        back[i] = fold_half(out[: rows // 2, DH:], out[rows // 2 :, DH:])
    for k, out in enumerate(outs):
        target = jnp.bitwise_xor(entry, k)

        @pl.when(target >= blocks)
        def _():
            out[...] = back[target - blocks]


def backward_kernel(sizes, pairs, queries, probs, *rest):
    heads = sizes[0] * sizes[1]
    blocks = sizes[1]
    ins, pair_out, query_out = rest[:heads], rest[heads : 2 * heads], rest[2 * heads : 3 * heads]
    grads, back, back_pairs, totals = rest[3 * heads :]
    seg, entry, model = place(sizes)
    rows = pair_out[0].shape[0]
    collect(entry, ins, grads, blocks, heads)
    low = lax.broadcasted_iota(jnp.int32, (rows, LANES), 1) < DH
    zero = jnp.zeros((rows, LANES), BF16)
    for i in range(blocks):
        half = queries[i]
        query = jnp.concatenate([half, swap_halves(half)], axis=0)
        query = jnp.where(low, query * BF16(SCALE), zero)
        half = grads[i]
        grad = jnp.concatenate([swap_halves(half), half], axis=0)
        grad = jnp.where(low, zero, grad)
        flip_query = query.astype(F32).T.astype(BF16)
        flip_grad = grad.astype(F32).T.astype(BF16)
        place_of = i * (i + 1) // 2
        products, delta = [], None
        for j in range(i + 1):
            product = right_product(grad, pairs[j, :rows, :])
            products.append(product)
            term = probs[place_of + j] * product
            delta = term if delta is None else delta + term
        delta = jnp.sum(delta, axis=1, keepdims=True)
        out = jnp.zeros((rows, LANES), F32)
        for j in range(i + 1):
            prob = probs[place_of + j]
            slope = (prob * (products[j] - delta)).astype(BF16)
            out += jnp.dot(slope, pairs[j, :rows, :], preferred_element_type=F32)
            tall = jnp.dot(flip_query, slope, preferred_element_type=F32)
            tall += jnp.dot(flip_grad, prob.astype(BF16), preferred_element_type=F32)
            if i == j:
                totals[j] = tall
            else:
                totals[j] += tall
        out = (out * SCALE).astype(BF16)
        back[i] = fold_half(out[: rows // 2, :DH], out[rows // 2 :, :DH])
    for j in range(blocks):
        back_pairs[j] = totals[j].T.astype(BF16)
    for k in range(heads):
        target = jnp.bitwise_xor(entry, k)

        @pl.when(target < blocks)
        def _():
            pair_out[k][...] = back_pairs[target]

        @pl.when(target >= blocks)
        def _():
            query_out[k][...] = back[target - blocks]


def unfold(half, target, cols):
    rows = target.shape[0]
    target[: rows // 2, cols] = half[:, :DH]
    target[rows // 2 :, cols] = half[:, DH:]


def output_kernel(sizes, counts, ws, *rest):
    heads = sizes[0] * sizes[1]
    ins, (sent, kept, left, parts) = rest[:heads], rest[heads:]
    seg, entry, model = place(sizes)
    feats = sent.shape[2]

    @pl.when(seg == 1)
    def _():
        for k, piece in enumerate(ins):
            parts[jnp.bitwise_xor(entry, k)] = piece[...]
        for head in range(heads):
            unfold(parts[head], left, slice(head * DH, (head + 1) * DH))
        line = lax.broadcasted_iota(jnp.int32, left.shape, 0)
        masked = jnp.where(line < counts[0, 1], left[...].astype(F32), 0.0).astype(BF16)
        for slot, (out, other) in enumerate(((sent, 3), (sent, 1), (kept, 2), (kept, 0))):
            start = pl.multiple_of(jnp.bitwise_xor(model, other) * feats, feats)
            product = right_product(masked, ws[pl.ds(start, feats), :])
            out[slot % 2] = product.astype(BF16)


def project_block(seg, start, wp, ws, lp, ls, store):
    feats = pl.ds(start, wp.shape[0] // 4)

    @pl.when(seg == 0)
    def _():
        store(right_product(lp[...], wp[feats, :]) + right_product(ls[...], ws[feats, :]))

    @pl.when(seg == 1)
    def _():
        store(right_product(lp[...], wp[feats, :]))


def split_rows(column):
    row = jnp.broadcast_to(column, (column.shape[0], LANES)).T[:TAIL, :]
    high = row.astype(BF16).astype(F32)
    line = lax.broadcasted_iota(jnp.int32, row.shape, 0)
    return jnp.where(line == 0, high, row - high).astype(BF16)


def send_kernel(sizes, prim, sec, spread, wp, ws, *rest):
    heads = sizes[0] * sizes[1]
    pair_in, query_in = rest[:heads], rest[heads : 2 * heads]
    sent, lp, ls, pairs, halves = rest[2 * heads :]
    seg, entry, model = place(sizes)
    rows = prim.shape[0]
    feats = sent.shape[2]

    def finish(column):
        sent[0, rows:, :] = jnp.zeros((TAIL, feats), BF16)
        sent[1, rows:, :] = jnp.zeros((TAIL, feats), BF16)
        sent[0, rows:, :rows] = split_rows(column * spread[:, :1])

    @pl.when(seg == 0)
    def _():
        for k, piece in enumerate(pair_in):
            pairs[jnp.bitwise_xor(entry, k)] = piece[...]
        for head in range(heads):
            cols = slice(head * DH, (head + 1) * DH)
            lp[:, cols] = pairs[head, :, :DH]
            ls[:, cols] = pairs[head, :, DH:]
        term = lp[...].astype(F32) * prim[...].astype(F32)
        term += ls[...].astype(F32) * sec[...].astype(F32)
        finish(jnp.sum(term, axis=1, keepdims=True))

    @pl.when(seg == 1)
    def _():
        for k, piece in enumerate(query_in):
            halves[jnp.bitwise_xor(entry, k)] = piece[...]
        for head in range(heads):
            unfold(halves[head], lp, slice(head * DH, (head + 1) * DH))
        term = lp[...].astype(F32) * prim[...].astype(F32)
        finish(jnp.sum(term, axis=1, keepdims=True))

    for slot, other in enumerate((3, 1)):

        def store(product):
            sent[slot, :rows, :] = product.astype(BF16)

        start = pl.multiple_of(jnp.bitwise_xor(model, other) * feats, feats)
        project_block(seg, start, wp, ws, lp, ls, store)


def keep_kernel(sizes, lp, ls, wp, ws, kept):
    seg, entry, model = place(sizes)
    feats = kept.shape[2]
    for slot, other in enumerate((2, 0)):

        def store(product):
            kept[slot] = product.astype(BF16)

        start = pl.multiple_of(jnp.bitwise_xor(model, other) * feats, feats)
        project_block(seg, start, wp, ws, lp, ls, store)


def fold_output_kernel(sizes, kept, got, out):
    @pl.when(lax.axis_index("segment") == 1)
    def _():
        out[...] = (kept[0].astype(F32) + got[0].astype(F32)).astype(BF16)


def fold_kernel(kept, got, sent, out):
    rows = kept.shape[1]
    out[:rows, :] = (kept[0].astype(F32) + got[0, :rows, :].astype(F32)).astype(BF16)
    mine = sent[0, rows:, :].astype(F32)
    theirs = got[0, rows:, :].astype(F32)
    total = mine[0:1] + mine[1:2] + theirs[0:1] + theirs[1:2]
    total = jnp.broadcast_to(total, mine.shape)
    high = total.astype(BF16).astype(F32)
    line = lax.broadcasted_iota(jnp.int32, mine.shape, 0)
    out[rows:, :] = jnp.where(line == 0, high, total - high).astype(BF16)


def finish_output_kernel(sizes, kept, got, far, own, out):
    seg = lax.axis_index("segment")

    @pl.when(seg == 0)
    def _():
        out[...] = own[...]

    @pl.when(seg == 1)
    def _():
        total = kept[1].astype(F32) + got[1].astype(F32) + far[...].astype(F32)
        out[...] = total.astype(BF16)


def leave_kernel(sizes, width, kept, got, half, far, states, gain, spread, grad, xbuf, gbuf, sems):
    seg, entry, model = place(sizes)
    rows, feats = grad.shape
    span = pl.ds(pl.multiple_of(model * feats, feats), feats)
    copies = [
        pltpu.make_async_copy(states.at[:, span], xbuf, sems.at[0]),
        pltpu.make_async_copy(gain.at[:, span], gbuf, sems.at[1]),
    ]
    for copy in copies:
        copy.start()
    ends = half[rows:, :].astype(F32) + far[rows:, :].astype(F32)
    row = jnp.broadcast_to(ends[0:1, :rows] + ends[1:2, :rows], (LANES, rows))
    term = row.T[:, :1]
    root = spread[:, :1]
    scaled = term / (width * root * root * root)
    for copy in copies:
        copy.wait()
    total = kept[1].astype(F32) + got[1, :rows, :].astype(F32) + far[:rows, :].astype(F32)
    grad[...] = (gbuf[...] * total * (1.0 / root) - xbuf[...].astype(F32) * scaled).astype(BF16)


ANYWHERE = pl.BlockSpec(memory_space=pl.ANY)
INSIDE = pl.BlockSpec(memory_space=pltpu.VMEM)
SCALARS = pl.BlockSpec(memory_space=pltpu.SMEM)


def call(body, name, ins, specs, outs, scratch=(), limit=16, flops=0):
    given = []
    for value, spec in zip(ins, specs):
        given.append(value)
    return pl.pallas_call(
        body,
        in_specs=list(specs),
        out_specs=[INSIDE] * len(outs),
        out_shape=[pltpu.VMEM(s, d) for s, d in outs],
        scratch_shapes=list(scratch),
        compiler_params=pltpu.CompilerParams(vmem_limit_bytes=limit << 20),
        cost_estimate=pl.CostEstimate(flops=flops, transcendentals=0, bytes_accessed=1 << 20),
        name=name,
    )(*given)


def per_device_heads(sizes, segment_in, norm_gains, projections, live_counts, cotangent):
    n_seg, n_blk, n_mp = sizes
    heads = n_seg * n_blk
    states = segment_in[0]
    rows, width = states.shape
    feats = cotangent.shape[1]
    group = projections.shape[3]
    counts = live_counts.T

    def swap(x, over_heads, over_mp, sends=lambda e: True):
        pairs = [
            (e * n_mp + m, (e ^ over_heads) * n_mp + (m ^ over_mp))
            for e in range(heads)
            for m in range(n_mp)
            if sends(e)
        ]
        return lax.ppermute(x, AXES, pairs)

    def document(e):
        return e < n_blk

    def summary(e):
        return e >= n_blk

    def exchange(pieces, sends):
        far_first = sorted(range(1, heads), key=lambda k: -((k % n_blk) * 2 + k // n_blk))
        moved = {k: swap(pieces[k], k, 0, functools.partial(sends, k)) for k in far_first}
        return [pieces[0]] + [moved[k] for k in range(1, heads)]

    far_cot = swap(cotangent, 0, 2, summary)
    near_cot = swap(cotangent, 0, 1, summary)
    tiles = group // LANES
    mixed = projections.reshape(width, 2, tiles, LANES).transpose(0, 2, 1, 3)
    mixed = mixed.reshape(width * 2 * tiles, LANES)
    chunks = 4
    pair_shape, half_shape = (rows + TAIL, LANES), (rows // 2, LANES)
    made = call(
        functools.partial(enter_kernel, sizes, chunks),
        "enter",
        (states, norm_gains, mixed, counts),
        [ANYWHERE, ANYWHERE, ANYWHERE, SCALARS],
        [
            ((width, group), BF16),
            ((width, group), BF16),
            ((rows, feats), BF16),
            ((rows, LANES), F32),
            ((rows, group), BF16),
            ((rows, group), BF16),
        ]
        + [(pair_shape, BF16)] * heads
        + [(half_shape, BF16)] * heads,
        [
            pltpu.VMEM((rows, width), BF16),
            pltpu.VMEM((1, width), F32),
            pltpu.VMEM((width * 2 * tiles, LANES), BF16),
            pltpu.VMEM((rows, width), BF16),
            pltpu.VMEM((rows, group), F32),
            pltpu.VMEM((rows, group), F32),
            pltpu.SemaphoreType.DMA((chunks,)),
            pltpu.SemaphoreType.DMA((2,)),
        ],
        24,
        8 << 30,
    )
    wp, ws, own, spread, prim, sec = made[:6]
    pairs, queries = made[6 : 6 + heads], made[6 + heads :]
    pairs = exchange(pairs, lambda k, e: document(e))
    queries = exchange(queries, lambda k, e: summary(e))
    cross_cot = swap(far_cot, 0, 1, summary)
    grads = call(
        functools.partial(pack_kernel, sizes),
        "pack",
        (counts, cotangent, near_cot, far_cot, cross_cot, ws),
        [SCALARS] + [INSIDE] * 5,
        [(half_shape, BF16)] * heads,
        [pltpu.VMEM((rows, group), F32)],
        16,
        1 << 30,
    )
    grads = exchange(grads, lambda k, e: summary(e))
    n_pairs = n_blk * (n_blk + 1) // 2
    made = call(
        functools.partial(forward_kernel, sizes),
        "forward",
        (*pairs, *queries),
        [INSIDE] * 2 * heads,
        [(half_shape, BF16)] * heads
        + [
            ((n_blk, *pair_shape), BF16),
            ((n_blk, *half_shape), BF16),
            ((n_pairs, rows, rows), F32),
        ],
        [pltpu.VMEM((n_blk, *half_shape), BF16)],
        16,
        2 << 30,
    )
    attended, (pairs, queries, probs) = made[:heads], made[heads:]
    attended = exchange(attended, lambda k, e: summary(e ^ k))
    sent2, kept2 = call(
        functools.partial(output_kernel, sizes),
        "output",
        (counts, ws, *attended),
        [SCALARS] + [INSIDE] * (1 + heads),
        [((2, rows, feats), BF16)] * 2,
        [pltpu.VMEM((rows, group), BF16), pltpu.VMEM((heads, *half_shape), BF16)],
        16,
        2 << 30,
    )
    got2 = swap(sent2, 0, 1, summary)
    (half2,) = call(
        functools.partial(fold_output_kernel, sizes),
        "fold_output",
        (kept2, got2),
        [INSIDE] * 2,
        [((rows, feats), BF16)],
    )
    far2 = swap(half2, 0, 2, summary)
    made = call(
        functools.partial(backward_kernel, sizes),
        "backward",
        (pairs, queries, probs, *grads),
        [INSIDE] * (3 + heads),
        [((rows, LANES), BF16)] * heads + [(half_shape, BF16)] * heads,
        [
            pltpu.VMEM((n_blk, *half_shape), BF16),
            pltpu.VMEM((n_blk, *half_shape), BF16),
            pltpu.VMEM((n_blk, rows, LANES), BF16),
            pltpu.VMEM((n_blk, LANES, rows), F32),
        ],
        16,
        3 << 30,
    )
    pair_grads, query_grads = made[:heads], made[heads:]
    pair_grads = exchange(pair_grads, lambda k, e: document(e ^ k))
    query_grads = exchange(query_grads, lambda k, e: summary(e ^ k))
    sent, lp, ls = call(
        functools.partial(send_kernel, sizes),
        "send",
        (prim, sec, spread, wp, ws, *pair_grads, *query_grads),
        [INSIDE] * (5 + 2 * heads),
        [
            ((2, rows + TAIL, feats), BF16),
            ((rows, group), BF16),
            ((rows, group), BF16),
        ],
        [pltpu.VMEM((heads, rows, LANES), BF16), pltpu.VMEM((heads, *half_shape), BF16)],
        16,
        2 << 30,
    )
    got = swap(sent, 0, 1)
    (kept,) = call(
        functools.partial(keep_kernel, sizes),
        "keep",
        (lp, ls, wp, ws),
        [INSIDE] * 4,
        [((2, rows, feats), BF16)],
        (),
        16,
        2 << 30,
    )
    (half,) = call(
        fold_kernel, "fold", (kept, got, sent), [INSIDE] * 3, [((rows + TAIL, feats), BF16)]
    )
    far = swap(half, 0, 2)
    (out,) = call(
        functools.partial(finish_output_kernel, sizes),
        "finish_output",
        (kept2, got2, far2, own),
        [INSIDE] * 4,
        [((rows, feats), BF16)],
    )
    (grad,) = call(
        functools.partial(leave_kernel, sizes, width),
        "leave",
        (kept, got, half, far, states, norm_gains, spread),
        [INSIDE] * 4 + [ANYWHERE] * 2 + [INSIDE],
        [((rows, feats), BF16)],
        [
            pltpu.VMEM((rows, feats), BF16),
            pltpu.VMEM((1, feats), F32),
            pltpu.SemaphoreType.DMA((2,)),
        ],
    )
    return (out[None], grad[None])


def solution(mesh):
    sizes = tuple(mesh.shape[axis] for axis in AXES)
    n_seg, n_blk, n_mp = sizes

    def body(segment_in, norm_gains, projections, live_counts, cotangent):
        heads = projections.shape[3] // DH
        rows = segment_in.shape[1]
        power = heads & (heads - 1) == 0
        fits = n_seg == 2 and n_seg * n_blk == heads and power and n_blk <= WIN
        if fits and n_mp == 4 and rows % LANES == 0 and projections.shape[3] == 4 * LANES:
            form = functools.partial(per_device_heads, sizes)
        else:
            form = per_device_windows
        return form(segment_in, norm_gains, projections, live_counts, cotangent)

    in_specs = (
        P("segment", "blk", None),
        P("segment", None),
        P("segment", None, None, "mp"),
        P(None, "blk"),
        P("blk", "mp"),
    )
    out_specs = (P("segment", "blk", "mp"), P("segment", "blk", "mp"))
    return jax.shard_map(body, mesh=mesh, in_specs=in_specs, out_specs=out_specs, check_vma=False)
```

```python
import functools

import jax
import jax.numpy as jnp
from jax import lax
from jax.experimental import pallas as pl
from jax.experimental.pallas import tpu as pltpu
from jax.sharding import PartitionSpec as P

DH = 64
WIN = 4


EPSILON = 1e-06
SCALE = 0.125
NEGATIVE = -1e30
LANES = 128
TAIL = 16
AXES = ("segment", "blk", "mp")

F32 = jnp.float32
BF16 = jnp.bfloat16


def from_behind(x, axis, by):
    size = lax.axis_size(axis)
    pairs = [(i, i + by) for i in range(size) if 0 <= i + by < size]
    return lax.ppermute(x, axis, pairs)


def normalize(states, gain_row):
    widened = states.astype(jnp.float32)
    spread = jnp.sqrt(jnp.mean(widened * widened, axis=-1, keepdims=True) + EPSILON)
    return ((widened / spread * gain_row).astype(jnp.bfloat16), spread)


def right_product(left, right):
    return lax.dot_general(
        left, right, (((1,), (1,)), ((), ())), preferred_element_type=jnp.float32
    )


def per_device_windows(segment_in, norm_gains, projections, live_counts, cotangent):
    segment_pos = lax.axis_index("segment")
    model_index = lax.axis_index("mp")
    states = segment_in[0]
    gain_row = norm_gains[0]
    row_count, full_width = states.shape
    feature_width = cotangent.shape[1]
    w_primary = projections[0, :, 0, :]
    w_secondary = projections[0, :, 1, :]
    group_width = w_primary.shape[1]
    group_heads = group_width // DH
    normed, spread = normalize(states, gain_row)
    primary = jnp.dot(normed, w_primary, preferred_element_type=jnp.float32).astype(jnp.bfloat16)
    secondary = lax.cond(
        segment_pos == 0,
        lambda: jnp.dot(normed, w_secondary, preferred_element_type=jnp.float32).astype(
            jnp.bfloat16
        ),
        lambda: jnp.zeros_like(primary),
    )
    doc_keys, doc_values = from_behind((primary, secondary), "segment", 1)
    own_block = (doc_keys, doc_values, live_counts[0])
    window = [own_block]
    moving = own_block
    for offset in range(1, WIN):
        moving = from_behind((moving[0], moving[1], moving[2]), "blk", 1)
        window.append(moving)
    position = jnp.arange(row_count, dtype=jnp.int32)
    all_keys = jnp.concatenate([piece[0] for piece in window], 0).reshape(
        WIN * row_count, group_heads, DH
    )
    all_values = jnp.concatenate([piece[1] for piece in window], 0).reshape(
        WIN * row_count, group_heads, DH
    )
    key_live = jnp.concatenate([position < piece[2][0] for piece in window], 0)
    query_live = position < live_counts[1][0]
    query_heads = primary.reshape(row_count, group_heads, DH)
    scores = (
        jnp.einsum("qhd,khd->hqk", query_heads, all_keys, preferred_element_type=jnp.float32)
        * SCALE
    )
    scores = jnp.where(key_live[None, None, :], scores, NEGATIVE)
    row_max = jnp.max(scores, axis=-1, keepdims=True)
    expo = jnp.exp(scores - row_max)
    row_total = jnp.sum(expo, axis=-1, keepdims=True)
    softmax_out = expo / row_total
    weights_low = softmax_out.astype(jnp.bfloat16)
    attended = jnp.einsum(
        "hqk,khd->qhd", weights_low, all_values, preferred_element_type=jnp.float32
    ).astype(jnp.bfloat16)
    attended = jnp.where(query_live[:, None, None], attended, jnp.zeros_like(attended)).reshape(
        row_count, group_width
    )
    projected = lax.cond(
        segment_pos == 1,
        lambda: right_product(attended, w_secondary),
        lambda: jnp.zeros((row_count, full_width), jnp.float32),
    )
    layer_out = lax.psum_scatter(
        projected.astype(jnp.bfloat16), "mp", scatter_dimension=1, tiled=True
    )
    own_normed = lax.dynamic_slice_in_dim(normed, model_index * feature_width, feature_width, 1)
    segment_out = jnp.where(segment_pos == 0, own_normed, layer_out)[None]
    grad_out = jnp.dot(
        lax.all_gather(cotangent, "mp", axis=1, tiled=True),
        w_secondary,
        preferred_element_type=jnp.float32,
    )
    grad_out = grad_out.astype(jnp.bfloat16)
    grad_out = jnp.where(query_live[:, None], grad_out, jnp.zeros_like(grad_out))
    grad_heads = grad_out.reshape(row_count, group_heads, DH)
    grad_probs = jnp.einsum(
        "qhd,khd->hqk", grad_heads, all_values, preferred_element_type=jnp.float32
    )
    row_delta = jnp.sum(softmax_out * grad_probs, axis=-1, keepdims=True)
    grad_scores = (softmax_out * (grad_probs - row_delta)).astype(jnp.bfloat16)
    grad_queries = (
        (
            SCALE
            * jnp.einsum("hqk,khd->qhd", grad_scores, all_keys, preferred_element_type=jnp.float32)
        )
        .astype(jnp.bfloat16)
        .reshape(row_count, group_width)
    )
    key_parts = (
        SCALE
        * jnp.einsum("hqk,qhd->khd", grad_scores, query_heads, preferred_element_type=jnp.float32)
    ).reshape(WIN, row_count, group_width)
    value_parts = jnp.einsum(
        "hqk,qhd->khd", weights_low, grad_heads, preferred_element_type=jnp.float32
    ).reshape(WIN, row_count, group_width)
    key_total = key_parts[WIN - 1]
    value_total = value_parts[WIN - 1]
    for offset in range(WIN - 2, -1, -1):
        arrived = (
            from_behind(key_total.astype(jnp.bfloat16), "blk", -1).astype(key_total.dtype),
            from_behind(value_total.astype(jnp.bfloat16), "blk", -1).astype(value_total.dtype),
        )
        key_total = arrived[0] + key_parts[offset]
        value_total = arrived[1] + value_parts[offset]
    grad_keys = key_total.astype(jnp.bfloat16)
    grad_values = value_total.astype(jnp.bfloat16)
    back_keys, back_values = from_behind((grad_keys, grad_values), "segment", -1)
    partial_grad = lax.cond(
        segment_pos == 0,
        lambda: right_product(back_keys, w_primary) + right_product(back_values, w_secondary),
        lambda: right_product(grad_queries, w_primary),
    )
    widened = states.astype(jnp.float32)
    summed = lax.psum_scatter(
        partial_grad.astype(jnp.bfloat16), "mp", scatter_dimension=1, tiled=True
    ).astype(jnp.float32)
    own_states = lax.dynamic_slice_in_dim(widened, model_index * feature_width, feature_width, 1)
    own_gain = lax.dynamic_slice_in_dim(gain_row, model_index * feature_width, feature_width, 0)
    row_term = lax.psum(jnp.sum(summed * own_gain * own_states, axis=-1, keepdims=True), "mp")
    input_grad = (
        own_gain * summed / spread - own_states * row_term / (full_width * spread**3)
    ).astype(jnp.bfloat16)
    return (segment_out, input_grad[None])


def place(sizes):
    seg = lax.axis_index("segment")
    return seg, seg * sizes[1] + lax.axis_index("blk"), lax.axis_index("mp")


def enter_kernel(sizes, chunks, states, gain, w, *rest):
    wp, ws, own, spread, prim, sec = rest[:6]
    xbuf, gbuf, wbuf, normed, pacc, sacc, sems, ready = rest[6:]
    seg, entry, model = place(sizes)
    rows, width = xbuf.shape
    out_width = own.shape[1]
    depth = width // chunks
    tiles = wp.shape[1] // LANES
    pack = 2 * tiles
    group = 2 * LANES // pack
    lines = depth * pack
    first_copies = [
        pltpu.make_async_copy(states, xbuf, ready.at[0]),
        pltpu.make_async_copy(gain, gbuf, ready.at[1]),
    ]
    copies = [
        pltpu.make_async_copy(
            w.at[pl.ds(c * lines, lines), :], wbuf.at[pl.ds(c * lines, lines), :], sems.at[c]
        )
        for c in range(chunks)
    ]
    for copy in first_copies + copies:
        copy.start()
    here = lax.broadcasted_iota(jnp.int32, (2 * LANES, 2 * LANES), 0)
    there = lax.broadcasted_iota(jnp.int32, (2 * LANES, 2 * LANES), 1)
    source = pack * lax.rem(here, group) + lax.div(here, group)
    mix = jnp.where(there == source, 1.0, 0.0).astype(BF16)
    for copy in first_copies:
        copy.wait()
    part_rows = 32

    def norm_rows(at, _):
        line = pl.ds(pl.multiple_of(at * part_rows, part_rows), part_rows)
        wide = xbuf[line, :].astype(F32)
        mean = jnp.sum(wide * wide, axis=1, keepdims=True) * (1.0 / width)
        root = jnp.sqrt(mean + EPSILON)
        normed[line, :] = (wide * (1.0 / root) * gbuf[...]).astype(BF16)
        spread[line, :] = jnp.broadcast_to(root, (part_rows, LANES))
        return 0

    lax.fori_loop(0, rows // part_rows, norm_rows, 0)
    for c in range(chunks):
        copies[c].wait()
        for pair in range(depth // (2 * group)):
            base = c * lines + pair * 4 * LANES
            left = wbuf[base : base + 2 * LANES, :]
            right = wbuf[base + 2 * LANES : base + 4 * LANES, :]
            both = jnp.concatenate([left, right], axis=1)
            ordered = jnp.dot(mix, both, preferred_element_type=F32).astype(BF16)
            first = c * depth + 2 * pair * group
            for slot in range(pack):
                target = (wp, ws)[slot % 2]
                tile = slice(slot // 2 * LANES, (slot // 2 + 1) * LANES)
                part = ordered[slot * group : (slot + 1) * group, :]
                target[first : first + group, tile] = part[:, :LANES]
                target[first + group : first + 2 * group, tile] = part[:, LANES:]
        span = slice(c * depth, (c + 1) * depth)
        piece = normed[:, span]
        term = jnp.dot(piece, wp[span, :], preferred_element_type=F32)
        if c == 0:
            pacc[...] = term
        else:
            pacc[...] += term

        @pl.when(seg == 0)
        def _():
            other = jnp.dot(normed[:, span], ws[span, :], preferred_element_type=F32)
            if c == 0:
                sacc[...] = other
            else:
                sacc[...] += other

    prim[...] = pacc[...].astype(BF16)

    @pl.when(seg == 0)
    def _():
        sec[...] = sacc[...].astype(BF16)

    own[...] = normed[:, pl.ds(pl.multiple_of(model * out_width, out_width), out_width)]


def pack_kernel(sizes, counts, prim, sec, c0, c1, c2, c3, ws, *rest):
    heads = sizes[0] * sizes[1]
    second, outs, (acc,) = rest[0], rest[1 : 1 + heads], rest[1 + heads :]
    seg, entry, model = place(sizes)
    rows, feats = c0.shape

    @pl.when(seg == 0)
    def _():
        second[...] = sec[...]

    @pl.when(seg == 1)
    def _():
        for at, cot in enumerate((c0, c1, c2, c3)):
            start = pl.multiple_of(jnp.bitwise_xor(model, at) * feats, feats)
            term = jnp.dot(cot[...], ws[pl.ds(start, feats), :], preferred_element_type=F32)
            if at == 0:
                acc[...] = term
            else:
                acc[...] += term
        line = lax.broadcasted_iota(jnp.int32, acc.shape, 0)
        second[...] = jnp.where(line < counts[0, 1], acc[...], 0.0).astype(BF16)

    tail = jnp.full((TAIL, LANES), 1.0, F32) * counts[0, 0].astype(F32)
    for head in range(heads):
        cols = slice(head * DH, (head + 1) * DH)
        pair = jnp.concatenate([prim[:, cols], second[:, cols]], axis=1)
        for k, out in enumerate(outs):

            @pl.when(jnp.bitwise_xor(entry, k) == head)
            def _():
                out[:rows, :] = pair
                out[rows:, :] = tail.astype(BF16)


def live_keys(piece, rows):
    position = lax.broadcasted_iota(jnp.int32, (1, rows), 1).astype(F32)
    count = piece[rows : rows + 1, :].astype(F32)
    return position < jnp.concatenate([count] * (rows // LANES), axis=1)


def attend_kernel(sizes, *rest):
    heads = sizes[0] * sizes[1]
    blocks = sizes[1]
    ins, outs = rest[:heads], rest[heads : 2 * heads]
    parts, back, totals = rest[2 * heads :]
    seg, entry, model = place(sizes)
    rows = outs[0].shape[0]
    for k, piece in enumerate(ins):
        parts[jnp.bitwise_xor(entry, k)] = piece[...]
    low = lax.broadcasted_iota(jnp.int32, (rows, LANES), 1) < DH
    zero = jnp.zeros((rows, LANES), BF16)
    live = [live_keys(parts[j], rows) for j in range(blocks)]
    for i in range(blocks):
        both = parts[blocks + i, :rows, :]
        query = jnp.where(low, both * BF16(SCALE), zero)
        grad = jnp.where(low, zero, both)
        flip_query = query.astype(F32).T.astype(BF16)
        flip_grad = grad.astype(F32).T.astype(BF16)
        scores = []
        for j in range(i + 1):
            product = right_product(query, parts[j, :rows, :])
            scores.append(jnp.where(live[j], product, NEGATIVE))
        top = jnp.max(functools.reduce(jnp.maximum, scores), axis=1, keepdims=True)
        expo = [jnp.exp(s - top) for s in scores]
        total = jnp.sum(functools.reduce(jnp.add, expo), axis=1, keepdims=True)
        share = 1.0 / total
        probs = [e * share for e in expo]
        slopes = [right_product(grad, parts[j, :rows, :]) for j in range(i + 1)]
        delta = functools.reduce(jnp.add, [p * g for p, g in zip(probs, slopes)])
        delta = jnp.sum(delta, axis=1, keepdims=True)
        out = jnp.zeros((rows, LANES), F32)
        other = jnp.zeros((rows, LANES), F32)
        for j in range(i + 1):
            prob = probs[j].astype(BF16)
            slope = (probs[j] * (slopes[j] - delta)).astype(BF16)
            other += jnp.dot(slope, parts[j, :rows, :], preferred_element_type=F32)
            out += jnp.dot(prob, parts[j, :rows, :], preferred_element_type=F32)
            tall = jnp.dot(flip_query, slope, preferred_element_type=F32)
            tall += jnp.dot(flip_grad, prob, preferred_element_type=F32)
            if i == j:
                totals[j] = tall
            else:
                totals[j] += tall
        back[blocks + i] = jnp.where(low, other * SCALE, out).astype(BF16)
    for j in range(blocks):
        back[j] = totals[j].T.astype(BF16)
    for k, out in enumerate(outs):
        out[...] = back[jnp.bitwise_xor(entry, k)]


def split_rows(column):
    row = jnp.broadcast_to(column, (column.shape[0], LANES)).T[:TAIL, :]
    high = row.astype(BF16).astype(F32)
    line = lax.broadcasted_iota(jnp.int32, row.shape, 0)
    return jnp.where(line == 0, high, row - high).astype(BF16)


def project_block(seg, start, feats, wp, ws, lp, ls, out, out2, slot):
    span = pl.ds(pl.multiple_of(start, feats), feats)
    first = right_product(lp[...], wp[span, :])
    second = right_product(ls[...], ws[span, :])
    rows = first.shape[0]

    @pl.when(seg == 0)
    def _():
        out[slot, :rows, :] = (first + second).astype(BF16)

    @pl.when(seg == 1)
    def _():
        out[slot, :rows, :] = first.astype(BF16)
        out2[slot] = second.astype(BF16)


def send_kernel(sizes, counts, prim, second, spread, wp, ws, *rest):
    heads = sizes[0] * sizes[1]
    ins = rest[:heads]
    sent, sent2, lp, ls, parts = rest[heads:]
    seg, entry, model = place(sizes)
    rows = prim.shape[0]
    feats = sent.shape[2]
    for k, piece in enumerate(ins):
        parts[jnp.bitwise_xor(entry, k)] = piece[...]
    for head in range(heads):
        cols = slice(head * DH, (head + 1) * DH)
        lp[:, cols] = parts[head, :, :DH]
        ls[:, cols] = parts[head, :, DH:]
    line = lax.broadcasted_iota(jnp.int32, ls.shape, 0)
    last = jnp.where(seg == 0, rows, counts[0, 1])
    ls[...] = jnp.where(line < last, ls[...].astype(F32), 0.0).astype(BF16)
    for slot, other in enumerate((3, 1)):
        start = jnp.bitwise_xor(model, other) * feats
        project_block(seg, start, feats, wp, ws, lp, ls, sent, sent2, slot)
    term = lp[...].astype(F32) * prim[...].astype(F32)
    also = ls[...].astype(F32) * second[...].astype(F32)
    term = term + jnp.where(seg == 0, also, 0.0)
    column = jnp.sum(term, axis=1, keepdims=True) * spread[:, :1]
    sent[0, rows:, :] = jnp.zeros((TAIL, feats), BF16)
    sent[1, rows:, :] = jnp.zeros((TAIL, feats), BF16)
    sent[0, rows:, :rows] = split_rows(column)


def keep_kernel(sizes, lp, ls, wp, ws, kept, kept2):
    seg, entry, model = place(sizes)
    feats = kept.shape[2]
    for slot, other in enumerate((2, 0)):
        start = jnp.bitwise_xor(model, other) * feats
        project_block(seg, start, feats, wp, ws, lp, ls, kept, kept2, slot)


def fold_output_kernel(sizes, kept, got, out):
    @pl.when(lax.axis_index("segment") == 1)
    def _():
        out[...] = (kept[0].astype(F32) + got[0].astype(F32)).astype(BF16)


def fold_kernel(kept, got, sent, out):
    rows = kept.shape[1]
    out[:rows, :] = (kept[0].astype(F32) + got[0, :rows, :].astype(F32)).astype(BF16)
    mine = sent[0, rows:, :].astype(F32)
    theirs = got[0, rows:, :].astype(F32)
    total = mine[0:1] + mine[1:2] + theirs[0:1] + theirs[1:2]
    total = jnp.broadcast_to(total, mine.shape)
    high = total.astype(BF16).astype(F32)
    line = lax.broadcasted_iota(jnp.int32, mine.shape, 0)
    out[rows:, :] = jnp.where(line == 0, high, total - high).astype(BF16)


def leave_kernel(sizes, width, kept, got, half, far, kept2, got2, far2, states, gain, spread, own, *rest):
    out, grad, xbuf, gbuf, obuf, sems = rest
    seg, entry, model = place(sizes)
    rows, feats = xbuf.shape
    span = pl.ds(pl.multiple_of(model * feats, feats), feats)
    copies = [
        pltpu.make_async_copy(states.at[:, span], xbuf, sems.at[0]),
        pltpu.make_async_copy(gain.at[:, span], gbuf, sems.at[1]),
    ]
    for copy in copies:
        copy.start()

    @pl.when(seg == 0)
    def _():
        obuf[...] = own[...]

    @pl.when(seg == 1)
    def _():
        layer = kept2[1].astype(F32) + got2[1].astype(F32) + far2[...].astype(F32)
        obuf[...] = layer.astype(BF16)

    leaving = pltpu.make_async_copy(obuf, out, sems.at[2])
    leaving.start()
    ends = half[rows:, :].astype(F32) + far[rows:, :].astype(F32)
    row = jnp.broadcast_to(ends[0:1, :rows] + ends[1:2, :rows], (LANES, rows))
    term = row.T[:, :1]
    root = spread[:, :1]
    scaled = term / (width * root * root * root)
    for copy in copies:
        copy.wait()
    total = kept[1].astype(F32) + got[1, :rows, :].astype(F32) + far[:rows, :].astype(F32)
    grad[...] = (gbuf[...] * total * (1.0 / root) - xbuf[...].astype(F32) * scaled).astype(BF16)
    leaving.wait()


ANYWHERE = pl.BlockSpec(memory_space=pltpu.HBM)
INSIDE = pl.BlockSpec(memory_space=pltpu.VMEM)
SCALARS = pl.BlockSpec(memory_space=pltpu.SMEM)


def call(body, name, ins, specs, outs, scratch=(), limit=16, flops=0, out_specs=None):
    inside = out_specs is None
    ins = [
        pltpu.with_memory_space_constraint(x, pltpu.HBM) if spec is ANYWHERE else x
        for x, spec in zip(ins, specs)
    ]
    return pl.pallas_call(
        body,
        in_specs=list(specs),
        out_specs=[INSIDE] * len(outs) if inside else out_specs,
        out_shape=[(pltpu.VMEM if inside else jax.ShapeDtypeStruct)(s, d) for s, d in outs],
        scratch_shapes=list(scratch),
        compiler_params=pltpu.CompilerParams(vmem_limit_bytes=limit << 20),
        cost_estimate=pl.CostEstimate(flops=flops, transcendentals=0, bytes_accessed=1 << 20),
        name=name,
    )(*ins)


def per_device_heads(sizes, segment_in, norm_gains, projections, live_counts, cotangent):
    n_seg, n_blk, n_mp = sizes
    heads = n_seg * n_blk
    states = segment_in[0]
    rows, width = states.shape
    feats = cotangent.shape[1]
    group = projections.shape[3]
    counts = live_counts.T

    def swap(x, over_heads, over_mp, least=0):
        pairs = [
            (e * n_mp + m, (e ^ over_heads) * n_mp + (m ^ over_mp))
            for e in range(least * n_blk, heads)
            for m in range(n_mp)
        ]
        return lax.ppermute(x, AXES, pairs)

    def exchange(pieces):
        far_first = sorted(range(1, heads), key=lambda k: -((k % n_blk) * 2 + 1 - k // n_blk))
        moved = {k: swap(pieces[k], k, 0) for k in far_first}
        return [pieces[0]] + [moved[k] for k in range(1, heads)]

    far_cot = swap(cotangent, 0, 2, 1)
    tiles = group // LANES
    mixed = projections.reshape(width, 2, tiles, LANES).transpose(0, 2, 1, 3)
    mixed = mixed.reshape(width * 2 * tiles, LANES)
    chunks = 4
    wp, ws, own, spread, prim, sec = call(
        functools.partial(enter_kernel, sizes, chunks),
        "enter",
        (states, norm_gains, mixed),
        [ANYWHERE] * 3,
        [
            ((width, group), BF16),
            ((width, group), BF16),
            ((rows, feats), BF16),
            ((rows, LANES), F32),
            ((rows, group), BF16),
            ((rows, group), BF16),
        ],
        [
            pltpu.VMEM((rows, width), BF16),
            pltpu.VMEM((1, width), F32),
            pltpu.VMEM((width * 2 * tiles, LANES), BF16),
            pltpu.VMEM((rows, width), BF16),
            pltpu.VMEM((rows, group), F32),
            pltpu.VMEM((rows, group), F32),
            pltpu.SemaphoreType.DMA((chunks,)),
            pltpu.SemaphoreType.DMA((2,)),
        ],
        24,
        8 << 30,
    )
    near_from, far_cot, spread = lax.optimization_barrier((cotangent, far_cot, spread))
    near_cot = swap(near_from, 0, 1, 1)
    cross_cot = swap(far_cot, 0, 1, 1)
    made = call(
        functools.partial(pack_kernel, sizes),
        "pack",
        (counts, prim, sec, cotangent, near_cot, far_cot, cross_cot, ws),
        [SCALARS] + [INSIDE] * 7,
        [((rows, group), BF16)] + [((rows + TAIL, LANES), BF16)] * heads,
        [pltpu.VMEM((rows, group), F32)],
        16,
        1 << 30,
    )
    second, pieces = made[0], exchange(made[1:])
    pieces = call(
        functools.partial(attend_kernel, sizes),
        "attend",
        pieces,
        [INSIDE] * heads,
        [((rows, LANES), BF16)] * heads,
        [
            pltpu.VMEM((heads, rows + TAIL, LANES), BF16),
            pltpu.VMEM((heads, rows, LANES), BF16),
            pltpu.VMEM((n_blk, LANES, rows), F32),
        ],
        24,
        4 << 30,
    )
    pieces = exchange(pieces)
    sent, sent2, lp, ls = call(
        functools.partial(send_kernel, sizes),
        "send",
        (counts, prim, second, spread, wp, ws, *pieces),
        [SCALARS] + [INSIDE] * (5 + heads),
        [
            ((2, rows + TAIL, feats), BF16),
            ((2, rows, feats), BF16),
            ((rows, group), BF16),
            ((rows, group), BF16),
        ],
        [pltpu.VMEM((heads, rows, LANES), BF16)],
        16,
        2 << 30,
    )
    got = swap(sent, 0, 1)
    got2 = swap(sent2, 0, 1, 1)
    kept, kept2 = call(
        functools.partial(keep_kernel, sizes),
        "keep",
        (lp, ls, wp, ws),
        [INSIDE] * 4,
        [((2, rows, feats), BF16)] * 2,
        (),
        16,
        2 << 30,
    )
    (half,) = call(
        fold_kernel, "fold", (kept, got, sent), [INSIDE] * 3, [((rows + TAIL, feats), BF16)]
    )
    far = swap(half, 0, 2)
    (half2,) = call(
        functools.partial(fold_output_kernel, sizes),
        "fold_output",
        (kept2, got2),
        [INSIDE] * 2,
        [((rows, feats), BF16)],
    )
    far2 = swap(half2, 0, 2, 1)
    out, grad = call(
        functools.partial(leave_kernel, sizes, width),
        "leave",
        (kept, got, half, far, kept2, got2, far2, states, norm_gains, spread, own),
        [INSIDE] * 7 + [ANYWHERE] * 2 + [INSIDE] * 2,
        [((rows, feats), BF16)] * 2,
        [
            pltpu.VMEM((rows, feats), BF16),
            pltpu.VMEM((1, feats), F32),
            pltpu.VMEM((rows, feats), BF16),
            pltpu.SemaphoreType.DMA((3,)),
        ],
        out_specs=[ANYWHERE, INSIDE],
    )
    return (out[None], grad[None])


def solution(mesh):
    sizes = tuple(mesh.shape[axis] for axis in AXES)
    n_seg, n_blk, n_mp = sizes

    def body(segment_in, norm_gains, projections, live_counts, cotangent):
        heads = projections.shape[3] // DH
        rows = segment_in.shape[1]
        power = heads & (heads - 1) == 0
        fits = n_seg == 2 and n_seg * n_blk == heads and power and n_blk <= WIN
        if fits and n_mp == 4 and rows % LANES == 0 and projections.shape[3] == 4 * LANES:
            form = functools.partial(per_device_heads, sizes)
        else:
            form = per_device_windows
        return form(segment_in, norm_gains, projections, live_counts, cotangent)

    in_specs = (
        P("segment", "blk", None),
        P("segment", None),
        P("segment", None, None, "mp"),
        P(None, "blk"),
        P("blk", "mp"),
    )
    out_specs = (P("segment", "blk", "mp"), P("segment", "blk", "mp"))
    return jax.shard_map(body, mesh=mesh, in_specs=in_specs, out_specs=out_specs, check_vma=False)
```

```python
import functools

import jax
import jax.numpy as jnp
from jax import lax
from jax.experimental import pallas as pl
from jax.experimental.pallas import tpu as pltpu
from jax.sharding import PartitionSpec as P


DH = 64
WIN = 4


EPSILON = 1e-06
SCALE = 0.125
NEGATIVE = -1e30
LANES = 128
TAIL = 16
AXES = ("segment", "blk", "mp")

F32 = jnp.float32
BF16 = jnp.bfloat16


def from_behind(x, axis, by):
    size = lax.axis_size(axis)
    pairs = [(i, i + by) for i in range(size) if 0 <= i + by < size]
    return lax.ppermute(x, axis, pairs)


def normalize(states, gain_row):
    widened = states.astype(jnp.float32)
    spread = jnp.sqrt(jnp.mean(widened * widened, axis=-1, keepdims=True) + EPSILON)
    return ((widened / spread * gain_row).astype(jnp.bfloat16), spread)


def right_product(left, right):
    return lax.dot_general(
        left, right, (((1,), (1,)), ((), ())), preferred_element_type=jnp.float32
    )


def per_device_windows(segment_in, norm_gains, projections, live_counts, cotangent):
    segment_pos = lax.axis_index("segment")
    model_index = lax.axis_index("mp")
    states = segment_in[0]
    gain_row = norm_gains[0]
    row_count, full_width = states.shape
    feature_width = cotangent.shape[1]
    w_primary = projections[0, :, 0, :]
    w_secondary = projections[0, :, 1, :]
    group_width = w_primary.shape[1]
    group_heads = group_width // DH
    normed, spread = normalize(states, gain_row)
    primary = jnp.dot(normed, w_primary, preferred_element_type=jnp.float32).astype(jnp.bfloat16)
    secondary = lax.cond(
        segment_pos == 0,
        lambda: jnp.dot(normed, w_secondary, preferred_element_type=jnp.float32).astype(
            jnp.bfloat16
        ),
        lambda: jnp.zeros_like(primary),
    )
    doc_keys, doc_values = from_behind((primary, secondary), "segment", 1)
    own_block = (doc_keys, doc_values, live_counts[0])
    window = [own_block]
    moving = own_block
    for _ in range(1, WIN):
        moving = from_behind((moving[0], moving[1], moving[2]), "blk", 1)
        window.append(moving)
    position = jnp.arange(row_count, dtype=jnp.int32)
    all_keys = jnp.concatenate([piece[0] for piece in window], 0).reshape(
        WIN * row_count, group_heads, DH
    )
    all_values = jnp.concatenate([piece[1] for piece in window], 0).reshape(
        WIN * row_count, group_heads, DH
    )
    key_live = jnp.concatenate([position < piece[2][0] for piece in window], 0)
    query_live = position < live_counts[1][0]
    query_heads = primary.reshape(row_count, group_heads, DH)
    scores = (
        jnp.einsum("qhd,khd->hqk", query_heads, all_keys, preferred_element_type=jnp.float32)
        * SCALE
    )
    scores = jnp.where(key_live[None, None, :], scores, NEGATIVE)
    row_max = jnp.max(scores, axis=-1, keepdims=True)
    expo = jnp.exp(scores - row_max)
    row_total = jnp.sum(expo, axis=-1, keepdims=True)
    softmax_out = expo / row_total
    weights_low = softmax_out.astype(jnp.bfloat16)
    attended = jnp.einsum(
        "hqk,khd->qhd", weights_low, all_values, preferred_element_type=jnp.float32
    ).astype(jnp.bfloat16)
    attended = jnp.where(query_live[:, None, None], attended, jnp.zeros_like(attended)).reshape(
        row_count, group_width
    )
    projected = lax.cond(
        segment_pos == 1,
        lambda: right_product(attended, w_secondary),
        lambda: jnp.zeros((row_count, full_width), jnp.float32),
    )
    layer_out = lax.psum_scatter(
        projected.astype(jnp.bfloat16), "mp", scatter_dimension=1, tiled=True
    )
    own_normed = lax.dynamic_slice_in_dim(normed, model_index * feature_width, feature_width, 1)
    segment_out = jnp.where(segment_pos == 0, own_normed, layer_out)[None]
    grad_out = jnp.dot(
        lax.all_gather(cotangent, "mp", axis=1, tiled=True),
        w_secondary,
        preferred_element_type=jnp.float32,
    )
    grad_out = grad_out.astype(jnp.bfloat16)
    grad_out = jnp.where(query_live[:, None], grad_out, jnp.zeros_like(grad_out))
    grad_heads = grad_out.reshape(row_count, group_heads, DH)
    grad_probs = jnp.einsum(
        "qhd,khd->hqk", grad_heads, all_values, preferred_element_type=jnp.float32
    )
    row_delta = jnp.sum(softmax_out * grad_probs, axis=-1, keepdims=True)
    grad_scores = (softmax_out * (grad_probs - row_delta)).astype(jnp.bfloat16)
    grad_queries = (
        (
            SCALE
            * jnp.einsum("hqk,khd->qhd", grad_scores, all_keys, preferred_element_type=jnp.float32)
        )
        .astype(jnp.bfloat16)
        .reshape(row_count, group_width)
    )
    key_parts = (
        SCALE
        * jnp.einsum("hqk,qhd->khd", grad_scores, query_heads, preferred_element_type=jnp.float32)
    ).reshape(WIN, row_count, group_width)
    value_parts = jnp.einsum(
        "hqk,qhd->khd", weights_low, grad_heads, preferred_element_type=jnp.float32
    ).reshape(WIN, row_count, group_width)
    key_total = key_parts[WIN - 1]
    value_total = value_parts[WIN - 1]
    for offset in range(WIN - 2, -1, -1):
        arrived = (
            from_behind(key_total.astype(jnp.bfloat16), "blk", -1).astype(key_total.dtype),
            from_behind(value_total.astype(jnp.bfloat16), "blk", -1).astype(value_total.dtype),
        )
        key_total = arrived[0] + key_parts[offset]
        value_total = arrived[1] + value_parts[offset]
    grad_keys = key_total.astype(jnp.bfloat16)
    grad_values = value_total.astype(jnp.bfloat16)
    back_keys, back_values = from_behind((grad_keys, grad_values), "segment", -1)
    partial_grad = lax.cond(
        segment_pos == 0,
        lambda: right_product(back_keys, w_primary) + right_product(back_values, w_secondary),
        lambda: right_product(grad_queries, w_primary),
    )
    widened = states.astype(jnp.float32)
    summed = lax.psum_scatter(
        partial_grad.astype(jnp.bfloat16), "mp", scatter_dimension=1, tiled=True
    ).astype(jnp.float32)
    own_states = lax.dynamic_slice_in_dim(widened, model_index * feature_width, feature_width, 1)
    own_gain = lax.dynamic_slice_in_dim(gain_row, model_index * feature_width, feature_width, 0)
    row_term = lax.psum(jnp.sum(summed * own_gain * own_states, axis=-1, keepdims=True), "mp")
    input_grad = (
        own_gain * summed / spread - own_states * row_term / (full_width * spread**3)
    ).astype(jnp.bfloat16)
    return (segment_out, input_grad[None])


def place(sizes):
    seg = lax.axis_index("segment")
    return seg, seg * sizes[1] + lax.axis_index("blk"), lax.axis_index("mp")


def enter_kernel(sizes, states, gain, w, *rest):
    n_mp = sizes[2]
    wp, ws = rest[0], rest[1 : 1 + n_mp]
    own, own_states, own_gain, spread, prim, sec = rest[1 + n_mp : 7 + n_mp]
    xbuf, gbuf, wbuf, normed, pacc, sacc, sems, ready = rest[7 + n_mp :]
    seg, _, model = place(sizes)
    rows, width = xbuf.shape
    depth = width // n_mp
    tiles = wp.shape[2] // LANES
    pack = 2 * tiles
    group = 2 * LANES // pack
    lines = depth * pack
    first_copies = [
        pltpu.make_async_copy(states, xbuf, ready.at[0]),
        pltpu.make_async_copy(gain, gbuf, ready.at[1]),
    ]
    copies = []
    for c in range(n_mp):
        start = pl.multiple_of(jnp.bitwise_xor(model, c) * lines, lines)
        copies.append(
            pltpu.make_async_copy(
                w.at[pl.ds(start, lines), :], wbuf.at[pl.ds(c * lines, lines), :], sems.at[c]
            )
        )
    for copy in first_copies + copies:
        copy.start()
    here = lax.broadcasted_iota(jnp.int32, (2 * LANES, 2 * LANES), 0)
    there = lax.broadcasted_iota(jnp.int32, (2 * LANES, 2 * LANES), 1)
    source = pack * lax.rem(here, group) + lax.div(here, group)
    mix = jnp.where(there == source, 1.0, 0.0).astype(BF16)
    for copy in first_copies:
        copy.wait()
    part_rows = 32

    def norm_rows(at, _):
        line = pl.ds(pl.multiple_of(at * part_rows, part_rows), part_rows)
        wide = xbuf[line, :].astype(F32)
        mean = jnp.sum(wide * wide, axis=1, keepdims=True) * (1.0 / width)
        root = jnp.sqrt(mean + EPSILON)
        normed[line, :] = (wide * (1.0 / root) * gbuf[...]).astype(BF16)
        spread[line, :] = jnp.broadcast_to(root, (part_rows, LANES))
        return 0

    lax.fori_loop(0, rows // part_rows, norm_rows, 0)
    for c in range(n_mp):
        copies[c].wait()
        for pair in range(depth // (2 * group)):
            base = c * lines + pair * 4 * LANES
            left = wbuf[base : base + 2 * LANES, :]
            right = wbuf[base + 2 * LANES : base + 4 * LANES, :]
            both = jnp.concatenate([left, right], axis=1)
            ordered = jnp.dot(mix, both, preferred_element_type=F32).astype(BF16)
            first = 2 * pair * group
            for slot in range(pack):
                target = (wp.at[c], ws[c])[slot % 2]
                tile = slice(slot // 2 * LANES, (slot // 2 + 1) * LANES)
                part = ordered[slot * group : (slot + 1) * group, :]
                target[first : first + group, tile] = part[:, :LANES]
                target[first + group : first + 2 * group, tile] = part[:, LANES:]
        span = pl.ds(pl.multiple_of(jnp.bitwise_xor(model, c) * depth, depth), depth)
        term = jnp.dot(normed[:, span], wp[c], preferred_element_type=F32)
        if c == 0:
            pacc[...] = term
        else:
            pacc[...] += term

        @pl.when(seg == 0)
        def _():
            other = jnp.dot(normed[:, span], ws[c][...], preferred_element_type=F32)
            if c == 0:
                sacc[...] = other
            else:
                sacc[...] += other

    prim[...] = pacc[...].astype(BF16)

    @pl.when(seg == 0)
    def _():
        sec[...] = sacc[...].astype(BF16)

    mine = pl.ds(pl.multiple_of(model * depth, depth), depth)
    own[...] = normed[:, mine]
    own_states[...] = xbuf[:, mine]
    own_gain[...] = gbuf[:, mine]


def part_kernel(c0, c1, c2, w0, w1, w2, acc):
    @pl.when(lax.axis_index("segment") == 1)
    def _():
        acc[...] = jnp.dot(c0[...], w0[...], preferred_element_type=F32)
        acc[...] += jnp.dot(c1[...], w1[...], preferred_element_type=F32)
        acc[...] += jnp.dot(c2[...], w2[...], preferred_element_type=F32)


def pack_kernel(sizes, counts, prim, sec, acc, c3, w3, *rest):
    heads = sizes[0] * sizes[1]
    second, outs = rest[0], rest[1:]
    seg, entry, _ = place(sizes)
    rows = prim.shape[0]

    @pl.when(seg == 0)
    def _():
        second[...] = sec[...]

    @pl.when(seg == 1)
    def _():
        total = acc[...] + jnp.dot(c3[...], w3[...], preferred_element_type=F32)
        line = lax.broadcasted_iota(jnp.int32, acc.shape, 0)
        second[...] = jnp.where(line < counts[0, 1], total, 0.0).astype(BF16)

    tail = jnp.full((TAIL, LANES), 1.0, F32) * counts[0, 0].astype(F32)
    for head in range(heads):
        cols = slice(head * DH, (head + 1) * DH)
        pair = jnp.concatenate([prim[:, cols], second[:, cols]], axis=1)
        for k, out in enumerate(outs):

            @pl.when(jnp.bitwise_xor(entry, k) == head)
            def _():
                out[:rows, :] = pair
                out[rows:, :] = tail.astype(BF16)


def live_keys(piece, rows):
    position = lax.broadcasted_iota(jnp.int32, (1, rows), 1).astype(F32)
    count = piece[rows : rows + 1, :].astype(F32)
    return position < jnp.concatenate([count] * (rows // LANES), axis=1)


def attend_kernel(sizes, *rest):
    heads = sizes[0] * sizes[1]
    blocks = sizes[1]
    ins, outs = rest[:heads], rest[heads : 2 * heads]
    parts, back, totals = rest[2 * heads :]
    _, entry, _ = place(sizes)
    rows = outs[0].shape[0]
    for k, piece in enumerate(ins):
        parts[jnp.bitwise_xor(entry, k)] = piece[...]
    low = lax.broadcasted_iota(jnp.int32, (rows, LANES), 1) < DH
    zero = jnp.zeros((rows, LANES), BF16)
    live = [live_keys(parts[j], rows) for j in range(blocks)]
    for i in range(blocks):
        both = parts[blocks + i, :rows, :]
        query = jnp.where(low, both * BF16(SCALE), zero)
        grad = jnp.where(low, zero, both)
        flip_query = query.astype(F32).T.astype(BF16)
        flip_grad = grad.astype(F32).T.astype(BF16)
        scores = []
        for j in range(i + 1):
            product = right_product(query, parts[j, :rows, :])
            scores.append(jnp.where(live[j], product, NEGATIVE))
        top = jnp.max(functools.reduce(jnp.maximum, scores), axis=1, keepdims=True)
        expo = [jnp.exp(s - top) for s in scores]
        total = jnp.sum(functools.reduce(jnp.add, expo), axis=1, keepdims=True)
        share = 1.0 / total
        probs = [e * share for e in expo]
        slopes = [right_product(grad, parts[j, :rows, :]) for j in range(i + 1)]
        delta = functools.reduce(jnp.add, [p * g for p, g in zip(probs, slopes)])
        delta = jnp.sum(delta, axis=1, keepdims=True)
        out = jnp.zeros((rows, LANES), F32)
        other = jnp.zeros((rows, LANES), F32)
        for j in range(i + 1):
            prob = probs[j].astype(BF16)
            slope = (probs[j] * (slopes[j] - delta)).astype(BF16)
            other += jnp.dot(slope, parts[j, :rows, :], preferred_element_type=F32)
            out += jnp.dot(prob, parts[j, :rows, :], preferred_element_type=F32)
            tall = jnp.dot(flip_query, slope, preferred_element_type=F32)
            tall += jnp.dot(flip_grad, prob, preferred_element_type=F32)
            if i == j:
                totals[j] = tall
            else:
                totals[j] += tall
        back[blocks + i] = jnp.where(low, other * SCALE, out).astype(BF16)
    for j in range(blocks):
        back[j] = totals[j].T.astype(BF16)
    for k, out in enumerate(outs):
        out[...] = back[jnp.bitwise_xor(entry, k)]


def split_rows(column):
    row = jnp.broadcast_to(column, (column.shape[0], LANES)).T[:TAIL, :]
    high = row.astype(BF16).astype(F32)
    line = lax.broadcasted_iota(jnp.int32, row.shape, 0)
    return jnp.where(line == 0, high, row - high).astype(BF16)


def regroup_kernel(sizes, counts, *rest):
    heads = sizes[0] * sizes[1]
    ins, (lp, ls, parts) = rest[:heads], rest[heads:]
    seg, entry, _ = place(sizes)
    rows = lp.shape[0]
    for k, piece in enumerate(ins):
        parts[jnp.bitwise_xor(entry, k)] = piece[...]
    line = lax.broadcasted_iota(jnp.int32, (rows, DH), 0)
    alive = line < jnp.where(seg == 0, rows, counts[0, 1])
    for head in range(heads):
        cols = slice(head * DH, (head + 1) * DH)
        lp[:, cols] = parts[head, :, :DH]
        ls[:, cols] = jnp.where(alive, parts[head, :, DH:].astype(F32), 0.0).astype(BF16)


def project_block(seg, wp, ws, lp, ls, out, slot):
    rows = lp.shape[0]

    @pl.when(seg == 0)
    def _():
        total = right_product(lp[...], wp) + right_product(ls[...], ws)
        out[slot, :rows, :] = total.astype(BF16)

    @pl.when(seg == 1)
    def _():
        out[slot, :rows, :] = right_product(lp[...], wp).astype(BF16)


def send_kernel(sizes, lp, ls, prim, second, spread, wp, w3, w1, sent):
    seg, _, _ = place(sizes)
    rows, feats = prim.shape[0], sent.shape[2]
    project_block(seg, wp[3], w3[...], lp, ls, sent, 0)
    project_block(seg, wp[1], w1[...], lp, ls, sent, 1)
    term = lp[...].astype(F32) * prim[...].astype(F32)
    also = ls[...].astype(F32) * second[...].astype(F32)
    term = term + jnp.where(seg == 0, also, 0.0)
    column = jnp.sum(term, axis=1, keepdims=True) * spread[:, :1]
    sent[0, rows:, :] = jnp.zeros((TAIL, feats), BF16)
    sent[1, rows:, :] = jnp.zeros((TAIL, feats), BF16)
    sent[0, rows:, :rows] = split_rows(column)


def keep_kernel(sizes, lp, ls, wp, w2, w0, kept):
    seg, _, _ = place(sizes)
    project_block(seg, wp[2], w2[...], lp, ls, kept, 0)
    project_block(seg, wp[0], w0[...], lp, ls, kept, 1)


def layer_kernel(a0, a1, a2, a3, w0, w1, w2, w3, own, out, obuf, sem):
    seg = lax.axis_index("segment")

    @pl.when(seg == 0)
    def _():
        obuf[...] = own[...]

    @pl.when(seg == 1)
    def _():
        total = right_product(a0[...], w0[...])
        for a, w in ((a1, w1), (a2, w2), (a3, w3)):
            total += right_product(a[...], w[...])
        obuf[...] = total.astype(BF16)

    leaving = pltpu.make_async_copy(obuf, out, sem)
    leaving.start()
    leaving.wait()


def fold_kernel(kept, got, sent, out):
    rows = kept.shape[1]
    out[:rows, :] = (kept[0].astype(F32) + got[0, :rows, :].astype(F32)).astype(BF16)
    mine = sent[0, rows:, :].astype(F32)
    theirs = got[0, rows:, :].astype(F32)
    total = mine[0:1] + mine[1:2] + theirs[0:1] + theirs[1:2]
    total = jnp.broadcast_to(total, mine.shape)
    high = total.astype(BF16).astype(F32)
    line = lax.broadcasted_iota(jnp.int32, mine.shape, 0)
    out[rows:, :] = jnp.where(line == 0, high, total - high).astype(BF16)


ANYWHERE = pl.BlockSpec(memory_space=pltpu.HBM)
INSIDE = pl.BlockSpec(memory_space=pltpu.VMEM)
SCALARS = pl.BlockSpec(memory_space=pltpu.SMEM)


def call(body, ins, specs, outs, scratch=(), limit=16, flops=0, out_specs=None):
    inside = out_specs is None
    ins = [
        pltpu.with_memory_space_constraint(x, pltpu.HBM) if spec is ANYWHERE else x
        for x, spec in zip(ins, specs)
    ]
    return pl.pallas_call(
        body,
        in_specs=list(specs),
        out_specs=[INSIDE] * len(outs) if inside else out_specs,
        out_shape=[(pltpu.VMEM if inside else jax.ShapeDtypeStruct)(s, d) for s, d in outs],
        scratch_shapes=list(scratch),
        compiler_params=pltpu.CompilerParams(vmem_limit_bytes=limit << 20),
        cost_estimate=pl.CostEstimate(flops=flops, transcendentals=0, bytes_accessed=1 << 20),
    )(*ins)


def leave_kernel(width, kept, got, half, far, states, gain, spread, grad):
    rows = states.shape[0]
    ends = half[rows:, :].astype(F32) + far[rows:, :].astype(F32)
    row = jnp.broadcast_to(ends[0:1, :rows] + ends[1:2, :rows], (LANES, rows))
    term = row.T[:, :1]
    root = spread[:, :1]
    scaled = term / (width * root * root * root)
    total = kept[1].astype(F32) + got[1, :rows, :].astype(F32) + far[:rows, :].astype(F32)
    grad[...] = (gain[...] * total * (1.0 / root) - states[...].astype(F32) * scaled).astype(BF16)


def per_device_heads(sizes, segment_in, norm_gains, projections, live_counts, cotangent):
    n_seg, n_blk, n_mp = sizes
    heads = n_seg * n_blk
    states = segment_in[0]
    rows, width = states.shape
    feats = cotangent.shape[1]
    group = projections.shape[3]
    counts = live_counts.T

    def swap(x, over_heads, over_mp, least=0):
        pairs = [
            (e * n_mp + m, (e ^ over_heads) * n_mp + (m ^ over_mp))
            for e in range(least * n_blk, heads)
            for m in range(n_mp)
        ]
        return lax.ppermute(x, AXES, pairs)

    def exchange(pieces):
        far_first = sorted(range(1, heads), key=lambda k: -((k % n_blk) * 2 + 1 - k // n_blk))
        moved = {k: swap(pieces[k], k, 0) for k in far_first}
        return [pieces[0]] + [moved[k] for k in range(1, heads)]

    far_cot = swap(cotangent, 0, 2, 1)
    tiles = group // LANES
    mixed = projections.reshape(width, 2, tiles, LANES).transpose(0, 2, 1, 3)
    mixed = mixed.reshape(width * 2 * tiles, LANES)
    made = call(
        functools.partial(enter_kernel, sizes),
        (states, norm_gains, mixed),
        [ANYWHERE] * 3,
        [((n_mp, feats, group), BF16)]
        + [((feats, group), BF16)] * n_mp
        + [
            ((rows, feats), BF16),
            ((rows, feats), BF16),
            ((1, feats), F32),
            ((rows, LANES), F32),
            ((rows, group), BF16),
            ((rows, group), BF16),
        ],
        [
            pltpu.VMEM((rows, width), BF16),
            pltpu.VMEM((1, width), F32),
            pltpu.VMEM((width * 2 * tiles, LANES), BF16),
            pltpu.VMEM((rows, width), BF16),
            pltpu.VMEM((rows, group), F32),
            pltpu.VMEM((rows, group), F32),
            pltpu.SemaphoreType.DMA((n_mp,)),
            pltpu.SemaphoreType.DMA((2,)),
        ],
        24,
        8 << 30,
    )
    wp, ws = made[0], made[1 : 1 + n_mp]
    own, own_states, own_gain, spread, prim, sec = made[1 + n_mp :]
    near_from, spread = lax.optimization_barrier((cotangent, spread))
    near_cot = swap(near_from, 0, 1, 1)
    lent_1 = swap(ws[1], 0, 1, 1)
    far_cot, spread = lax.optimization_barrier((far_cot, spread))
    cross_cot = swap(far_cot, 0, 1, 1)
    acc = call(
        part_kernel,
        (cotangent, near_cot, far_cot, *ws[:3]),
        [INSIDE] * 6,
        [((rows, group), F32)],
        (),
        16,
        1 << 30,
    )[0]
    lent_2, lent_3, far_cot = lax.optimization_barrier((ws[2], ws[3], far_cot))
    lent_2 = swap(lent_2, 0, 2, 1)
    lent_3 = swap(lent_3, 0, 3, 1)
    made = call(
        functools.partial(pack_kernel, sizes),
        (counts, prim, sec, acc, cross_cot, ws[3]),
        [SCALARS] + [INSIDE] * 5,
        [((rows, group), BF16)] + [((rows + TAIL, LANES), BF16)] * heads,
        (),
        16,
        1 << 30,
    )
    second, pieces = made[0], made[1:]
    pieces = exchange(pieces)
    pieces = call(
        functools.partial(attend_kernel, sizes),
        pieces,
        [INSIDE] * heads,
        [((rows, LANES), BF16)] * heads,
        [
            pltpu.VMEM((heads, rows + TAIL, LANES), BF16),
            pltpu.VMEM((heads, rows, LANES), BF16),
            pltpu.VMEM((n_blk, LANES, rows), F32),
        ],
        24,
        4 << 30,
    )
    pieces = exchange(pieces)
    lp, ls = call(
        functools.partial(regroup_kernel, sizes),
        (counts, *pieces),
        [SCALARS] + [INSIDE] * heads,
        [((rows, group), BF16)] * 2,
        [pltpu.VMEM((heads, rows, LANES), BF16)],
    )
    far_att = swap(ls, 0, 2, 1)
    (sent,) = call(
        functools.partial(send_kernel, sizes),
        (lp, ls, prim, second, spread, wp, ws[3], ws[1]),
        [INSIDE] * 8,
        [((2, rows + TAIL, feats), BF16)],
        (),
        16,
        2 << 30,
    )
    got = swap(sent, 0, 1)
    (kept,) = call(
        functools.partial(keep_kernel, sizes),
        (lp, ls, wp, ws[2], ws[0]),
        [INSIDE] * 5,
        [((2, rows, feats), BF16)],
        (),
        16,
        2 << 30,
    )
    (half,) = call(fold_kernel, (kept, got, sent), [INSIDE] * 3, [((rows + TAIL, feats), BF16)])
    far = swap(half, 0, 2)
    far_att, own_att, half_seen = lax.optimization_barrier((far_att, ls, half))
    near_att = swap(own_att, 0, 1, 1)
    cross_att = swap(far_att, 0, 1, 1)
    (out,) = call(
        layer_kernel,
        (ls, near_att, far_att, cross_att, ws[0], lent_1, lent_2, lent_3, own),
        [INSIDE] * 9,
        [((rows, feats), BF16)],
        [pltpu.VMEM((rows, feats), BF16), pltpu.SemaphoreType.DMA],
        16,
        2 << 30,
        [ANYWHERE],
    )
    (grad,) = call(
        functools.partial(leave_kernel, width),
        (kept, got, half_seen, far, own_states, own_gain, spread),
        [INSIDE] * 7,
        [((rows, feats), BF16)],
        out_specs=[INSIDE],
    )
    return (out[None], grad[None])


def solution(mesh):
    sizes = tuple(mesh.shape[axis] for axis in AXES)
    n_seg, n_blk, n_mp = sizes
    by_heads = n_seg == 2 and n_blk <= WIN and n_blk & (n_blk - 1) == 0 and n_mp == 4

    def body(segment_in, norm_gains, projections, live_counts, cotangent):
        rows, group = segment_in.shape[1], projections.shape[3]
        if by_heads:
            assert n_seg * n_blk * DH == group and group == 4 * LANES and rows % LANES == 0
            return per_device_heads(
                sizes, segment_in, norm_gains, projections, live_counts, cotangent
            )
        return per_device_windows(segment_in, norm_gains, projections, live_counts, cotangent)

    in_specs = (
        P("segment", "blk", None),
        P("segment", None),
        P("segment", None, None, "mp"),
        P(None, "blk"),
        P("blk", "mp"),
    )
    out_specs = (P("segment", "blk", "mp"), P("segment", "blk", "mp"))
    return jax.shard_map(body, mesh=mesh, in_specs=in_specs, out_specs=out_specs, check_vma=False)
```

```python
import functools

import jax
import jax.numpy as jnp
from jax import lax
from jax.experimental import pallas as pl
from jax.experimental.pallas import tpu as pltpu
from jax.sharding import PartitionSpec as P


DH = 64
WIN = 4


EPSILON = 1e-06
SCALE = 0.125
NEGATIVE = -1e30
LANES = 128
TAIL = 16
AXES = ("segment", "blk", "mp")

F32 = jnp.float32
BF16 = jnp.bfloat16


def from_behind(x, axis, by):
    size = lax.axis_size(axis)
    pairs = [(i, i + by) for i in range(size) if 0 <= i + by < size]
    return lax.ppermute(x, axis, pairs)


def normalize(states, gain_row):
    widened = states.astype(jnp.float32)
    spread = jnp.sqrt(jnp.mean(widened * widened, axis=-1, keepdims=True) + EPSILON)
    return ((widened / spread * gain_row).astype(jnp.bfloat16), spread)


def right_product(left, right):
    return lax.dot_general(
        left, right, (((1,), (1,)), ((), ())), preferred_element_type=jnp.float32
    )


def per_device_windows(segment_in, norm_gains, projections, live_counts, cotangent):
    segment_pos = lax.axis_index("segment")
    model_index = lax.axis_index("mp")
    states = segment_in[0]
    gain_row = norm_gains[0]
    row_count, full_width = states.shape
    feature_width = cotangent.shape[1]
    w_primary = projections[0, :, 0, :]
    w_secondary = projections[0, :, 1, :]
    group_width = w_primary.shape[1]
    group_heads = group_width // DH
    normed, spread = normalize(states, gain_row)
    primary = jnp.dot(normed, w_primary, preferred_element_type=jnp.float32).astype(jnp.bfloat16)
    secondary = lax.cond(
        segment_pos == 0,
        lambda: jnp.dot(normed, w_secondary, preferred_element_type=jnp.float32).astype(
            jnp.bfloat16
        ),
        lambda: jnp.zeros_like(primary),
    )
    doc_keys, doc_values = from_behind((primary, secondary), "segment", 1)
    own_block = (doc_keys, doc_values, live_counts[0])
    window = [own_block]
    moving = own_block
    for _ in range(1, WIN):
        moving = from_behind((moving[0], moving[1], moving[2]), "blk", 1)
        window.append(moving)
    position = jnp.arange(row_count, dtype=jnp.int32)
    all_keys = jnp.concatenate([piece[0] for piece in window], 0).reshape(
        WIN * row_count, group_heads, DH
    )
    all_values = jnp.concatenate([piece[1] for piece in window], 0).reshape(
        WIN * row_count, group_heads, DH
    )
    key_live = jnp.concatenate([position < piece[2][0] for piece in window], 0)
    query_live = position < live_counts[1][0]
    query_heads = primary.reshape(row_count, group_heads, DH)
    scores = (
        jnp.einsum("qhd,khd->hqk", query_heads, all_keys, preferred_element_type=jnp.float32)
        * SCALE
    )
    scores = jnp.where(key_live[None, None, :], scores, NEGATIVE)
    row_max = jnp.max(scores, axis=-1, keepdims=True)
    expo = jnp.exp(scores - row_max)
    row_total = jnp.sum(expo, axis=-1, keepdims=True)
    softmax_out = expo / row_total
    weights_low = softmax_out.astype(jnp.bfloat16)
    attended = jnp.einsum(
        "hqk,khd->qhd", weights_low, all_values, preferred_element_type=jnp.float32
    ).astype(jnp.bfloat16)
    attended = jnp.where(query_live[:, None, None], attended, jnp.zeros_like(attended)).reshape(
        row_count, group_width
    )
    projected = lax.cond(
        segment_pos == 1,
        lambda: right_product(attended, w_secondary),
        lambda: jnp.zeros((row_count, full_width), jnp.float32),
    )
    layer_out = lax.psum_scatter(
        projected.astype(jnp.bfloat16), "mp", scatter_dimension=1, tiled=True
    )
    own_normed = lax.dynamic_slice_in_dim(normed, model_index * feature_width, feature_width, 1)
    segment_out = jnp.where(segment_pos == 0, own_normed, layer_out)[None]
    grad_out = jnp.dot(
        lax.all_gather(cotangent, "mp", axis=1, tiled=True),
        w_secondary,
        preferred_element_type=jnp.float32,
    )
    grad_out = grad_out.astype(jnp.bfloat16)
    grad_out = jnp.where(query_live[:, None], grad_out, jnp.zeros_like(grad_out))
    grad_heads = grad_out.reshape(row_count, group_heads, DH)
    grad_probs = jnp.einsum(
        "qhd,khd->hqk", grad_heads, all_values, preferred_element_type=jnp.float32
    )
    row_delta = jnp.sum(softmax_out * grad_probs, axis=-1, keepdims=True)
    grad_scores = (softmax_out * (grad_probs - row_delta)).astype(jnp.bfloat16)
    grad_queries = (
        (
            SCALE
            * jnp.einsum("hqk,khd->qhd", grad_scores, all_keys, preferred_element_type=jnp.float32)
        )
        .astype(jnp.bfloat16)
        .reshape(row_count, group_width)
    )
    key_parts = (
        SCALE
        * jnp.einsum("hqk,qhd->khd", grad_scores, query_heads, preferred_element_type=jnp.float32)
    ).reshape(WIN, row_count, group_width)
    value_parts = jnp.einsum(
        "hqk,qhd->khd", weights_low, grad_heads, preferred_element_type=jnp.float32
    ).reshape(WIN, row_count, group_width)
    key_total = key_parts[WIN - 1]
    value_total = value_parts[WIN - 1]
    for offset in range(WIN - 2, -1, -1):
        arrived = (
            from_behind(key_total.astype(jnp.bfloat16), "blk", -1).astype(key_total.dtype),
            from_behind(value_total.astype(jnp.bfloat16), "blk", -1).astype(value_total.dtype),
        )
        key_total = arrived[0] + key_parts[offset]
        value_total = arrived[1] + value_parts[offset]
    grad_keys = key_total.astype(jnp.bfloat16)
    grad_values = value_total.astype(jnp.bfloat16)
    back_keys, back_values = from_behind((grad_keys, grad_values), "segment", -1)
    partial_grad = lax.cond(
        segment_pos == 0,
        lambda: right_product(back_keys, w_primary) + right_product(back_values, w_secondary),
        lambda: right_product(grad_queries, w_primary),
    )
    widened = states.astype(jnp.float32)
    summed = lax.psum_scatter(
        partial_grad.astype(jnp.bfloat16), "mp", scatter_dimension=1, tiled=True
    ).astype(jnp.float32)
    own_states = lax.dynamic_slice_in_dim(widened, model_index * feature_width, feature_width, 1)
    own_gain = lax.dynamic_slice_in_dim(gain_row, model_index * feature_width, feature_width, 0)
    row_term = lax.psum(jnp.sum(summed * own_gain * own_states, axis=-1, keepdims=True), "mp")
    input_grad = (
        own_gain * summed / spread - own_states * row_term / (full_width * spread**3)
    ).astype(jnp.bfloat16)
    return (segment_out, input_grad[None])


def place(sizes):
    seg = lax.axis_index("segment")
    return seg, seg * sizes[1] + lax.axis_index("blk"), lax.axis_index("mp")


def enter_kernel(sizes, states, gain, w, *rest):
    n_mp = sizes[2]
    wp, ws = rest[0], rest[1 : 1 + n_mp]
    own, own_states, own_gain, spread, prim, sec = rest[1 + n_mp : 7 + n_mp]
    xbuf, gbuf, wbuf, normed, pacc, sacc, sems, ready = rest[7 + n_mp :]
    seg, _, model = place(sizes)
    rows, width = xbuf.shape
    depth = width // n_mp
    tiles = wp.shape[2] // LANES
    pack = 2 * tiles
    group = 2 * LANES // pack
    lines = depth * pack
    first_copies = [
        pltpu.make_async_copy(states, xbuf, ready.at[0]),
        pltpu.make_async_copy(gain, gbuf, ready.at[1]),
    ]
    copies = []
    for c in range(n_mp):
        start = pl.multiple_of(jnp.bitwise_xor(model, c) * lines, lines)
        copies.append(
            pltpu.make_async_copy(
                w.at[pl.ds(start, lines), :], wbuf.at[pl.ds(c * lines, lines), :], sems.at[c]
            )
        )
    for copy in first_copies + copies:
        copy.start()
    here = lax.broadcasted_iota(jnp.int32, (2 * LANES, 2 * LANES), 0)
    there = lax.broadcasted_iota(jnp.int32, (2 * LANES, 2 * LANES), 1)
    source = pack * lax.rem(here, group) + lax.div(here, group)
    mix = jnp.where(there == source, 1.0, 0.0).astype(BF16)
    for copy in first_copies:
        copy.wait()
    part_rows = 32

    def norm_rows(at, _):
        line = pl.ds(pl.multiple_of(at * part_rows, part_rows), part_rows)
        wide = xbuf[line, :].astype(F32)
        mean = jnp.sum(wide * wide, axis=1, keepdims=True) * (1.0 / width)
        root = jnp.sqrt(mean + EPSILON)
        normed[line, :] = (wide * (1.0 / root) * gbuf[...]).astype(BF16)
        spread[line, :] = jnp.broadcast_to(root, (part_rows, LANES))
        return 0

    lax.fori_loop(0, rows // part_rows, norm_rows, 0)
    for c in range(n_mp):
        copies[c].wait()
        for pair in range(depth // (2 * group)):
            base = c * lines + pair * 4 * LANES
            left = wbuf[base : base + 2 * LANES, :]
            right = wbuf[base + 2 * LANES : base + 4 * LANES, :]
            both = jnp.concatenate([left, right], axis=1)
            ordered = jnp.dot(mix, both, preferred_element_type=F32).astype(BF16)
            first = 2 * pair * group
            for slot in range(pack):
                target = (wp.at[c], ws[c])[slot % 2]
                tile = slice(slot // 2 * LANES, (slot // 2 + 1) * LANES)
                part = ordered[slot * group : (slot + 1) * group, :]
                target[first : first + group, tile] = part[:, :LANES]
                target[first + group : first + 2 * group, tile] = part[:, LANES:]
        span = pl.ds(pl.multiple_of(jnp.bitwise_xor(model, c) * depth, depth), depth)
        term = jnp.dot(normed[:, span], wp[c], preferred_element_type=F32)
        if c == 0:
            pacc[...] = term
        else:
            pacc[...] += term

        @pl.when(seg == 0)
        def _():
            other = jnp.dot(normed[:, span], ws[c][...], preferred_element_type=F32)
            if c == 0:
                sacc[...] = other
            else:
                sacc[...] += other

    prim[...] = pacc[...].astype(BF16)

    @pl.when(seg == 0)
    def _():
        sec[...] = sacc[...].astype(BF16)

    mine = pl.ds(pl.multiple_of(model * depth, depth), depth)
    own[...] = normed[:, mine]
    own_states[...] = xbuf[:, mine]
    own_gain[...] = gbuf[:, mine]


def part_kernel(c0, c1, c2, w0, w1, w2, acc):
    @pl.when(lax.axis_index("segment") == 1)
    def _():
        acc[...] = jnp.dot(c0[...], w0[...], preferred_element_type=F32)
        acc[...] += jnp.dot(c1[...], w1[...], preferred_element_type=F32)
        acc[...] += jnp.dot(c2[...], w2[...], preferred_element_type=F32)


def pack_kernel(sizes, counts, prim, sec, acc, c3, w3, *rest):
    heads = sizes[0] * sizes[1]
    second, outs = rest[0], rest[1:]
    seg, entry, _ = place(sizes)
    rows = prim.shape[0]

    @pl.when(seg == 0)
    def _():
        second[...] = sec[...]

    @pl.when(seg == 1)
    def _():
        total = acc[...] + jnp.dot(c3[...], w3[...], preferred_element_type=F32)
        line = lax.broadcasted_iota(jnp.int32, acc.shape, 0)
        second[...] = jnp.where(line < counts[0, 1], total, 0.0).astype(BF16)

    tail = jnp.full((TAIL, LANES), 1.0, F32) * counts[0, 0].astype(F32)
    for head in range(heads):
        cols = slice(head * DH, (head + 1) * DH)
        pair = jnp.concatenate([prim[:, cols], second[:, cols]], axis=1)
        for k, out in enumerate(outs):

            @pl.when(jnp.bitwise_xor(entry, k) == head)
            def _():
                out[:rows, :] = pair
                out[rows:, :] = tail.astype(BF16)


def live_keys(piece, rows):
    position = lax.broadcasted_iota(jnp.int32, (1, rows), 1).astype(F32)
    count = piece[rows : rows + 1, :].astype(F32)
    return position < jnp.concatenate([count] * (rows // LANES), axis=1)


def attend_kernel(sizes, *rest):
    heads = sizes[0] * sizes[1]
    blocks = sizes[1]
    ins, outs = rest[:heads], rest[heads : 2 * heads]
    parts, back, totals = rest[2 * heads :]
    _, entry, _ = place(sizes)
    rows = outs[0].shape[0]
    for k, piece in enumerate(ins):
        parts[jnp.bitwise_xor(entry, k)] = piece[...]
    low = lax.broadcasted_iota(jnp.int32, (rows, LANES), 1) < DH
    zero = jnp.zeros((rows, LANES), BF16)
    live = [live_keys(parts[j], rows) for j in range(blocks)]
    for i in range(blocks):
        both = parts[blocks + i, :rows, :]
        query = jnp.where(low, both * BF16(SCALE), zero)
        grad = jnp.where(low, zero, both)
        flip_query = query.astype(F32).T.astype(BF16)
        flip_grad = grad.astype(F32).T.astype(BF16)
        scores = []
        for j in range(i + 1):
            product = right_product(query, parts[j, :rows, :])
            scores.append(jnp.where(live[j], product, NEGATIVE))
        top = jnp.max(functools.reduce(jnp.maximum, scores), axis=1, keepdims=True)
        expo = [jnp.exp(s - top) for s in scores]
        total = jnp.sum(functools.reduce(jnp.add, expo), axis=1, keepdims=True)
        share = 1.0 / total
        probs = [e * share for e in expo]
        slopes = [right_product(grad, parts[j, :rows, :]) for j in range(i + 1)]
        delta = functools.reduce(jnp.add, [p * g for p, g in zip(probs, slopes)])
        delta = jnp.sum(delta, axis=1, keepdims=True)
        out = jnp.zeros((rows, LANES), F32)
        other = jnp.zeros((rows, LANES), F32)
        for j in range(i + 1):
            prob = probs[j].astype(BF16)
            slope = (probs[j] * (slopes[j] - delta)).astype(BF16)
            other += jnp.dot(slope, parts[j, :rows, :], preferred_element_type=F32)
            out += jnp.dot(prob, parts[j, :rows, :], preferred_element_type=F32)
            tall = jnp.dot(flip_query, slope, preferred_element_type=F32)
            tall += jnp.dot(flip_grad, prob, preferred_element_type=F32)
            if i == j:
                totals[j] = tall
            else:
                totals[j] += tall
        back[blocks + i] = jnp.where(low, other * SCALE, out).astype(BF16)
    for j in range(blocks):
        back[j] = totals[j].T.astype(BF16)
    for k, out in enumerate(outs):
        out[...] = back[jnp.bitwise_xor(entry, k)]


def split_rows(column):
    row = jnp.broadcast_to(column, (column.shape[0], LANES)).T[:TAIL, :]
    high = row.astype(BF16).astype(F32)
    line = lax.broadcasted_iota(jnp.int32, row.shape, 0)
    return jnp.where(line == 0, high, row - high).astype(BF16)


def regroup_kernel(sizes, counts, *rest):
    heads = sizes[0] * sizes[1]
    ins, (lp, ls, parts) = rest[:heads], rest[heads:]
    seg, entry, _ = place(sizes)
    rows = lp.shape[0]
    for k, piece in enumerate(ins):
        parts[jnp.bitwise_xor(entry, k)] = piece[...]
    line = lax.broadcasted_iota(jnp.int32, (rows, DH), 0)
    alive = line < jnp.where(seg == 0, rows, counts[0, 1])
    for head in range(heads):
        cols = slice(head * DH, (head + 1) * DH)
        lp[:, cols] = parts[head, :, :DH]
        ls[:, cols] = jnp.where(alive, parts[head, :, DH:].astype(F32), 0.0).astype(BF16)


def project_block(seg, wp, ws, lp, ls, out, slot):
    rows = lp.shape[0]

    @pl.when(seg == 0)
    def _():
        total = right_product(lp[...], wp) + right_product(ls[...], ws)
        out[slot, :rows, :] = total.astype(BF16)

    @pl.when(seg == 1)
    def _():
        out[slot, :rows, :] = right_product(lp[...], wp).astype(BF16)


def send_kernel(sizes, lp, ls, prim, second, spread, wp, w3, w1, sent):
    seg, _, _ = place(sizes)
    rows, feats = prim.shape[0], sent.shape[2]
    project_block(seg, wp[3], w3[...], lp, ls, sent, 0)
    project_block(seg, wp[1], w1[...], lp, ls, sent, 1)
    term = lp[...].astype(F32) * prim[...].astype(F32)
    also = ls[...].astype(F32) * second[...].astype(F32)
    term = term + jnp.where(seg == 0, also, 0.0)
    column = jnp.sum(term, axis=1, keepdims=True) * spread[:, :1]
    sent[0, rows:, :] = jnp.zeros((TAIL, feats), BF16)
    sent[1, rows:, :] = jnp.zeros((TAIL, feats), BF16)
    sent[0, rows:, :rows] = split_rows(column)


def keep_kernel(sizes, lp, ls, wp, w2, w0, kept):
    seg, _, _ = place(sizes)
    project_block(seg, wp[2], w2[...], lp, ls, kept, 0)
    project_block(seg, wp[0], w0[...], lp, ls, kept, 1)


def layer_kernel(a0, a1, a2, a3, w0, w1, w2, w3, own, out, obuf, sem):
    seg = lax.axis_index("segment")

    @pl.when(seg == 0)
    def _():
        obuf[...] = own[...]

    @pl.when(seg == 1)
    def _():
        total = right_product(a0[...], w0[...])
        for a, w in ((a1, w1), (a2, w2), (a3, w3)):
            total += right_product(a[...], w[...])
        obuf[...] = total.astype(BF16)

    leaving = pltpu.make_async_copy(obuf, out, sem)
    leaving.start()
    leaving.wait()


def fold_kernel(kept, got, sent, out):
    rows = kept.shape[1]
    out[:rows, :] = (kept[0].astype(F32) + got[0, :rows, :].astype(F32)).astype(BF16)
    mine = sent[0, rows:, :].astype(F32)
    theirs = got[0, rows:, :].astype(F32)
    total = mine[0:1] + mine[1:2] + theirs[0:1] + theirs[1:2]
    total = jnp.broadcast_to(total, mine.shape)
    high = total.astype(BF16).astype(F32)
    line = lax.broadcasted_iota(jnp.int32, mine.shape, 0)
    out[rows:, :] = jnp.where(line == 0, high, total - high).astype(BF16)


ANYWHERE = pl.BlockSpec(memory_space=pltpu.HBM)
INSIDE = pl.BlockSpec(memory_space=pltpu.VMEM)
SCALARS = pl.BlockSpec(memory_space=pltpu.SMEM)


def call(body, ins, specs, outs, scratch=(), limit=16, flops=0, out_specs=None):
    inside = out_specs is None
    ins = [
        pltpu.with_memory_space_constraint(x, pltpu.HBM) if spec is ANYWHERE else x
        for x, spec in zip(ins, specs)
    ]
    return pl.pallas_call(
        body,
        in_specs=list(specs),
        out_specs=[INSIDE] * len(outs) if inside else out_specs,
        out_shape=[(pltpu.VMEM if inside else jax.ShapeDtypeStruct)(s, d) for s, d in outs],
        scratch_shapes=list(scratch),
        compiler_params=pltpu.CompilerParams(vmem_limit_bytes=limit << 20),
        cost_estimate=pl.CostEstimate(flops=flops, transcendentals=0, bytes_accessed=1 << 20),
    )(*ins)


def scales_kernel(width, spread, inverse, shrink):
    root = spread[...]
    inverse[...] = 1.0 / root
    shrink[...] = 1.0 / (width * root * root * root)


def leave_kernel(kept, got, half, far, states, gain, inverse, shrink, grad):
    rows = states.shape[0]
    ends = half[rows:, :].astype(F32) + far[rows:, :].astype(F32)
    row = jnp.broadcast_to(ends[0:1, :rows] + ends[1:2, :rows], (LANES, rows))
    term = row.T[:, :1]
    scaled = term * shrink[:, :1]
    total = kept[1].astype(F32) + got[1, :rows, :].astype(F32) + far[:rows, :].astype(F32)
    grad[...] = (gain[...] * total * inverse[:, :1] - states[...].astype(F32) * scaled).astype(BF16)


def per_device_heads(sizes, segment_in, norm_gains, projections, live_counts, cotangent):
    n_seg, n_blk, n_mp = sizes
    heads = n_seg * n_blk
    states = segment_in[0]
    rows, width = states.shape
    feats = cotangent.shape[1]
    group = projections.shape[3]
    counts = live_counts.T

    def swap(x, over_heads, over_mp, least=0):
        pairs = [
            (e * n_mp + m, (e ^ over_heads) * n_mp + (m ^ over_mp))
            for e in range(least * n_blk, heads)
            for m in range(n_mp)
        ]
        return lax.ppermute(x, AXES, pairs)

    far_first = sorted(range(1, heads), key=lambda k: -((k % n_blk) * 2 + 1 - k // n_blk))

    def exchange(pieces):
        moved = {}
        for k in far_first:
            moved[k] = swap(pieces[k], k, 0)
        return [pieces[0]] + [moved[k] for k in range(1, heads)]

    far_cot = swap(cotangent, 0, 2, 1)
    near_cot = swap(cotangent, 0, 1, 1)
    tiles = group // LANES
    mixed = projections.reshape(width, 2, tiles, LANES).transpose(0, 2, 1, 3)
    mixed = mixed.reshape(width * 2 * tiles, LANES)
    made = call(
        functools.partial(enter_kernel, sizes),
        (states, norm_gains, mixed),
        [ANYWHERE] * 3,
        [((n_mp, feats, group), BF16)]
        + [((feats, group), BF16)] * n_mp
        + [
            ((rows, feats), BF16),
            ((rows, feats), BF16),
            ((1, feats), F32),
            ((rows, LANES), F32),
            ((rows, group), BF16),
            ((rows, group), BF16),
        ],
        [
            pltpu.VMEM((rows, width), BF16),
            pltpu.VMEM((1, width), F32),
            pltpu.VMEM((width * 2 * tiles, LANES), BF16),
            pltpu.VMEM((rows, width), BF16),
            pltpu.VMEM((rows, group), F32),
            pltpu.VMEM((rows, group), F32),
            pltpu.SemaphoreType.DMA((n_mp,)),
            pltpu.SemaphoreType.DMA((2,)),
        ],
        24,
        8 << 30,
    )
    wp, ws = made[0], made[1 : 1 + n_mp]
    own, own_states, own_gain, spread, prim, sec = made[1 + n_mp :]
    lent_1 = swap(ws[1], 0, 1, 1)
    far_cot, spread = lax.optimization_barrier((far_cot, spread))
    cross_cot = swap(far_cot, 0, 1, 1)
    acc = call(
        part_kernel,
        (cotangent, near_cot, far_cot, *ws[:3]),
        [INSIDE] * 6,
        [((rows, group), F32)],
        (),
        16,
        1 << 30,
    )[0]
    lent_2, lent_3, far_cot = lax.optimization_barrier((ws[2], ws[3], far_cot))
    lent_2 = swap(lent_2, 0, 2, 1)
    lent_3 = swap(lent_3, 0, 3, 1)
    made = call(
        functools.partial(pack_kernel, sizes),
        (counts, prim, sec, acc, cross_cot, ws[3]),
        [SCALARS] + [INSIDE] * 5,
        [((rows, group), BF16)] + [((rows + TAIL, LANES), BF16)] * heads,
        (),
        16,
        1 << 30,
    )
    second, pieces = made[0], made[1:]
    pieces = exchange(pieces)
    inverse, shrink = call(
        functools.partial(scales_kernel, width), (spread,), [INSIDE], [((rows, LANES), F32)] * 2
    )
    pieces = call(
        functools.partial(attend_kernel, sizes),
        pieces,
        [INSIDE] * heads,
        [((rows, LANES), BF16)] * heads,
        [
            pltpu.VMEM((heads, rows + TAIL, LANES), BF16),
            pltpu.VMEM((heads, rows, LANES), BF16),
            pltpu.VMEM((n_blk, LANES, rows), F32),
        ],
        24,
        4 << 30,
    )
    pieces = exchange(pieces)
    lp, ls = call(
        functools.partial(regroup_kernel, sizes),
        (counts, *pieces),
        [SCALARS] + [INSIDE] * heads,
        [((rows, group), BF16)] * 2,
        [pltpu.VMEM((heads, rows, LANES), BF16)],
    )
    far_att = swap(ls, 0, 2, 1)
    (sent,) = call(
        functools.partial(send_kernel, sizes),
        (lp, ls, prim, second, spread, wp, ws[3], ws[1]),
        [INSIDE] * 8,
        [((2, rows + TAIL, feats), BF16)],
        (),
        16,
        2 << 30,
    )
    got = swap(sent, 0, 1)
    (kept,) = call(
        functools.partial(keep_kernel, sizes),
        (lp, ls, wp, ws[2], ws[0]),
        [INSIDE] * 5,
        [((2, rows, feats), BF16)],
        (),
        16,
        2 << 30,
    )
    (half,) = call(fold_kernel, (kept, got, sent), [INSIDE] * 3, [((rows + TAIL, feats), BF16)])
    far = swap(half, 0, 2)
    far_att, own_att, half_seen = lax.optimization_barrier((far_att, ls, half))
    near_att = swap(own_att, 0, 1, 1)
    cross_att = swap(far_att, 0, 1, 1)
    (out,) = call(
        layer_kernel,
        (ls, near_att, far_att, cross_att, ws[0], lent_1, lent_2, lent_3, own),
        [INSIDE] * 9,
        [((rows, feats), BF16)],
        [pltpu.VMEM((rows, feats), BF16), pltpu.SemaphoreType.DMA],
        16,
        2 << 30,
        [ANYWHERE],
    )
    (grad,) = call(
        leave_kernel,
        (kept, got, half_seen, far, own_states, own_gain, inverse, shrink),
        [INSIDE] * 8,
        [((rows, feats), BF16)],
        out_specs=[INSIDE],
    )
    return (out[None], grad[None])


def solution(mesh):
    sizes = tuple(mesh.shape[axis] for axis in AXES)
    n_seg, n_blk, n_mp = sizes
    by_heads = n_seg == 2 and n_blk <= WIN and n_blk & (n_blk - 1) == 0 and n_mp == 4

    def body(segment_in, norm_gains, projections, live_counts, cotangent):
        rows, group = segment_in.shape[1], projections.shape[3]
        if by_heads:
            assert n_seg * n_blk * DH == group and group == 4 * LANES and rows % LANES == 0
            return per_device_heads(
                sizes, segment_in, norm_gains, projections, live_counts, cotangent
            )
        return per_device_windows(segment_in, norm_gains, projections, live_counts, cotangent)

    in_specs = (
        P("segment", "blk", None),
        P("segment", None),
        P("segment", None, None, "mp"),
        P(None, "blk"),
        P("blk", "mp"),
    )
    out_specs = (P("segment", "blk", "mp"), P("segment", "blk", "mp"))
    return jax.shard_map(body, mesh=mesh, in_specs=in_specs, out_specs=out_specs, check_vma=False)
```

```python
import functools

import jax
import jax.numpy as jnp
from jax import lax
from jax.experimental import pallas as pl
from jax.experimental.pallas import tpu as pltpu
from jax.sharding import PartitionSpec as P


DH = 64
WIN = 4


EPSILON = 1e-06
SCALE = 0.125
NEGATIVE = -1e30
LANES = 128
TAIL = 16
AXES = ("segment", "blk", "mp")

F32 = jnp.float32
BF16 = jnp.bfloat16


def from_behind(x, axis, by):
    size = lax.axis_size(axis)
    pairs = [(i, i + by) for i in range(size) if 0 <= i + by < size]
    return lax.ppermute(x, axis, pairs)


def normalize(states, gain_row):
    widened = states.astype(jnp.float32)
    spread = jnp.sqrt(jnp.mean(widened * widened, axis=-1, keepdims=True) + EPSILON)
    return ((widened / spread * gain_row).astype(jnp.bfloat16), spread)


def right_product(left, right):
    return lax.dot_general(
        left, right, (((1,), (1,)), ((), ())), preferred_element_type=jnp.float32
    )


def per_device_windows(segment_in, norm_gains, projections, live_counts, cotangent):
    segment_pos = lax.axis_index("segment")
    model_index = lax.axis_index("mp")
    states = segment_in[0]
    gain_row = norm_gains[0]
    row_count, full_width = states.shape
    feature_width = cotangent.shape[1]
    w_primary = projections[0, :, 0, :]
    w_secondary = projections[0, :, 1, :]
    group_width = w_primary.shape[1]
    group_heads = group_width // DH
    normed, spread = normalize(states, gain_row)
    primary = jnp.dot(normed, w_primary, preferred_element_type=jnp.float32).astype(jnp.bfloat16)
    secondary = lax.cond(
        segment_pos == 0,
        lambda: jnp.dot(normed, w_secondary, preferred_element_type=jnp.float32).astype(
            jnp.bfloat16
        ),
        lambda: jnp.zeros_like(primary),
    )
    doc_keys, doc_values = from_behind((primary, secondary), "segment", 1)
    own_block = (doc_keys, doc_values, live_counts[0])
    window = [own_block]
    moving = own_block
    for _ in range(1, WIN):
        moving = from_behind((moving[0], moving[1], moving[2]), "blk", 1)
        window.append(moving)
    position = jnp.arange(row_count, dtype=jnp.int32)
    all_keys = jnp.concatenate([piece[0] for piece in window], 0).reshape(
        WIN * row_count, group_heads, DH
    )
    all_values = jnp.concatenate([piece[1] for piece in window], 0).reshape(
        WIN * row_count, group_heads, DH
    )
    key_live = jnp.concatenate([position < piece[2][0] for piece in window], 0)
    query_live = position < live_counts[1][0]
    query_heads = primary.reshape(row_count, group_heads, DH)
    scores = (
        jnp.einsum("qhd,khd->hqk", query_heads, all_keys, preferred_element_type=jnp.float32)
        * SCALE
    )
    scores = jnp.where(key_live[None, None, :], scores, NEGATIVE)
    row_max = jnp.max(scores, axis=-1, keepdims=True)
    expo = jnp.exp(scores - row_max)
    row_total = jnp.sum(expo, axis=-1, keepdims=True)
    softmax_out = expo / row_total
    weights_low = softmax_out.astype(jnp.bfloat16)
    attended = jnp.einsum(
        "hqk,khd->qhd", weights_low, all_values, preferred_element_type=jnp.float32
    ).astype(jnp.bfloat16)
    attended = jnp.where(query_live[:, None, None], attended, jnp.zeros_like(attended)).reshape(
        row_count, group_width
    )
    projected = lax.cond(
        segment_pos == 1,
        lambda: right_product(attended, w_secondary),
        lambda: jnp.zeros((row_count, full_width), jnp.float32),
    )
    layer_out = lax.psum_scatter(
        projected.astype(jnp.bfloat16), "mp", scatter_dimension=1, tiled=True
    )
    own_normed = lax.dynamic_slice_in_dim(normed, model_index * feature_width, feature_width, 1)
    segment_out = jnp.where(segment_pos == 0, own_normed, layer_out)[None]
    grad_out = jnp.dot(
        lax.all_gather(cotangent, "mp", axis=1, tiled=True),
        w_secondary,
        preferred_element_type=jnp.float32,
    )
    grad_out = grad_out.astype(jnp.bfloat16)
    grad_out = jnp.where(query_live[:, None], grad_out, jnp.zeros_like(grad_out))
    grad_heads = grad_out.reshape(row_count, group_heads, DH)
    grad_probs = jnp.einsum(
        "qhd,khd->hqk", grad_heads, all_values, preferred_element_type=jnp.float32
    )
    row_delta = jnp.sum(softmax_out * grad_probs, axis=-1, keepdims=True)
    grad_scores = (softmax_out * (grad_probs - row_delta)).astype(jnp.bfloat16)
    grad_queries = (
        (
            SCALE
            * jnp.einsum("hqk,khd->qhd", grad_scores, all_keys, preferred_element_type=jnp.float32)
        )
        .astype(jnp.bfloat16)
        .reshape(row_count, group_width)
    )
    key_parts = (
        SCALE
        * jnp.einsum("hqk,qhd->khd", grad_scores, query_heads, preferred_element_type=jnp.float32)
    ).reshape(WIN, row_count, group_width)
    value_parts = jnp.einsum(
        "hqk,qhd->khd", weights_low, grad_heads, preferred_element_type=jnp.float32
    ).reshape(WIN, row_count, group_width)
    key_total = key_parts[WIN - 1]
    value_total = value_parts[WIN - 1]
    for offset in range(WIN - 2, -1, -1):
        arrived = (
            from_behind(key_total.astype(jnp.bfloat16), "blk", -1).astype(key_total.dtype),
            from_behind(value_total.astype(jnp.bfloat16), "blk", -1).astype(value_total.dtype),
        )
        key_total = arrived[0] + key_parts[offset]
        value_total = arrived[1] + value_parts[offset]
    grad_keys = key_total.astype(jnp.bfloat16)
    grad_values = value_total.astype(jnp.bfloat16)
    back_keys, back_values = from_behind((grad_keys, grad_values), "segment", -1)
    partial_grad = lax.cond(
        segment_pos == 0,
        lambda: right_product(back_keys, w_primary) + right_product(back_values, w_secondary),
        lambda: right_product(grad_queries, w_primary),
    )
    widened = states.astype(jnp.float32)
    summed = lax.psum_scatter(
        partial_grad.astype(jnp.bfloat16), "mp", scatter_dimension=1, tiled=True
    ).astype(jnp.float32)
    own_states = lax.dynamic_slice_in_dim(widened, model_index * feature_width, feature_width, 1)
    own_gain = lax.dynamic_slice_in_dim(gain_row, model_index * feature_width, feature_width, 0)
    row_term = lax.psum(jnp.sum(summed * own_gain * own_states, axis=-1, keepdims=True), "mp")
    input_grad = (
        own_gain * summed / spread - own_states * row_term / (full_width * spread**3)
    ).astype(jnp.bfloat16)
    return (segment_out, input_grad[None])


def place(sizes):
    seg = lax.axis_index("segment")
    return seg, seg * sizes[1] + lax.axis_index("blk"), lax.axis_index("mp")


def enter_kernel(sizes, states, gain, w, *rest):
    n_mp = sizes[2]
    wp, ws = rest[0], rest[1 : 1 + n_mp]
    own, own_states, own_gain, spread, prim, sec = rest[1 + n_mp : 7 + n_mp]
    xbuf, gbuf, wbuf, normed, pacc, sacc, sems, ready = rest[7 + n_mp :]
    seg, _, model = place(sizes)
    rows, width = xbuf.shape
    depth = width // n_mp
    tiles = wp.shape[2] // LANES
    pack = 2 * tiles
    group = 2 * LANES // pack
    lines = depth * pack
    first_copies = [
        pltpu.make_async_copy(states, xbuf, ready.at[0]),
        pltpu.make_async_copy(gain, gbuf, ready.at[1]),
    ]
    copies = []
    for c in range(n_mp):
        start = pl.multiple_of(jnp.bitwise_xor(model, c) * lines, lines)
        copies.append(
            pltpu.make_async_copy(
                w.at[pl.ds(start, lines), :], wbuf.at[pl.ds(c * lines, lines), :], sems.at[c]
            )
        )
    for copy in first_copies + copies:
        copy.start()
    here = lax.broadcasted_iota(jnp.int32, (2 * LANES, 2 * LANES), 0)
    there = lax.broadcasted_iota(jnp.int32, (2 * LANES, 2 * LANES), 1)
    source = pack * lax.rem(here, group) + lax.div(here, group)
    mix = jnp.where(there == source, 1.0, 0.0).astype(BF16)
    for copy in first_copies:
        copy.wait()
    part_rows = 32

    def norm_rows(at, _):
        line = pl.ds(pl.multiple_of(at * part_rows, part_rows), part_rows)
        wide = xbuf[line, :].astype(F32)
        mean = jnp.sum(wide * wide, axis=1, keepdims=True) * (1.0 / width)
        root = jnp.sqrt(mean + EPSILON)
        normed[line, :] = (wide * (1.0 / root) * gbuf[...]).astype(BF16)
        spread[line, :] = jnp.broadcast_to(root, (part_rows, LANES))
        return 0

    lax.fori_loop(0, rows // part_rows, norm_rows, 0)
    for c in range(n_mp):
        copies[c].wait()
        for pair in range(depth // (2 * group)):
            base = c * lines + pair * 4 * LANES
            left = wbuf[base : base + 2 * LANES, :]
            right = wbuf[base + 2 * LANES : base + 4 * LANES, :]
            both = jnp.concatenate([left, right], axis=1)
            ordered = jnp.dot(mix, both, preferred_element_type=F32).astype(BF16)
            first = 2 * pair * group
            for slot in range(pack):
                target = (wp.at[c], ws[c])[slot % 2]
                tile = slice(slot // 2 * LANES, (slot // 2 + 1) * LANES)
                part = ordered[slot * group : (slot + 1) * group, :]
                target[first : first + group, tile] = part[:, :LANES]
                target[first + group : first + 2 * group, tile] = part[:, LANES:]
        span = pl.ds(pl.multiple_of(jnp.bitwise_xor(model, c) * depth, depth), depth)
        term = jnp.dot(normed[:, span], wp[c], preferred_element_type=F32)
        if c == 0:
            pacc[...] = term
        else:
            pacc[...] += term

        @pl.when(seg == 0)
        def _():
            other = jnp.dot(normed[:, span], ws[c][...], preferred_element_type=F32)
            if c == 0:
                sacc[...] = other
            else:
                sacc[...] += other

    prim[...] = pacc[...].astype(BF16)

    @pl.when(seg == 0)
    def _():
        sec[...] = sacc[...].astype(BF16)

    mine = pl.ds(pl.multiple_of(model * depth, depth), depth)
    own[...] = normed[:, mine]
    own_states[...] = xbuf[:, mine]
    own_gain[...] = gbuf[:, mine]


def part_kernel(c0, c1, c2, w0, w1, w2, acc):
    @pl.when(lax.axis_index("segment") == 1)
    def _():
        acc[...] = jnp.dot(c0[...], w0[...], preferred_element_type=F32)
        acc[...] += jnp.dot(c1[...], w1[...], preferred_element_type=F32)
        acc[...] += jnp.dot(c2[...], w2[...], preferred_element_type=F32)


def pack_kernel(sizes, counts, prim, sec, acc, c3, w3, *rest):
    heads = sizes[0] * sizes[1]
    second, outs = rest[0], rest[1:]
    seg, entry, _ = place(sizes)
    rows = prim.shape[0]

    @pl.when(seg == 0)
    def _():
        second[...] = sec[...]

    @pl.when(seg == 1)
    def _():
        total = acc[...] + jnp.dot(c3[...], w3[...], preferred_element_type=F32)
        line = lax.broadcasted_iota(jnp.int32, acc.shape, 0)
        second[...] = jnp.where(line < counts[0, 1], total, 0.0).astype(BF16)

    tail = jnp.full((TAIL, LANES), 1.0, F32) * counts[0, 0].astype(F32)
    for head in range(heads):
        cols = slice(head * DH, (head + 1) * DH)
        pair = jnp.concatenate([prim[:, cols], second[:, cols]], axis=1)
        for k, out in enumerate(outs):

            @pl.when(jnp.bitwise_xor(entry, k) == head)
            def _():
                out[:rows, :] = pair
                out[rows:, :] = tail.astype(BF16)


def live_keys(piece, rows):
    position = lax.broadcasted_iota(jnp.int32, (1, rows), 1).astype(F32)
    count = piece[rows : rows + 1, :].astype(F32)
    return position < jnp.concatenate([count] * (rows // LANES), axis=1)


def attend_kernel(sizes, *rest):
    heads = sizes[0] * sizes[1]
    blocks = sizes[1]
    ins, outs = rest[:heads], rest[heads : 2 * heads]
    parts, back, totals = rest[2 * heads :]
    _, entry, _ = place(sizes)
    rows = outs[0].shape[0]
    for k, piece in enumerate(ins):
        parts[jnp.bitwise_xor(entry, k)] = piece[...]
    low = lax.broadcasted_iota(jnp.int32, (rows, LANES), 1) < DH
    zero = jnp.zeros((rows, LANES), BF16)
    live = [live_keys(parts[j], rows) for j in range(blocks)]
    for i in range(blocks):
        both = parts[blocks + i, :rows, :]
        query = jnp.where(low, both * BF16(SCALE), zero)
        grad = jnp.where(low, zero, both)
        flip_query = query.astype(F32).T.astype(BF16)
        flip_grad = grad.astype(F32).T.astype(BF16)
        scores = []
        for j in range(i + 1):
            product = right_product(query, parts[j, :rows, :])
            scores.append(jnp.where(live[j], product, NEGATIVE))
        top = jnp.max(functools.reduce(jnp.maximum, scores), axis=1, keepdims=True)
        expo = [jnp.exp(s - top) for s in scores]
        total = jnp.sum(functools.reduce(jnp.add, expo), axis=1, keepdims=True)
        share = 1.0 / total
        probs = [e * share for e in expo]
        slopes = [right_product(grad, parts[j, :rows, :]) for j in range(i + 1)]
        delta = functools.reduce(jnp.add, [p * g for p, g in zip(probs, slopes)])
        delta = jnp.sum(delta, axis=1, keepdims=True)
        out = jnp.zeros((rows, LANES), F32)
        other = jnp.zeros((rows, LANES), F32)
        for j in range(i + 1):
            prob = probs[j].astype(BF16)
            slope = (probs[j] * (slopes[j] - delta)).astype(BF16)
            other += jnp.dot(slope, parts[j, :rows, :], preferred_element_type=F32)
            out += jnp.dot(prob, parts[j, :rows, :], preferred_element_type=F32)
            tall = jnp.dot(flip_query, slope, preferred_element_type=F32)
            tall += jnp.dot(flip_grad, prob, preferred_element_type=F32)
            if i == j:
                totals[j] = tall
            else:
                totals[j] += tall
        back[blocks + i] = jnp.where(low, other * SCALE, out).astype(BF16)
    for j in range(blocks):
        back[j] = totals[j].T.astype(BF16)
    for k, out in enumerate(outs):
        out[...] = back[jnp.bitwise_xor(entry, k)]


def split_rows(column):
    row = jnp.broadcast_to(column, (column.shape[0], LANES)).T[:TAIL, :]
    high = row.astype(BF16).astype(F32)
    line = lax.broadcasted_iota(jnp.int32, row.shape, 0)
    return jnp.where(line == 0, high, row - high).astype(BF16)


def regroup_kernel(sizes, counts, *rest):
    heads = sizes[0] * sizes[1]
    ins, (lp, ls, parts) = rest[:heads], rest[heads:]
    seg, entry, _ = place(sizes)
    rows = lp.shape[0]
    for k, piece in enumerate(ins):
        parts[jnp.bitwise_xor(entry, k)] = piece[...]
    line = lax.broadcasted_iota(jnp.int32, (rows, DH), 0)
    alive = line < jnp.where(seg == 0, rows, counts[0, 1])
    for head in range(heads):
        cols = slice(head * DH, (head + 1) * DH)
        lp[:, cols] = parts[head, :, :DH]
        ls[:, cols] = jnp.where(alive, parts[head, :, DH:].astype(F32), 0.0).astype(BF16)


def project_block(seg, wp, ws, lp, ls, out, slot):
    rows = lp.shape[0]

    @pl.when(seg == 0)
    def _():
        total = right_product(lp[...], wp) + right_product(ls[...], ws)
        out[slot, :rows, :] = total.astype(BF16)

    @pl.when(seg == 1)
    def _():
        out[slot, :rows, :] = right_product(lp[...], wp).astype(BF16)


def send_kernel(sizes, lp, ls, prim, second, spread, wp, w3, w1, sent):
    seg, _, _ = place(sizes)
    rows, feats = prim.shape[0], sent.shape[2]
    project_block(seg, wp[3], w3[...], lp, ls, sent, 0)
    project_block(seg, wp[1], w1[...], lp, ls, sent, 1)
    term = lp[...].astype(F32) * prim[...].astype(F32)
    also = ls[...].astype(F32) * second[...].astype(F32)
    term = term + jnp.where(seg == 0, also, 0.0)
    column = jnp.sum(term, axis=1, keepdims=True) * spread[:, :1]
    sent[0, rows:, :] = jnp.zeros((TAIL, feats), BF16)
    sent[1, rows:, :] = jnp.zeros((TAIL, feats), BF16)
    sent[0, rows:, :rows] = split_rows(column)


def keep_kernel(sizes, lp, ls, wp, w2, w0, kept):
    seg, _, _ = place(sizes)
    project_block(seg, wp[2], w2[...], lp, ls, kept, 0)
    project_block(seg, wp[0], w0[...], lp, ls, kept, 1)


def layer_kernel(a0, a1, a2, a3, w0, w1, w2, w3, own, out, obuf, sem):
    seg = lax.axis_index("segment")

    @pl.when(seg == 0)
    def _():
        obuf[...] = own[...]

    @pl.when(seg == 1)
    def _():
        total = right_product(a0[...], w0[...])
        for a, w in ((a1, w1), (a2, w2), (a3, w3)):
            total += right_product(a[...], w[...])
        obuf[...] = total.astype(BF16)

    leaving = pltpu.make_async_copy(obuf, out, sem)
    leaving.start()
    leaving.wait()


def fold_kernel(kept, got, sent, out):
    rows = kept.shape[1]
    out[:rows, :] = (kept[0].astype(F32) + got[0, :rows, :].astype(F32)).astype(BF16)
    mine = sent[0, rows:, :].astype(F32)
    theirs = got[0, rows:, :].astype(F32)
    total = mine[0:1] + mine[1:2] + theirs[0:1] + theirs[1:2]
    total = jnp.broadcast_to(total, mine.shape)
    high = total.astype(BF16).astype(F32)
    line = lax.broadcasted_iota(jnp.int32, mine.shape, 0)
    out[rows:, :] = jnp.where(line == 0, high, total - high).astype(BF16)


ANYWHERE = pl.BlockSpec(memory_space=pltpu.HBM)
INSIDE = pl.BlockSpec(memory_space=pltpu.VMEM)
SCALARS = pl.BlockSpec(memory_space=pltpu.SMEM)


def call(body, ins, specs, outs, scratch=(), limit=16, flops=0, out_specs=None):
    inside = out_specs is None
    ins = [
        pltpu.with_memory_space_constraint(x, pltpu.HBM) if spec is ANYWHERE else x
        for x, spec in zip(ins, specs)
    ]
    return pl.pallas_call(
        body,
        in_specs=list(specs),
        out_specs=[INSIDE] * len(outs) if inside else out_specs,
        out_shape=[(pltpu.VMEM if inside else jax.ShapeDtypeStruct)(s, d) for s, d in outs],
        scratch_shapes=list(scratch),
        compiler_params=pltpu.CompilerParams(vmem_limit_bytes=limit << 20),
        cost_estimate=pl.CostEstimate(flops=flops, transcendentals=0, bytes_accessed=1 << 20),
    )(*ins)


def inverse_kernel(spread, inverse):
    inverse[...] = 1.0 / spread[...]


def shrink_kernel(width, spread, shrink):
    root = spread[...]
    shrink[...] = 1.0 / (width * root * root * root)


def leave_kernel(kept, got, half, far, states, gain, inverse, shrink, grad):
    rows = states.shape[0]
    ends = half[rows:, :].astype(F32) + far[rows:, :].astype(F32)
    row = jnp.broadcast_to(ends[0:1, :rows] + ends[1:2, :rows], (LANES, rows))
    term = row.T[:, :1]
    scaled = term * shrink[:, :1]
    total = kept[1].astype(F32) + got[1, :rows, :].astype(F32) + far[:rows, :].astype(F32)
    grad[...] = (gain[...] * total * inverse[:, :1] - states[...].astype(F32) * scaled).astype(BF16)


def per_device_heads(sizes, segment_in, norm_gains, projections, live_counts, cotangent):
    n_seg, n_blk, n_mp = sizes
    heads = n_seg * n_blk
    states = segment_in[0]
    rows, width = states.shape
    feats = cotangent.shape[1]
    group = projections.shape[3]
    counts = live_counts.T

    def swap(x, over_heads, over_mp, senders=range(n_seg)):
        pairs = [
            (e * n_mp + m, (e ^ over_heads) * n_mp + (m ^ over_mp))
            for e in range(heads)
            for m in range(n_mp)
            if e // n_blk in senders
        ]
        return lax.ppermute(x, AXES, pairs)

    document, summary = (0,), (1,)

    def exchange(pieces):
        moved = [pieces[0]]
        for k in range(1, heads):
            moved.append(swap(pieces[k], k, 0))
        return moved

    far_cot = swap(cotangent, 0, 2, summary)
    near_cot = swap(cotangent, 0, 1, summary)
    tiles = group // LANES
    mixed = projections.reshape(width, 2, tiles, LANES).transpose(0, 2, 1, 3)
    mixed = mixed.reshape(width * 2 * tiles, LANES)
    made = call(
        functools.partial(enter_kernel, sizes),
        (states, norm_gains, mixed),
        [ANYWHERE] * 3,
        [((n_mp, feats, group), BF16)]
        + [((feats, group), BF16)] * n_mp
        + [
            ((rows, feats), BF16),
            ((rows, feats), BF16),
            ((1, feats), F32),
            ((rows, LANES), F32),
            ((rows, group), BF16),
            ((rows, group), BF16),
        ],
        [
            pltpu.VMEM((rows, width), BF16),
            pltpu.VMEM((1, width), F32),
            pltpu.VMEM((width * 2 * tiles, LANES), BF16),
            pltpu.VMEM((rows, width), BF16),
            pltpu.VMEM((rows, group), F32),
            pltpu.VMEM((rows, group), F32),
            pltpu.SemaphoreType.DMA((n_mp,)),
            pltpu.SemaphoreType.DMA((2,)),
        ],
        24,
        8 << 30,
    )
    wp, ws = made[0], made[1 : 1 + n_mp]
    own, own_states, own_gain, spread, prim, sec = made[1 + n_mp :]
    lent_3 = swap(ws[3], n_blk, 3, summary)
    far_cot, spread = lax.optimization_barrier((far_cot, spread))
    cross_cot = swap(far_cot, 0, 1, summary)
    acc = call(
        part_kernel,
        (cotangent, near_cot, far_cot, *ws[:3]),
        [INSIDE] * 6,
        [((rows, group), F32)],
        (),
        16,
        1 << 30,
    )[0]
    made = call(
        functools.partial(pack_kernel, sizes),
        (counts, prim, sec, acc, cross_cot, ws[3]),
        [SCALARS] + [INSIDE] * 5,
        [((rows, group), BF16)] + [((rows + TAIL, LANES), BF16)] * heads,
        (),
        16,
        1 << 30,
    )
    second, pieces = made[0], made[1:]
    pieces = exchange(pieces)
    lent_2 = swap(ws[2], 0, 2, summary)
    (inverse,) = call(inverse_kernel, (spread,), [INSIDE], [((rows, LANES), F32)])
    pieces = call(
        functools.partial(attend_kernel, sizes),
        pieces,
        [INSIDE] * heads,
        [((rows, LANES), BF16)] * heads,
        [
            pltpu.VMEM((heads, rows + TAIL, LANES), BF16),
            pltpu.VMEM((heads, rows, LANES), BF16),
            pltpu.VMEM((n_blk, LANES, rows), F32),
        ],
        24,
        4 << 30,
    )
    pieces = exchange(pieces)
    lent_3 = swap(lent_3, n_blk, 0, document)
    (shrink,) = call(
        functools.partial(shrink_kernel, width), (spread,), [INSIDE], [((rows, LANES), F32)]
    )
    lp, ls = call(
        functools.partial(regroup_kernel, sizes),
        (counts, *pieces),
        [SCALARS] + [INSIDE] * heads,
        [((rows, group), BF16)] * 2,
        [pltpu.VMEM((heads, rows, LANES), BF16)],
    )
    far_att = swap(ls, 0, 2, summary)
    (sent,) = call(
        functools.partial(send_kernel, sizes),
        (lp, ls, prim, second, spread, wp, ws[3], ws[1]),
        [INSIDE] * 8,
        [((2, rows + TAIL, feats), BF16)],
        (),
        16,
        2 << 30,
    )
    got = swap(sent, 0, 1)
    (kept,) = call(
        functools.partial(keep_kernel, sizes),
        (lp, ls, wp, ws[2], ws[0]),
        [INSIDE] * 5,
        [((2, rows, feats), BF16)],
        (),
        16,
        2 << 30,
    )
    (half,) = call(fold_kernel, (kept, got, sent), [INSIDE] * 3, [((rows + TAIL, feats), BF16)])
    far = swap(half, 0, 2)
    far_att, own_att, lent_1, half_seen = lax.optimization_barrier((far_att, ls, ws[1], half))
    lent_1 = swap(lent_1, 0, 1, summary)
    near_att = swap(own_att, 0, 1, summary)
    cross_att = swap(far_att, 0, 1, summary)
    (out,) = call(
        layer_kernel,
        (ls, near_att, far_att, cross_att, ws[0], lent_1, lent_2, lent_3, own),
        [INSIDE] * 9,
        [((rows, feats), BF16)],
        [pltpu.VMEM((rows, feats), BF16), pltpu.SemaphoreType.DMA],
        16,
        2 << 30,
        [ANYWHERE],
    )
    (grad,) = call(
        leave_kernel,
        (kept, got, half_seen, far, own_states, own_gain, inverse, shrink),
        [INSIDE] * 8,
        [((rows, feats), BF16)],
        out_specs=[INSIDE],
    )
    return (out[None], grad[None])


def solution(mesh):
    sizes = tuple(mesh.shape[axis] for axis in AXES)
    n_seg, n_blk, n_mp = sizes
    by_heads = n_seg == 2 and n_blk <= WIN and n_blk & (n_blk - 1) == 0 and n_mp == 4

    def body(segment_in, norm_gains, projections, live_counts, cotangent):
        rows, group = segment_in.shape[1], projections.shape[3]
        if by_heads:
            assert n_seg * n_blk * DH == group and group == 4 * LANES and rows % LANES == 0
            return per_device_heads(
                sizes, segment_in, norm_gains, projections, live_counts, cotangent
            )
        return per_device_windows(segment_in, norm_gains, projections, live_counts, cotangent)

    in_specs = (
        P("segment", "blk", None),
        P("segment", None),
        P("segment", None, None, "mp"),
        P(None, "blk"),
        P("blk", "mp"),
    )
    out_specs = (P("segment", "blk", "mp"), P("segment", "blk", "mp"))
    return jax.shard_map(body, mesh=mesh, in_specs=in_specs, out_specs=out_specs, check_vma=False)
```

```python
import functools

import jax
import jax.numpy as jnp
from jax import lax
from jax.experimental import pallas as pl
from jax.experimental.pallas import tpu as pltpu
from jax.sharding import PartitionSpec as P


DH = 64
WIN = 4


EPSILON = 1e-06
SCALE = 0.125
NEGATIVE = -1e30
LANES = 128
TAIL = 16
AXES = ("segment", "blk", "mp")

F32 = jnp.float32
BF16 = jnp.bfloat16


def from_behind(x, axis, by):
    size = lax.axis_size(axis)
    pairs = [(i, i + by) for i in range(size) if 0 <= i + by < size]
    return lax.ppermute(x, axis, pairs)


def normalize(states, gain_row):
    widened = states.astype(jnp.float32)
    spread = jnp.sqrt(jnp.mean(widened * widened, axis=-1, keepdims=True) + EPSILON)
    return ((widened / spread * gain_row).astype(jnp.bfloat16), spread)


def right_product(left, right):
    return lax.dot_general(
        left, right, (((1,), (1,)), ((), ())), preferred_element_type=jnp.float32
    )


def per_device_windows(segment_in, norm_gains, projections, live_counts, cotangent):
    segment_pos = lax.axis_index("segment")
    model_index = lax.axis_index("mp")
    states = segment_in[0]
    gain_row = norm_gains[0]
    row_count, full_width = states.shape
    feature_width = cotangent.shape[1]
    w_primary = projections[0, :, 0, :]
    w_secondary = projections[0, :, 1, :]
    group_width = w_primary.shape[1]
    group_heads = group_width // DH
    normed, spread = normalize(states, gain_row)
    primary = jnp.dot(normed, w_primary, preferred_element_type=jnp.float32).astype(jnp.bfloat16)
    secondary = lax.cond(
        segment_pos == 0,
        lambda: jnp.dot(normed, w_secondary, preferred_element_type=jnp.float32).astype(
            jnp.bfloat16
        ),
        lambda: jnp.zeros_like(primary),
    )
    doc_keys, doc_values = from_behind((primary, secondary), "segment", 1)
    own_block = (doc_keys, doc_values, live_counts[0])
    window = [own_block]
    moving = own_block
    for _ in range(1, WIN):
        moving = from_behind((moving[0], moving[1], moving[2]), "blk", 1)
        window.append(moving)
    position = jnp.arange(row_count, dtype=jnp.int32)
    all_keys = jnp.concatenate([piece[0] for piece in window], 0).reshape(
        WIN * row_count, group_heads, DH
    )
    all_values = jnp.concatenate([piece[1] for piece in window], 0).reshape(
        WIN * row_count, group_heads, DH
    )
    key_live = jnp.concatenate([position < piece[2][0] for piece in window], 0)
    query_live = position < live_counts[1][0]
    query_heads = primary.reshape(row_count, group_heads, DH)
    scores = (
        jnp.einsum("qhd,khd->hqk", query_heads, all_keys, preferred_element_type=jnp.float32)
        * SCALE
    )
    scores = jnp.where(key_live[None, None, :], scores, NEGATIVE)
    row_max = jnp.max(scores, axis=-1, keepdims=True)
    expo = jnp.exp(scores - row_max)
    row_total = jnp.sum(expo, axis=-1, keepdims=True)
    softmax_out = expo / row_total
    weights_low = softmax_out.astype(jnp.bfloat16)
    attended = jnp.einsum(
        "hqk,khd->qhd", weights_low, all_values, preferred_element_type=jnp.float32
    ).astype(jnp.bfloat16)
    attended = jnp.where(query_live[:, None, None], attended, jnp.zeros_like(attended)).reshape(
        row_count, group_width
    )
    projected = lax.cond(
        segment_pos == 1,
        lambda: right_product(attended, w_secondary),
        lambda: jnp.zeros((row_count, full_width), jnp.float32),
    )
    layer_out = lax.psum_scatter(
        projected.astype(jnp.bfloat16), "mp", scatter_dimension=1, tiled=True
    )
    own_normed = lax.dynamic_slice_in_dim(normed, model_index * feature_width, feature_width, 1)
    segment_out = jnp.where(segment_pos == 0, own_normed, layer_out)[None]
    grad_out = jnp.dot(
        lax.all_gather(cotangent, "mp", axis=1, tiled=True),
        w_secondary,
        preferred_element_type=jnp.float32,
    )
    grad_out = grad_out.astype(jnp.bfloat16)
    grad_out = jnp.where(query_live[:, None], grad_out, jnp.zeros_like(grad_out))
    grad_heads = grad_out.reshape(row_count, group_heads, DH)
    grad_probs = jnp.einsum(
        "qhd,khd->hqk", grad_heads, all_values, preferred_element_type=jnp.float32
    )
    row_delta = jnp.sum(softmax_out * grad_probs, axis=-1, keepdims=True)
    grad_scores = (softmax_out * (grad_probs - row_delta)).astype(jnp.bfloat16)
    grad_queries = (
        (
            SCALE
            * jnp.einsum("hqk,khd->qhd", grad_scores, all_keys, preferred_element_type=jnp.float32)
        )
        .astype(jnp.bfloat16)
        .reshape(row_count, group_width)
    )
    key_parts = (
        SCALE
        * jnp.einsum("hqk,qhd->khd", grad_scores, query_heads, preferred_element_type=jnp.float32)
    ).reshape(WIN, row_count, group_width)
    value_parts = jnp.einsum(
        "hqk,qhd->khd", weights_low, grad_heads, preferred_element_type=jnp.float32
    ).reshape(WIN, row_count, group_width)
    key_total = key_parts[WIN - 1]
    value_total = value_parts[WIN - 1]
    for offset in range(WIN - 2, -1, -1):
        arrived = (
            from_behind(key_total.astype(jnp.bfloat16), "blk", -1).astype(key_total.dtype),
            from_behind(value_total.astype(jnp.bfloat16), "blk", -1).astype(value_total.dtype),
        )
        key_total = arrived[0] + key_parts[offset]
        value_total = arrived[1] + value_parts[offset]
    grad_keys = key_total.astype(jnp.bfloat16)
    grad_values = value_total.astype(jnp.bfloat16)
    back_keys, back_values = from_behind((grad_keys, grad_values), "segment", -1)
    partial_grad = lax.cond(
        segment_pos == 0,
        lambda: right_product(back_keys, w_primary) + right_product(back_values, w_secondary),
        lambda: right_product(grad_queries, w_primary),
    )
    widened = states.astype(jnp.float32)
    summed = lax.psum_scatter(
        partial_grad.astype(jnp.bfloat16), "mp", scatter_dimension=1, tiled=True
    ).astype(jnp.float32)
    own_states = lax.dynamic_slice_in_dim(widened, model_index * feature_width, feature_width, 1)
    own_gain = lax.dynamic_slice_in_dim(gain_row, model_index * feature_width, feature_width, 0)
    row_term = lax.psum(jnp.sum(summed * own_gain * own_states, axis=-1, keepdims=True), "mp")
    input_grad = (
        own_gain * summed / spread - own_states * row_term / (full_width * spread**3)
    ).astype(jnp.bfloat16)
    return (segment_out, input_grad[None])


def place(sizes):
    seg = lax.axis_index("segment")
    return seg, seg * sizes[1] + lax.axis_index("blk"), lax.axis_index("mp")


def enter_kernel(sizes, states, gain, w, *rest):
    n_mp = sizes[2]
    wp, ws = rest[0], rest[1 : 1 + n_mp]
    own, own_states, own_gain, spread, prim, sec = rest[1 + n_mp : 7 + n_mp]
    xbuf, gbuf, wbuf, normed, pacc, sacc, sems, ready = rest[7 + n_mp :]
    seg, _, model = place(sizes)
    rows, width = xbuf.shape
    depth = width // n_mp
    tiles = wp.shape[2] // LANES
    pack = 2 * tiles
    group = 2 * LANES // pack
    lines = depth * pack
    first_copies = [
        pltpu.make_async_copy(states, xbuf, ready.at[0]),
        pltpu.make_async_copy(gain, gbuf, ready.at[1]),
    ]
    copies = []
    for c in range(n_mp):
        start = pl.multiple_of(jnp.bitwise_xor(model, c) * lines, lines)
        copies.append(
            pltpu.make_async_copy(
                w.at[pl.ds(start, lines), :], wbuf.at[pl.ds(c * lines, lines), :], sems.at[c]
            )
        )
    for copy in first_copies + copies:
        copy.start()
    here = lax.broadcasted_iota(jnp.int32, (2 * LANES, 2 * LANES), 0)
    there = lax.broadcasted_iota(jnp.int32, (2 * LANES, 2 * LANES), 1)
    source = pack * lax.rem(here, group) + lax.div(here, group)
    mix = jnp.where(there == source, 1.0, 0.0).astype(BF16)
    for copy in first_copies:
        copy.wait()
    part_rows = 32

    def norm_rows(at, _):
        line = pl.ds(pl.multiple_of(at * part_rows, part_rows), part_rows)
        wide = xbuf[line, :].astype(F32)
        mean = jnp.sum(wide * wide, axis=1, keepdims=True) * (1.0 / width)
        root = jnp.sqrt(mean + EPSILON)
        normed[line, :] = (wide * (1.0 / root) * gbuf[...]).astype(BF16)
        spread[line, :] = jnp.broadcast_to(root, (part_rows, LANES))
        return 0

    lax.fori_loop(0, rows // part_rows, norm_rows, 0)
    for c in range(n_mp):
        copies[c].wait()
        for pair in range(depth // (2 * group)):
            base = c * lines + pair * 4 * LANES
            left = wbuf[base : base + 2 * LANES, :]
            right = wbuf[base + 2 * LANES : base + 4 * LANES, :]
            both = jnp.concatenate([left, right], axis=1)
            ordered = jnp.dot(mix, both, preferred_element_type=F32).astype(BF16)
            first = 2 * pair * group
            for slot in range(pack):
                target = (wp.at[c], ws[c])[slot % 2]
                tile = slice(slot // 2 * LANES, (slot // 2 + 1) * LANES)
                part = ordered[slot * group : (slot + 1) * group, :]
                target[first : first + group, tile] = part[:, :LANES]
                target[first + group : first + 2 * group, tile] = part[:, LANES:]
        span = pl.ds(pl.multiple_of(jnp.bitwise_xor(model, c) * depth, depth), depth)
        term = jnp.dot(normed[:, span], wp[c], preferred_element_type=F32)
        if c == 0:
            pacc[...] = term
        else:
            pacc[...] += term

        @pl.when(seg == 0)
        def _():
            other = jnp.dot(normed[:, span], ws[c][...], preferred_element_type=F32)
            if c == 0:
                sacc[...] = other
            else:
                sacc[...] += other

    prim[...] = pacc[...].astype(BF16)

    @pl.when(seg == 0)
    def _():
        sec[...] = sacc[...].astype(BF16)

    mine = pl.ds(pl.multiple_of(model * depth, depth), depth)
    own[...] = normed[:, mine]
    own_states[...] = xbuf[:, mine]
    own_gain[...] = gbuf[:, mine]


def part_kernel(c0, c1, c2, w0, w1, w2, acc):
    @pl.when(lax.axis_index("segment") == 1)
    def _():
        acc[...] = jnp.dot(c0[...], w0[...], preferred_element_type=F32)
        acc[...] += jnp.dot(c1[...], w1[...], preferred_element_type=F32)
        acc[...] += jnp.dot(c2[...], w2[...], preferred_element_type=F32)


def pack_kernel(sizes, counts, prim, sec, acc, c3, w3, *rest):
    heads = sizes[0] * sizes[1]
    second, outs = rest[0], rest[1:]
    seg, entry, _ = place(sizes)
    rows = prim.shape[0]

    @pl.when(seg == 0)
    def _():
        second[...] = sec[...]

    @pl.when(seg == 1)
    def _():
        total = acc[...] + jnp.dot(c3[...], w3[...], preferred_element_type=F32)
        line = lax.broadcasted_iota(jnp.int32, acc.shape, 0)
        second[...] = jnp.where(line < counts[0, 1], total, 0.0).astype(BF16)

    tail = jnp.full((TAIL, LANES), 1.0, F32) * counts[0, 0].astype(F32)
    for head in range(heads):
        cols = slice(head * DH, (head + 1) * DH)
        pair = jnp.concatenate([prim[:, cols], second[:, cols]], axis=1)
        for k, out in enumerate(outs):

            @pl.when(jnp.bitwise_xor(entry, k) == head)
            def _():
                out[:rows, :] = pair
                out[rows:, :] = tail.astype(BF16)


def live_keys(piece, rows):
    position = lax.broadcasted_iota(jnp.int32, (1, rows), 1).astype(F32)
    count = piece[rows : rows + 1, :].astype(F32)
    return position < jnp.concatenate([count] * (rows // LANES), axis=1)


def attend_kernel(sizes, *rest):
    heads = sizes[0] * sizes[1]
    blocks = sizes[1]
    ins, outs = rest[:heads], rest[heads : 2 * heads]
    parts, back, totals = rest[2 * heads :]
    _, entry, _ = place(sizes)
    rows = outs[0].shape[0]
    for k, piece in enumerate(ins):
        parts[jnp.bitwise_xor(entry, k)] = piece[...]
    low = lax.broadcasted_iota(jnp.int32, (rows, LANES), 1) < DH
    zero = jnp.zeros((rows, LANES), BF16)
    live = [live_keys(parts[j], rows) for j in range(blocks)]
    for i in range(blocks):
        both = parts[blocks + i, :rows, :]
        query = jnp.where(low, both * BF16(SCALE), zero)
        grad = jnp.where(low, zero, both)
        flip_query = query.astype(F32).T.astype(BF16)
        flip_grad = grad.astype(F32).T.astype(BF16)
        scores = []
        for j in range(i + 1):
            product = right_product(query, parts[j, :rows, :])
            scores.append(jnp.where(live[j], product, NEGATIVE))
        top = jnp.max(functools.reduce(jnp.maximum, scores), axis=1, keepdims=True)
        expo = [jnp.exp(s - top) for s in scores]
        total = jnp.sum(functools.reduce(jnp.add, expo), axis=1, keepdims=True)
        share = 1.0 / total
        probs = [e * share for e in expo]
        slopes = [right_product(grad, parts[j, :rows, :]) for j in range(i + 1)]
        delta = functools.reduce(jnp.add, [p * g for p, g in zip(probs, slopes)])
        delta = jnp.sum(delta, axis=1, keepdims=True)
        out = jnp.zeros((rows, LANES), F32)
        other = jnp.zeros((rows, LANES), F32)
        for j in range(i + 1):
            prob = probs[j].astype(BF16)
            slope = (probs[j] * (slopes[j] - delta)).astype(BF16)
            other += jnp.dot(slope, parts[j, :rows, :], preferred_element_type=F32)
            out += jnp.dot(prob, parts[j, :rows, :], preferred_element_type=F32)
            tall = jnp.dot(flip_query, slope, preferred_element_type=F32)
            tall += jnp.dot(flip_grad, prob, preferred_element_type=F32)
            if i == j:
                totals[j] = tall
            else:
                totals[j] += tall
        back[blocks + i] = jnp.where(low, other * SCALE, out).astype(BF16)
    for j in range(blocks):
        back[j] = totals[j].T.astype(BF16)
    for k, out in enumerate(outs):
        out[...] = back[jnp.bitwise_xor(entry, k)]


def split_rows(column):
    row = jnp.broadcast_to(column, (column.shape[0], LANES)).T[:TAIL, :]
    high = row.astype(BF16).astype(F32)
    line = lax.broadcasted_iota(jnp.int32, row.shape, 0)
    return jnp.where(line == 0, high, row - high).astype(BF16)


def regroup_kernel(sizes, counts, *rest):
    heads = sizes[0] * sizes[1]
    ins, (lp, ls, parts) = rest[:heads], rest[heads:]
    seg, entry, _ = place(sizes)
    rows = lp.shape[0]
    for k, piece in enumerate(ins):
        parts[jnp.bitwise_xor(entry, k)] = piece[...]
    line = lax.broadcasted_iota(jnp.int32, (rows, DH), 0)
    alive = line < jnp.where(seg == 0, rows, counts[0, 1])
    for head in range(heads):
        cols = slice(head * DH, (head + 1) * DH)
        lp[:, cols] = parts[head, :, :DH]
        ls[:, cols] = jnp.where(alive, parts[head, :, DH:].astype(F32), 0.0).astype(BF16)


def project_block(seg, wp, ws, lp, ls, out, slot):
    rows = lp.shape[0]

    @pl.when(seg == 0)
    def _():
        total = right_product(lp[...], wp) + right_product(ls[...], ws)
        out[slot, :rows, :] = total.astype(BF16)

    @pl.when(seg == 1)
    def _():
        out[slot, :rows, :] = right_product(lp[...], wp).astype(BF16)


def send_kernel(sizes, lp, ls, prim, second, spread, wp, w3, w1, sent):
    seg, _, _ = place(sizes)
    rows, feats = prim.shape[0], sent.shape[2]
    project_block(seg, wp[3], w3[...], lp, ls, sent, 0)
    project_block(seg, wp[1], w1[...], lp, ls, sent, 1)
    term = lp[...].astype(F32) * prim[...].astype(F32)
    also = ls[...].astype(F32) * second[...].astype(F32)
    term = term + jnp.where(seg == 0, also, 0.0)
    column = jnp.sum(term, axis=1, keepdims=True) * spread[:, :1]
    sent[0, rows:, :] = jnp.zeros((TAIL, feats), BF16)
    sent[1, rows:, :] = jnp.zeros((TAIL, feats), BF16)
    sent[0, rows:, :rows] = split_rows(column)


def keep_kernel(sizes, lp, ls, wp, w2, w0, kept):
    seg, _, _ = place(sizes)
    project_block(seg, wp[2], w2[...], lp, ls, kept, 0)
    project_block(seg, wp[0], w0[...], lp, ls, kept, 1)


def layer_kernel(a0, a1, a2, a3, w0, w1, w2, w3, own, out, obuf, sem):
    seg = lax.axis_index("segment")

    @pl.when(seg == 0)
    def _():
        obuf[...] = own[...]

    @pl.when(seg == 1)
    def _():
        total = right_product(a0[...], w0[...])
        for a, w in ((a1, w1), (a2, w2), (a3, w3)):
            total += right_product(a[...], w[...])
        obuf[...] = total.astype(BF16)

    leaving = pltpu.make_async_copy(obuf, out, sem)
    leaving.start()
    leaving.wait()


def fold_kernel(kept, got, sent, out):
    rows = kept.shape[1]
    out[:rows, :] = (kept[0].astype(F32) + got[0, :rows, :].astype(F32)).astype(BF16)
    mine = sent[0, rows:, :].astype(F32)
    theirs = got[0, rows:, :].astype(F32)
    total = mine[0:1] + mine[1:2] + theirs[0:1] + theirs[1:2]
    total = jnp.broadcast_to(total, mine.shape)
    high = total.astype(BF16).astype(F32)
    line = lax.broadcasted_iota(jnp.int32, mine.shape, 0)
    out[rows:, :] = jnp.where(line == 0, high, total - high).astype(BF16)


ANYWHERE = pl.BlockSpec(memory_space=pltpu.HBM)
INSIDE = pl.BlockSpec(memory_space=pltpu.VMEM)
SCALARS = pl.BlockSpec(memory_space=pltpu.SMEM)


def call(body, ins, specs, outs, scratch=(), limit=16, flops=0, out_specs=None):
    inside = out_specs is None
    ins = [
        pltpu.with_memory_space_constraint(x, pltpu.HBM) if spec is ANYWHERE else x
        for x, spec in zip(ins, specs)
    ]
    return pl.pallas_call(
        body,
        in_specs=list(specs),
        out_specs=[INSIDE] * len(outs) if inside else out_specs,
        out_shape=[(pltpu.VMEM if inside else jax.ShapeDtypeStruct)(s, d) for s, d in outs],
        scratch_shapes=list(scratch),
        compiler_params=pltpu.CompilerParams(vmem_limit_bytes=limit << 20),
        cost_estimate=pl.CostEstimate(flops=flops, transcendentals=0, bytes_accessed=1 << 20),
    )(*ins)


def scales_kernel(width, spread, inverse, shrink):
    root = spread[...]
    inverse[...] = 1.0 / root
    shrink[...] = 1.0 / (width * root * root * root)


def leave_kernel(kept, got, half, far, states, gain, inverse, shrink, grad):
    rows = states.shape[0]
    ends = half[rows:, :].astype(F32) + far[rows:, :].astype(F32)
    row = jnp.broadcast_to(ends[0:1, :rows] + ends[1:2, :rows], (LANES, rows))
    term = row.T[:, :1]
    scaled = term * shrink[:, :1]
    total = kept[1].astype(F32) + got[1, :rows, :].astype(F32) + far[:rows, :].astype(F32)
    grad[...] = (gain[...] * total * inverse[:, :1] - states[...].astype(F32) * scaled).astype(BF16)


def per_device_heads(sizes, segment_in, norm_gains, projections, live_counts, cotangent):
    n_seg, n_blk, n_mp = sizes
    heads = n_seg * n_blk
    states = segment_in[0]
    rows, width = states.shape
    feats = cotangent.shape[1]
    group = projections.shape[3]
    counts = live_counts.T

    def swap(x, over_heads, over_mp, senders=range(n_seg)):
        pairs = [
            (e * n_mp + m, (e ^ over_heads) * n_mp + (m ^ over_mp))
            for e in range(heads)
            for m in range(n_mp)
            if e // n_blk in senders
        ]
        return lax.ppermute(x, AXES, pairs)

    summary = (1,)

    def exchange(pieces):
        moved = [pieces[0]]
        for k in range(1, heads):
            moved.append(swap(pieces[k], k, 0))
        return moved

    far_cot = swap(cotangent, 0, 2, summary)
    near_cot = swap(cotangent, 0, 1, summary)
    tiles = group // LANES
    mixed = projections.reshape(width, 2, tiles, LANES).transpose(0, 2, 1, 3)
    mixed = mixed.reshape(width * 2 * tiles, LANES)
    made = call(
        functools.partial(enter_kernel, sizes),
        (states, norm_gains, mixed),
        [ANYWHERE] * 3,
        [((n_mp, feats, group), BF16)]
        + [((feats, group), BF16)] * n_mp
        + [
            ((rows, feats), BF16),
            ((rows, feats), BF16),
            ((1, feats), F32),
            ((rows, LANES), F32),
            ((rows, group), BF16),
            ((rows, group), BF16),
        ],
        [
            pltpu.VMEM((rows, width), BF16),
            pltpu.VMEM((1, width), F32),
            pltpu.VMEM((width * 2 * tiles, LANES), BF16),
            pltpu.VMEM((rows, width), BF16),
            pltpu.VMEM((rows, group), F32),
            pltpu.VMEM((rows, group), F32),
            pltpu.SemaphoreType.DMA((n_mp,)),
            pltpu.SemaphoreType.DMA((2,)),
        ],
        24,
        8 << 30,
    )
    wp, ws = made[0], made[1 : 1 + n_mp]
    own, own_states, own_gain, spread, prim, sec = made[1 + n_mp :]
    lent_3 = swap(ws[3], 0, 3, summary)
    far_cot, spread = lax.optimization_barrier((far_cot, spread))
    cross_cot = swap(far_cot, 0, 1, summary)
    acc = call(
        part_kernel,
        (cotangent, near_cot, far_cot, *ws[:3]),
        [INSIDE] * 6,
        [((rows, group), F32)],
        (),
        16,
        1 << 30,
    )[0]
    made = call(
        functools.partial(pack_kernel, sizes),
        (counts, prim, sec, acc, cross_cot, ws[3]),
        [SCALARS] + [INSIDE] * 5,
        [((rows, group), BF16)] + [((rows + TAIL, LANES), BF16)] * heads,
        (),
        16,
        1 << 30,
    )
    second, pieces = made[0], made[1:]
    pieces = exchange(pieces)
    lent_2 = swap(ws[2], 0, 2, summary)
    inverse, shrink = call(
        functools.partial(scales_kernel, width), (spread,), [INSIDE], [((rows, LANES), F32)] * 2
    )
    pieces = call(
        functools.partial(attend_kernel, sizes),
        pieces,
        [INSIDE] * heads,
        [((rows, LANES), BF16)] * heads,
        [
            pltpu.VMEM((heads, rows + TAIL, LANES), BF16),
            pltpu.VMEM((heads, rows, LANES), BF16),
            pltpu.VMEM((n_blk, LANES, rows), F32),
        ],
        24,
        4 << 30,
    )
    pieces = exchange(pieces)
    lp, ls = call(
        functools.partial(regroup_kernel, sizes),
        (counts, *pieces),
        [SCALARS] + [INSIDE] * heads,
        [((rows, group), BF16)] * 2,
        [pltpu.VMEM((heads, rows, LANES), BF16)],
    )
    far_att = swap(ls, 0, 2, summary)
    (sent,) = call(
        functools.partial(send_kernel, sizes),
        (lp, ls, prim, second, spread, wp, ws[3], ws[1]),
        [INSIDE] * 8,
        [((2, rows + TAIL, feats), BF16)],
        (),
        16,
        2 << 30,
    )
    got = swap(sent, 0, 1)
    (kept,) = call(
        functools.partial(keep_kernel, sizes),
        (lp, ls, wp, ws[2], ws[0]),
        [INSIDE] * 5,
        [((2, rows, feats), BF16)],
        (),
        16,
        2 << 30,
    )
    (half,) = call(fold_kernel, (kept, got, sent), [INSIDE] * 3, [((rows + TAIL, feats), BF16)])
    far = swap(half, 0, 2)
    own_att, lent_1, half_seen = lax.optimization_barrier((ls, ws[1], half))
    lent_1 = swap(lent_1, 0, 1, summary)
    near_att = swap(own_att, 0, 1, summary)
    cross_att = swap(far_att, 0, 1, summary)
    (out,) = call(
        layer_kernel,
        (ls, near_att, far_att, cross_att, ws[0], lent_1, lent_2, lent_3, own),
        [INSIDE] * 9,
        [((rows, feats), BF16)],
        [pltpu.VMEM((rows, feats), BF16), pltpu.SemaphoreType.DMA],
        16,
        2 << 30,
        [ANYWHERE],
    )
    (grad,) = call(
        leave_kernel,
        (kept, got, half_seen, far, own_states, own_gain, inverse, shrink),
        [INSIDE] * 8,
        [((rows, feats), BF16)],
        out_specs=[INSIDE],
    )
    return (out[None], grad[None])


def solution(mesh):
    sizes = tuple(mesh.shape[axis] for axis in AXES)
    n_seg, n_blk, n_mp = sizes
    by_heads = n_seg == 2 and n_blk <= WIN and n_blk & (n_blk - 1) == 0 and n_mp == 4

    def body(segment_in, norm_gains, projections, live_counts, cotangent):
        rows, group = segment_in.shape[1], projections.shape[3]
        if by_heads:
            assert n_seg * n_blk * DH == group and group == 4 * LANES and rows % LANES == 0
            return per_device_heads(
                sizes, segment_in, norm_gains, projections, live_counts, cotangent
            )
        return per_device_windows(segment_in, norm_gains, projections, live_counts, cotangent)

    in_specs = (
        P("segment", "blk", None),
        P("segment", None),
        P("segment", None, None, "mp"),
        P(None, "blk"),
        P("blk", "mp"),
    )
    out_specs = (P("segment", "blk", "mp"), P("segment", "blk", "mp"))
    return jax.shard_map(body, mesh=mesh, in_specs=in_specs, out_specs=out_specs, check_vma=False)
```

```python
import functools

import jax
import jax.numpy as jnp
from jax import lax
from jax.experimental import pallas as pl
from jax.experimental.pallas import tpu as pltpu
from jax.sharding import PartitionSpec as P


DH = 64
WIN = 4


EPSILON = 1e-06
SCALE = 0.125
NEGATIVE = -1e30
LANES = 128
TAIL = 16
AXES = ("segment", "blk", "mp")

F32 = jnp.float32
BF16 = jnp.bfloat16


def from_behind(x, axis, by):
    size = lax.axis_size(axis)
    pairs = [(i, i + by) for i in range(size) if 0 <= i + by < size]
    return lax.ppermute(x, axis, pairs)


def normalize(states, gain_row):
    widened = states.astype(jnp.float32)
    spread = jnp.sqrt(jnp.mean(widened * widened, axis=-1, keepdims=True) + EPSILON)
    return ((widened / spread * gain_row).astype(jnp.bfloat16), spread)


def right_product(left, right):
    return lax.dot_general(
        left, right, (((1,), (1,)), ((), ())), preferred_element_type=jnp.float32
    )


def per_device_windows(segment_in, norm_gains, projections, live_counts, cotangent):
    segment_pos = lax.axis_index("segment")
    model_index = lax.axis_index("mp")
    states = segment_in[0]
    gain_row = norm_gains[0]
    row_count, full_width = states.shape
    feature_width = cotangent.shape[1]
    w_primary = projections[0, :, 0, :]
    w_secondary = projections[0, :, 1, :]
    group_width = w_primary.shape[1]
    group_heads = group_width // DH
    normed, spread = normalize(states, gain_row)
    primary = jnp.dot(normed, w_primary, preferred_element_type=jnp.float32).astype(jnp.bfloat16)
    secondary = lax.cond(
        segment_pos == 0,
        lambda: jnp.dot(normed, w_secondary, preferred_element_type=jnp.float32).astype(
            jnp.bfloat16
        ),
        lambda: jnp.zeros_like(primary),
    )
    doc_keys, doc_values = from_behind((primary, secondary), "segment", 1)
    own_block = (doc_keys, doc_values, live_counts[0])
    window = [own_block]
    moving = own_block
    for _ in range(1, WIN):
        moving = from_behind((moving[0], moving[1], moving[2]), "blk", 1)
        window.append(moving)
    position = jnp.arange(row_count, dtype=jnp.int32)
    all_keys = jnp.concatenate([piece[0] for piece in window], 0).reshape(
        WIN * row_count, group_heads, DH
    )
    all_values = jnp.concatenate([piece[1] for piece in window], 0).reshape(
        WIN * row_count, group_heads, DH
    )
    key_live = jnp.concatenate([position < piece[2][0] for piece in window], 0)
    query_live = position < live_counts[1][0]
    query_heads = primary.reshape(row_count, group_heads, DH)
    scores = (
        jnp.einsum("qhd,khd->hqk", query_heads, all_keys, preferred_element_type=jnp.float32)
        * SCALE
    )
    scores = jnp.where(key_live[None, None, :], scores, NEGATIVE)
    row_max = jnp.max(scores, axis=-1, keepdims=True)
    expo = jnp.exp(scores - row_max)
    row_total = jnp.sum(expo, axis=-1, keepdims=True)
    softmax_out = expo / row_total
    weights_low = softmax_out.astype(jnp.bfloat16)
    attended = jnp.einsum(
        "hqk,khd->qhd", weights_low, all_values, preferred_element_type=jnp.float32
    ).astype(jnp.bfloat16)
    attended = jnp.where(query_live[:, None, None], attended, jnp.zeros_like(attended)).reshape(
        row_count, group_width
    )
    projected = lax.cond(
        segment_pos == 1,
        lambda: right_product(attended, w_secondary),
        lambda: jnp.zeros((row_count, full_width), jnp.float32),
    )
    layer_out = lax.psum_scatter(
        projected.astype(jnp.bfloat16), "mp", scatter_dimension=1, tiled=True
    )
    own_normed = lax.dynamic_slice_in_dim(normed, model_index * feature_width, feature_width, 1)
    segment_out = jnp.where(segment_pos == 0, own_normed, layer_out)[None]
    grad_out = jnp.dot(
        lax.all_gather(cotangent, "mp", axis=1, tiled=True),
        w_secondary,
        preferred_element_type=jnp.float32,
    )
    grad_out = grad_out.astype(jnp.bfloat16)
    grad_out = jnp.where(query_live[:, None], grad_out, jnp.zeros_like(grad_out))
    grad_heads = grad_out.reshape(row_count, group_heads, DH)
    grad_probs = jnp.einsum(
        "qhd,khd->hqk", grad_heads, all_values, preferred_element_type=jnp.float32
    )
    row_delta = jnp.sum(softmax_out * grad_probs, axis=-1, keepdims=True)
    grad_scores = (softmax_out * (grad_probs - row_delta)).astype(jnp.bfloat16)
    grad_queries = (
        (
            SCALE
            * jnp.einsum("hqk,khd->qhd", grad_scores, all_keys, preferred_element_type=jnp.float32)
        )
        .astype(jnp.bfloat16)
        .reshape(row_count, group_width)
    )
    key_parts = (
        SCALE
        * jnp.einsum("hqk,qhd->khd", grad_scores, query_heads, preferred_element_type=jnp.float32)
    ).reshape(WIN, row_count, group_width)
    value_parts = jnp.einsum(
        "hqk,qhd->khd", weights_low, grad_heads, preferred_element_type=jnp.float32
    ).reshape(WIN, row_count, group_width)
    key_total = key_parts[WIN - 1]
    value_total = value_parts[WIN - 1]
    for offset in range(WIN - 2, -1, -1):
        arrived = (
            from_behind(key_total.astype(jnp.bfloat16), "blk", -1).astype(key_total.dtype),
            from_behind(value_total.astype(jnp.bfloat16), "blk", -1).astype(value_total.dtype),
        )
        key_total = arrived[0] + key_parts[offset]
        value_total = arrived[1] + value_parts[offset]
    grad_keys = key_total.astype(jnp.bfloat16)
    grad_values = value_total.astype(jnp.bfloat16)
    back_keys, back_values = from_behind((grad_keys, grad_values), "segment", -1)
    partial_grad = lax.cond(
        segment_pos == 0,
        lambda: right_product(back_keys, w_primary) + right_product(back_values, w_secondary),
        lambda: right_product(grad_queries, w_primary),
    )
    widened = states.astype(jnp.float32)
    summed = lax.psum_scatter(
        partial_grad.astype(jnp.bfloat16), "mp", scatter_dimension=1, tiled=True
    ).astype(jnp.float32)
    own_states = lax.dynamic_slice_in_dim(widened, model_index * feature_width, feature_width, 1)
    own_gain = lax.dynamic_slice_in_dim(gain_row, model_index * feature_width, feature_width, 0)
    row_term = lax.psum(jnp.sum(summed * own_gain * own_states, axis=-1, keepdims=True), "mp")
    input_grad = (
        own_gain * summed / spread - own_states * row_term / (full_width * spread**3)
    ).astype(jnp.bfloat16)
    return (segment_out, input_grad[None])


def place(sizes):
    seg = lax.axis_index("segment")
    return seg, seg * sizes[1] + lax.axis_index("blk"), lax.axis_index("mp")


def enter_kernel(sizes, states, gain, w, *rest):
    n_mp = sizes[2]
    wp, ws = rest[0], rest[1 : 1 + n_mp]
    own, own_states, own_gain, spread, prim, sec = rest[1 + n_mp : 7 + n_mp]
    xbuf, gbuf, wbuf, normed, sems, ready = rest[7 + n_mp :]
    seg, _, model = place(sizes)
    rows, width = xbuf.shape
    depth = width // n_mp
    tiles = wp.shape[2] // LANES
    pack = 2 * tiles
    group = 2 * LANES // pack
    lines = depth * pack
    first_copies = [
        pltpu.make_async_copy(states, xbuf, ready.at[0]),
        pltpu.make_async_copy(gain, gbuf, ready.at[1]),
    ]
    copies = []
    for c in range(n_mp):
        start = pl.multiple_of(jnp.bitwise_xor(model, c) * lines, lines)
        copies.append(
            pltpu.make_async_copy(
                w.at[pl.ds(start, lines), :], wbuf.at[pl.ds(c * lines, lines), :], sems.at[c]
            )
        )
    for copy in first_copies + copies:
        copy.start()
    here = lax.broadcasted_iota(jnp.int32, (2 * LANES, 2 * LANES), 0)
    there = lax.broadcasted_iota(jnp.int32, (2 * LANES, 2 * LANES), 1)
    source = pack * lax.rem(here, group) + lax.div(here, group)
    mix = jnp.where(there == source, 1.0, 0.0).astype(BF16)
    part_rows = 16

    def norm_rows(first):
        line = slice(first, first + part_rows)
        wide = xbuf[line, :].astype(F32)
        mean = jnp.sum(wide * wide, axis=1, keepdims=True) * (1.0 / width)
        root = jnp.sqrt(mean + EPSILON)
        normed[line, :] = (wide * (1.0 / root) * gbuf[...]).astype(BF16)
        spread[line, :] = jnp.broadcast_to(root, (part_rows, LANES))

    for copy in first_copies:
        copy.wait()
    pairs = depth // (2 * group)
    every = n_mp * pairs * part_rows // rows
    for c in range(n_mp):
        copies[c].wait()
        for pair in range(pairs):
            if (c * pairs + pair) % every == 0:
                norm_rows((c * pairs + pair) // every * part_rows)
            base = c * lines + pair * 4 * LANES
            left = wbuf[base : base + 2 * LANES, :]
            right = wbuf[base + 2 * LANES : base + 4 * LANES, :]
            both = jnp.concatenate([left, right], axis=1)
            ordered = jnp.dot(mix, both, preferred_element_type=F32).astype(BF16)
            first = 2 * pair * group
            for slot in range(pack):
                target = (wp.at[c], ws[c])[slot % 2]
                tile = slice(slot // 2 * LANES, (slot // 2 + 1) * LANES)
                part = ordered[slot * group : (slot + 1) * group, :]
                target[first : first + group, tile] = part[:, :LANES]
                target[first + group : first + 2 * group, tile] = part[:, LANES:]

    def product(weights):
        total = None
        for c in range(n_mp):
            span = pl.ds(pl.multiple_of(jnp.bitwise_xor(model, c) * depth, depth), depth)
            term = jnp.dot(normed[:, span], weights(c), preferred_element_type=F32)
            total = term if total is None else total + term
        return total.astype(BF16)

    prim[...] = product(lambda c: wp[c])

    @pl.when(seg == 0)
    def _():
        sec[...] = product(lambda c: ws[c][...])

    mine = pl.ds(pl.multiple_of(model * depth, depth), depth)
    own[...] = normed[:, mine]
    own_states[...] = xbuf[:, mine]
    own_gain[...] = gbuf[:, mine]


def part_kernel(c0, c1, c2, w0, w1, w2, acc):
    @pl.when(lax.axis_index("segment") == 1)
    def _():
        acc[...] = jnp.dot(c0[...], w0[...], preferred_element_type=F32)
        acc[...] += jnp.dot(c1[...], w1[...], preferred_element_type=F32)
        acc[...] += jnp.dot(c2[...], w2[...], preferred_element_type=F32)


def pack_kernel(sizes, counts, prim, sec, acc, c3, w3, *rest):
    heads = sizes[0] * sizes[1]
    second, outs = rest[0], rest[1:]
    seg, entry, _ = place(sizes)
    rows = prim.shape[0]

    @pl.when(seg == 0)
    def _():
        second[...] = sec[...]

    @pl.when(seg == 1)
    def _():
        total = acc[...] + jnp.dot(c3[...], w3[...], preferred_element_type=F32)
        line = lax.broadcasted_iota(jnp.int32, acc.shape, 0)
        second[...] = jnp.where(line < counts[0, 1], total, 0.0).astype(BF16)

    tail = jnp.full((TAIL, LANES), 1.0, F32) * counts[0, 0].astype(F32)
    for head in range(heads):
        cols = slice(head * DH, (head + 1) * DH)
        pair = jnp.concatenate([prim[:, cols], second[:, cols]], axis=1)
        for k, out in enumerate(outs):

            @pl.when(jnp.bitwise_xor(entry, k) == head)
            def _():
                out[:rows, :] = pair
                out[rows:, :] = tail.astype(BF16)


def live_keys(piece, rows):
    position = lax.broadcasted_iota(jnp.int32, (1, rows), 1).astype(F32)
    count = piece[rows : rows + 1, :].astype(F32)
    return position < jnp.concatenate([count] * (rows // LANES), axis=1)


def attend_kernel(sizes, *rest):
    heads = sizes[0] * sizes[1]
    blocks = sizes[1]
    ins, outs = rest[:heads], rest[heads : 2 * heads]
    parts, back, totals = rest[2 * heads :]
    _, entry, _ = place(sizes)
    rows = outs[0].shape[0]
    for k, piece in enumerate(ins):
        parts[jnp.bitwise_xor(entry, k)] = piece[...]
    low = lax.broadcasted_iota(jnp.int32, (rows, LANES), 1) < DH
    zero = jnp.zeros((rows, LANES), BF16)
    live = [live_keys(parts[j], rows) for j in range(blocks)]
    for i in range(blocks):
        both = parts[blocks + i, :rows, :]
        query = jnp.where(low, both * BF16(SCALE), zero)
        grad = jnp.where(low, zero, both)
        flip_query = query.astype(F32).T.astype(BF16)
        flip_grad = grad.astype(F32).T.astype(BF16)
        scores = []
        for j in range(i + 1):
            product = right_product(query, parts[j, :rows, :])
            scores.append(jnp.where(live[j], product, NEGATIVE))
        top = jnp.max(functools.reduce(jnp.maximum, scores), axis=1, keepdims=True)
        expo = [jnp.exp(s - top) for s in scores]
        total = jnp.sum(functools.reduce(jnp.add, expo), axis=1, keepdims=True)
        share = 1.0 / total
        probs = [e * share for e in expo]
        slopes = [right_product(grad, parts[j, :rows, :]) for j in range(i + 1)]
        delta = functools.reduce(jnp.add, [p * g for p, g in zip(probs, slopes)])
        delta = jnp.sum(delta, axis=1, keepdims=True)
        out = jnp.zeros((rows, LANES), F32)
        other = jnp.zeros((rows, LANES), F32)
        for j in range(i + 1):
            prob = probs[j].astype(BF16)
            slope = (probs[j] * (slopes[j] - delta)).astype(BF16)
            other += jnp.dot(slope, parts[j, :rows, :], preferred_element_type=F32)
            out += jnp.dot(prob, parts[j, :rows, :], preferred_element_type=F32)
            tall = jnp.dot(flip_query, slope, preferred_element_type=F32)
            tall += jnp.dot(flip_grad, prob, preferred_element_type=F32)
            if i == j:
                totals[j] = tall
            else:
                totals[j] += tall
        back[blocks + i] = jnp.where(low, other * SCALE, out).astype(BF16)
    for j in range(blocks):
        back[j] = totals[j].T.astype(BF16)
    for k, out in enumerate(outs):
        out[...] = back[jnp.bitwise_xor(entry, k)]


def split_rows(column):
    row = jnp.broadcast_to(column, (column.shape[0], LANES)).T[:TAIL, :]
    high = row.astype(BF16).astype(F32)
    line = lax.broadcasted_iota(jnp.int32, row.shape, 0)
    return jnp.where(line == 0, high, row - high).astype(BF16)


def regroup_kernel(sizes, counts, *rest):
    heads = sizes[0] * sizes[1]
    ins, (lp, ls, parts) = rest[:heads], rest[heads:]
    seg, entry, _ = place(sizes)
    rows = lp.shape[0]
    for k, piece in enumerate(ins):
        parts[jnp.bitwise_xor(entry, k)] = piece[...]
    low = lax.broadcasted_iota(jnp.int32, (rows, LANES), 0)
    alive = low < jnp.where(seg == 0, rows, counts[0, 1])
    for head in range(0, heads, 2):
        cols = slice(head * DH, (head + 2) * DH)
        one, two = parts[head], parts[head + 1]
        lp[:, cols] = jnp.concatenate([one[:, :DH], two[:, :DH]], axis=1)
        both = jnp.concatenate([one[:, DH:], two[:, DH:]], axis=1)
        ls[:, cols] = jnp.where(alive, both.astype(F32), 0.0).astype(BF16)


def project_block(seg, wp, ws, lp, ls, out, slot):
    rows = lp.shape[0]

    @pl.when(seg == 0)
    def _():
        total = right_product(lp[...], wp) + right_product(ls[...], ws)
        out[slot, :rows, :] = total.astype(BF16)

    @pl.when(seg == 1)
    def _():
        out[slot, :rows, :] = right_product(lp[...], wp).astype(BF16)


def send_kernel(sizes, lp, ls, prim, second, spread, wp, w3, w1, sent):
    seg, _, _ = place(sizes)
    rows, feats = prim.shape[0], sent.shape[2]
    project_block(seg, wp[3], w3[...], lp, ls, sent, 0)
    project_block(seg, wp[1], w1[...], lp, ls, sent, 1)
    term = lp[...].astype(F32) * prim[...].astype(F32)
    also = ls[...].astype(F32) * second[...].astype(F32)
    term = term + jnp.where(seg == 0, also, 0.0)
    column = jnp.sum(term, axis=1, keepdims=True) * spread[:, :1]
    sent[0, rows:, :] = jnp.zeros((TAIL, feats), BF16)
    sent[1, rows:, :] = jnp.zeros((TAIL, feats), BF16)
    sent[0, rows:, :rows] = split_rows(column)


def keep_kernel(sizes, lp, ls, wp, w2, w0, kept):
    seg, _, _ = place(sizes)
    project_block(seg, wp[2], w2[...], lp, ls, kept, 0)
    project_block(seg, wp[0], w0[...], lp, ls, kept, 1)


def layer_kernel(a0, a1, a2, a3, w0, w1, w2, w3, own, out, obuf, sem):
    seg = lax.axis_index("segment")

    @pl.when(seg == 0)
    def _():
        obuf[...] = own[...]

    @pl.when(seg == 1)
    def _():
        total = right_product(a0[...], w0[...])
        for a, w in ((a1, w1), (a2, w2), (a3, w3)):
            total += right_product(a[...], w[...])
        obuf[...] = total.astype(BF16)

    leaving = pltpu.make_async_copy(obuf, out, sem)
    leaving.start()
    leaving.wait()


def fold_kernel(kept, got, sent, out, ends):
    rows = kept.shape[1]
    out[...] = (kept[0].astype(F32) + got[0, :rows, :].astype(F32)).astype(BF16)
    mine = sent[0, rows:, :rows].astype(F32)
    theirs = got[0, rows:, :rows].astype(F32)
    total = mine[0:1] + mine[1:2] + theirs[0:1] + theirs[1:2]
    ends[...] = jnp.broadcast_to(total, ends.shape)


ANYWHERE = pl.BlockSpec(memory_space=pltpu.HBM)
INSIDE = pl.BlockSpec(memory_space=pltpu.VMEM)
SCALARS = pl.BlockSpec(memory_space=pltpu.SMEM)


def call(body, ins, specs, outs, scratch=(), limit=16, flops=0, out_specs=None):
    inside = out_specs is None
    ins = [
        pltpu.with_memory_space_constraint(x, pltpu.HBM) if spec is ANYWHERE else x
        for x, spec in zip(ins, specs)
    ]
    return pl.pallas_call(
        body,
        in_specs=list(specs),
        out_specs=[INSIDE] * len(outs) if inside else out_specs,
        out_shape=[(pltpu.VMEM if inside else jax.ShapeDtypeStruct)(s, d) for s, d in outs],
        scratch_shapes=list(scratch),
        compiler_params=pltpu.CompilerParams(vmem_limit_bytes=limit << 20),
        cost_estimate=pl.CostEstimate(flops=flops, transcendentals=0, bytes_accessed=1 << 20),
    )(*ins)


def scales_kernel(width, spread, inverse, shrink):
    root = spread[...]
    inverse[...] = 1.0 / root
    shrink[...] = 1.0 / (width * root * root * root)


def leave_kernel(kept, got, ends, far_ends, far, states, gain, inverse, shrink, grad):
    rows = states.shape[0]
    row = ends[...] + far_ends[...]
    term = jnp.broadcast_to(row[:1], (LANES, rows)).T[:, :1]
    scaled = term * shrink[:, :1]
    total = kept[1].astype(F32) + got[1, :rows, :].astype(F32) + far[...].astype(F32)
    grad[...] = (gain[...] * total * inverse[:, :1] - states[...].astype(F32) * scaled).astype(BF16)


def per_device_heads(sizes, segment_in, norm_gains, projections, live_counts, cotangent):
    n_seg, n_blk, n_mp = sizes
    heads = n_seg * n_blk
    states = segment_in[0]
    rows, width = states.shape
    feats = cotangent.shape[1]
    group = projections.shape[3]
    counts = live_counts.T

    def swap(x, over_heads, over_mp, senders=range(n_seg)):
        pairs = [
            (e * n_mp + m, (e ^ over_heads) * n_mp + (m ^ over_mp))
            for e in range(heads)
            for m in range(n_mp)
            if e // n_blk in senders
        ]
        return lax.ppermute(x, AXES, pairs)

    summary = (1,)

    def exchange(pieces):
        moved = [pieces[0]]
        for k in range(1, heads):
            moved.append(swap(pieces[k], k, 0))
        return moved

    far_cot = swap(cotangent, 0, 2, summary)
    near_cot = swap(cotangent, 0, 1, summary)
    tiles = group // LANES
    mixed = projections.reshape(width, 2, tiles, LANES).transpose(0, 2, 1, 3)
    mixed = mixed.reshape(width * 2 * tiles, LANES)
    made = call(
        functools.partial(enter_kernel, sizes),
        (states, norm_gains, mixed),
        [ANYWHERE] * 3,
        [((n_mp, feats, group), BF16)]
        + [((feats, group), BF16)] * n_mp
        + [
            ((rows, feats), BF16),
            ((rows, feats), BF16),
            ((1, feats), F32),
            ((rows, LANES), F32),
            ((rows, group), BF16),
            ((rows, group), BF16),
        ],
        [
            pltpu.VMEM((rows, width), BF16),
            pltpu.VMEM((1, width), F32),
            pltpu.VMEM((width * 2 * tiles, LANES), BF16),
            pltpu.VMEM((rows, width), BF16),
            pltpu.SemaphoreType.DMA((n_mp,)),
            pltpu.SemaphoreType.DMA((2,)),
        ],
        24,
        8 << 30,
    )
    wp, ws = made[0], made[1 : 1 + n_mp]
    own, own_states, own_gain, spread, prim, sec = made[1 + n_mp :]
    lent_3 = swap(ws[3], 0, 3, summary)
    far_cot, spread = lax.optimization_barrier((far_cot, spread))
    cross_cot = swap(far_cot, 0, 1, summary)
    acc = call(
        part_kernel,
        (cotangent, near_cot, far_cot, *ws[:3]),
        [INSIDE] * 6,
        [((rows, group), F32)],
        (),
        16,
        1 << 30,
    )[0]
    made = call(
        functools.partial(pack_kernel, sizes),
        (counts, prim, sec, acc, cross_cot, ws[3]),
        [SCALARS] + [INSIDE] * 5,
        [((rows, group), BF16)] + [((rows + TAIL, LANES), BF16)] * heads,
        (),
        16,
        1 << 30,
    )
    second, pieces = made[0], made[1:]
    pieces = exchange(pieces)
    lent_2 = swap(ws[2], 0, 2, summary)
    inverse, shrink = call(
        functools.partial(scales_kernel, width), (spread,), [INSIDE], [((rows, LANES), F32)] * 2
    )
    pieces = call(
        functools.partial(attend_kernel, sizes),
        pieces,
        [INSIDE] * heads,
        [((rows, LANES), BF16)] * heads,
        [
            pltpu.VMEM((heads, rows + TAIL, LANES), BF16),
            pltpu.VMEM((heads, rows, LANES), BF16),
            pltpu.VMEM((n_blk, LANES, rows), F32),
        ],
        24,
        4 << 30,
    )
    pieces = exchange(pieces)
    lp, ls = call(
        functools.partial(regroup_kernel, sizes),
        (counts, *pieces),
        [SCALARS] + [INSIDE] * heads,
        [((rows, group), BF16)] * 2,
        [pltpu.VMEM((heads, rows, LANES), BF16)],
    )
    far_att = swap(ls, 0, 2, summary)
    (sent,) = call(
        functools.partial(send_kernel, sizes),
        (lp, ls, prim, second, spread, wp, ws[3], ws[1]),
        [INSIDE] * 8,
        [((2, rows + TAIL, feats), BF16)],
        (),
        16,
        2 << 30,
    )
    got = swap(sent, 0, 1)
    (kept,) = call(
        functools.partial(keep_kernel, sizes),
        (lp, ls, wp, ws[2], ws[0]),
        [INSIDE] * 5,
        [((2, rows, feats), BF16)],
        (),
        16,
        2 << 30,
    )
    half, ends = call(
        fold_kernel, (kept, got, sent), [INSIDE] * 3, [((rows, feats), BF16), ((8, rows), F32)]
    )
    far = swap(half, 0, 2)
    far_ends = swap(ends, 0, 2)
    own_att, lent_1, ends = lax.optimization_barrier((ls, ws[1], ends))
    lent_1 = swap(lent_1, 0, 1, summary)
    near_att = swap(own_att, 0, 1, summary)
    cross_att = swap(far_att, 0, 1, summary)
    (out,) = call(
        layer_kernel,
        (ls, near_att, far_att, cross_att, ws[0], lent_1, lent_2, lent_3, own),
        [INSIDE] * 9,
        [((rows, feats), BF16)],
        [pltpu.VMEM((rows, feats), BF16), pltpu.SemaphoreType.DMA],
        16,
        2 << 30,
        [ANYWHERE],
    )
    (grad,) = call(
        leave_kernel,
        (kept, got, ends, far_ends, far, own_states, own_gain, inverse, shrink),
        [INSIDE] * 9,
        [((rows, feats), BF16)],
        out_specs=[INSIDE],
    )
    return (out[None], grad[None])


def solution(mesh):
    sizes = tuple(mesh.shape[axis] for axis in AXES)
    n_seg, n_blk, n_mp = sizes
    by_heads = n_seg == 2 and n_blk <= WIN and n_blk & (n_blk - 1) == 0 and n_mp == 4

    def body(segment_in, norm_gains, projections, live_counts, cotangent):
        rows, group = segment_in.shape[1], projections.shape[3]
        if by_heads:
            assert n_seg * n_blk * DH == group and group == 4 * LANES and rows % LANES == 0
            return per_device_heads(
                sizes, segment_in, norm_gains, projections, live_counts, cotangent
            )
        return per_device_windows(segment_in, norm_gains, projections, live_counts, cotangent)

    in_specs = (
        P("segment", "blk", None),
        P("segment", None),
        P("segment", None, None, "mp"),
        P(None, "blk"),
        P("blk", "mp"),
    )
    out_specs = (P("segment", "blk", "mp"), P("segment", "blk", "mp"))
    return jax.shard_map(body, mesh=mesh, in_specs=in_specs, out_specs=out_specs, check_vma=False)
```

```python
import functools

import jax
import jax.numpy as jnp
from jax import lax
from jax.experimental import pallas as pl
from jax.experimental.pallas import tpu as pltpu
from jax.sharding import PartitionSpec as P


DH = 64
WIN = 4


EPSILON = 1e-06
SCALE = 0.125
NEGATIVE = -1e30
LANES = 128
TAIL = 16
AXES = ("segment", "blk", "mp")

F32 = jnp.float32
BF16 = jnp.bfloat16


def from_behind(x, axis, by):
    size = lax.axis_size(axis)
    pairs = [(i, i + by) for i in range(size) if 0 <= i + by < size]
    return lax.ppermute(x, axis, pairs)


def normalize(states, gain_row):
    widened = states.astype(jnp.float32)
    spread = jnp.sqrt(jnp.mean(widened * widened, axis=-1, keepdims=True) + EPSILON)
    return ((widened / spread * gain_row).astype(jnp.bfloat16), spread)


def right_product(left, right):
    return lax.dot_general(
        left, right, (((1,), (1,)), ((), ())), preferred_element_type=jnp.float32
    )


def per_device_windows(segment_in, norm_gains, projections, live_counts, cotangent):
    segment_pos = lax.axis_index("segment")
    model_index = lax.axis_index("mp")
    states = segment_in[0]
    gain_row = norm_gains[0]
    row_count, full_width = states.shape
    feature_width = cotangent.shape[1]
    w_primary = projections[0, :, 0, :]
    w_secondary = projections[0, :, 1, :]
    group_width = w_primary.shape[1]
    group_heads = group_width // DH
    normed, spread = normalize(states, gain_row)
    primary = jnp.dot(normed, w_primary, preferred_element_type=jnp.float32).astype(jnp.bfloat16)
    secondary = lax.cond(
        segment_pos == 0,
        lambda: jnp.dot(normed, w_secondary, preferred_element_type=jnp.float32).astype(
            jnp.bfloat16
        ),
        lambda: jnp.zeros_like(primary),
    )
    doc_keys, doc_values = from_behind((primary, secondary), "segment", 1)
    own_block = (doc_keys, doc_values, live_counts[0])
    window = [own_block]
    moving = own_block
    for _ in range(1, WIN):
        moving = from_behind((moving[0], moving[1], moving[2]), "blk", 1)
        window.append(moving)
    position = jnp.arange(row_count, dtype=jnp.int32)
    all_keys = jnp.concatenate([piece[0] for piece in window], 0).reshape(
        WIN * row_count, group_heads, DH
    )
    all_values = jnp.concatenate([piece[1] for piece in window], 0).reshape(
        WIN * row_count, group_heads, DH
    )
    key_live = jnp.concatenate([position < piece[2][0] for piece in window], 0)
    query_live = position < live_counts[1][0]
    query_heads = primary.reshape(row_count, group_heads, DH)
    scores = (
        jnp.einsum("qhd,khd->hqk", query_heads, all_keys, preferred_element_type=jnp.float32)
        * SCALE
    )
    scores = jnp.where(key_live[None, None, :], scores, NEGATIVE)
    row_max = jnp.max(scores, axis=-1, keepdims=True)
    expo = jnp.exp(scores - row_max)
    row_total = jnp.sum(expo, axis=-1, keepdims=True)
    softmax_out = expo / row_total
    weights_low = softmax_out.astype(jnp.bfloat16)
    attended = jnp.einsum(
        "hqk,khd->qhd", weights_low, all_values, preferred_element_type=jnp.float32
    ).astype(jnp.bfloat16)
    attended = jnp.where(query_live[:, None, None], attended, jnp.zeros_like(attended)).reshape(
        row_count, group_width
    )
    projected = lax.cond(
        segment_pos == 1,
        lambda: right_product(attended, w_secondary),
        lambda: jnp.zeros((row_count, full_width), jnp.float32),
    )
    layer_out = lax.psum_scatter(
        projected.astype(jnp.bfloat16), "mp", scatter_dimension=1, tiled=True
    )
    own_normed = lax.dynamic_slice_in_dim(normed, model_index * feature_width, feature_width, 1)
    segment_out = jnp.where(segment_pos == 0, own_normed, layer_out)[None]
    grad_out = jnp.dot(
        lax.all_gather(cotangent, "mp", axis=1, tiled=True),
        w_secondary,
        preferred_element_type=jnp.float32,
    )
    grad_out = grad_out.astype(jnp.bfloat16)
    grad_out = jnp.where(query_live[:, None], grad_out, jnp.zeros_like(grad_out))
    grad_heads = grad_out.reshape(row_count, group_heads, DH)
    grad_probs = jnp.einsum(
        "qhd,khd->hqk", grad_heads, all_values, preferred_element_type=jnp.float32
    )
    row_delta = jnp.sum(softmax_out * grad_probs, axis=-1, keepdims=True)
    grad_scores = (softmax_out * (grad_probs - row_delta)).astype(jnp.bfloat16)
    grad_queries = (
        (
            SCALE
            * jnp.einsum("hqk,khd->qhd", grad_scores, all_keys, preferred_element_type=jnp.float32)
        )
        .astype(jnp.bfloat16)
        .reshape(row_count, group_width)
    )
    key_parts = (
        SCALE
        * jnp.einsum("hqk,qhd->khd", grad_scores, query_heads, preferred_element_type=jnp.float32)
    ).reshape(WIN, row_count, group_width)
    value_parts = jnp.einsum(
        "hqk,qhd->khd", weights_low, grad_heads, preferred_element_type=jnp.float32
    ).reshape(WIN, row_count, group_width)
    key_total = key_parts[WIN - 1]
    value_total = value_parts[WIN - 1]
    for offset in range(WIN - 2, -1, -1):
        arrived = (
            from_behind(key_total.astype(jnp.bfloat16), "blk", -1).astype(key_total.dtype),
            from_behind(value_total.astype(jnp.bfloat16), "blk", -1).astype(value_total.dtype),
        )
        key_total = arrived[0] + key_parts[offset]
        value_total = arrived[1] + value_parts[offset]
    grad_keys = key_total.astype(jnp.bfloat16)
    grad_values = value_total.astype(jnp.bfloat16)
    back_keys, back_values = from_behind((grad_keys, grad_values), "segment", -1)
    partial_grad = lax.cond(
        segment_pos == 0,
        lambda: right_product(back_keys, w_primary) + right_product(back_values, w_secondary),
        lambda: right_product(grad_queries, w_primary),
    )
    widened = states.astype(jnp.float32)
    summed = lax.psum_scatter(
        partial_grad.astype(jnp.bfloat16), "mp", scatter_dimension=1, tiled=True
    ).astype(jnp.float32)
    own_states = lax.dynamic_slice_in_dim(widened, model_index * feature_width, feature_width, 1)
    own_gain = lax.dynamic_slice_in_dim(gain_row, model_index * feature_width, feature_width, 0)
    row_term = lax.psum(jnp.sum(summed * own_gain * own_states, axis=-1, keepdims=True), "mp")
    input_grad = (
        own_gain * summed / spread - own_states * row_term / (full_width * spread**3)
    ).astype(jnp.bfloat16)
    return (segment_out, input_grad[None])


def place(sizes):
    seg = lax.axis_index("segment")
    return seg, seg * sizes[1] + lax.axis_index("blk"), lax.axis_index("mp")


def enter_kernel(sizes, states, gain, w, *rest):
    n_mp = sizes[2]
    wp, ws = rest[0], rest[1 : 1 + n_mp]
    own, own_states, own_gain, spread, prim, sec = rest[1 + n_mp : 7 + n_mp]
    xbuf, gbuf, wbuf, normed, sems, ready = rest[7 + n_mp :]
    seg, _, model = place(sizes)
    rows, width = xbuf.shape
    depth = width // n_mp
    tiles = wp.shape[2] // LANES
    pack = 2 * tiles
    group = 2 * LANES // pack
    lines = depth * pack
    first_copies = [
        pltpu.make_async_copy(states, xbuf, ready.at[0]),
        pltpu.make_async_copy(gain, gbuf, ready.at[1]),
    ]
    copies = []
    for c in range(n_mp):
        start = pl.multiple_of(jnp.bitwise_xor(model, c) * lines, lines)
        copies.append(
            pltpu.make_async_copy(
                w.at[pl.ds(start, lines), :], wbuf.at[pl.ds(c * lines, lines), :], sems.at[c]
            )
        )
    for copy in first_copies + copies:
        copy.start()
    here = lax.broadcasted_iota(jnp.int32, (2 * LANES, 2 * LANES), 0)
    there = lax.broadcasted_iota(jnp.int32, (2 * LANES, 2 * LANES), 1)
    source = pack * lax.rem(here, group) + lax.div(here, group)
    mix = jnp.where(there == source, 1.0, 0.0).astype(BF16)
    part_rows = 16

    def norm_rows(first):
        line = slice(first, first + part_rows)
        wide = xbuf[line, :].astype(F32)
        mean = jnp.sum(wide * wide, axis=1, keepdims=True) * (1.0 / width)
        root = jnp.sqrt(mean + EPSILON)
        normed[line, :] = (wide * (1.0 / root) * gbuf[...]).astype(BF16)
        spread[line, :] = jnp.broadcast_to(root, (part_rows, LANES))

    for copy in first_copies:
        copy.wait()
    pairs = depth // (2 * group)
    every = n_mp * pairs * part_rows // rows
    for c in range(n_mp):
        copies[c].wait()
        for pair in range(pairs):
            if (c * pairs + pair) % every == 0:
                norm_rows((c * pairs + pair) // every * part_rows)
            base = c * lines + pair * 4 * LANES
            left = wbuf[base : base + 2 * LANES, :]
            right = wbuf[base + 2 * LANES : base + 4 * LANES, :]
            both = jnp.concatenate([left, right], axis=1)
            ordered = jnp.dot(mix, both, preferred_element_type=F32).astype(BF16)
            first = 2 * pair * group
            for slot in range(pack):
                target = (wp.at[c], ws[c])[slot % 2]
                tile = slice(slot // 2 * LANES, (slot // 2 + 1) * LANES)
                part = ordered[slot * group : (slot + 1) * group, :]
                target[first : first + group, tile] = part[:, :LANES]
                target[first + group : first + 2 * group, tile] = part[:, LANES:]

    def product(weights):
        total = None
        for c in range(n_mp):
            span = pl.ds(pl.multiple_of(jnp.bitwise_xor(model, c) * depth, depth), depth)
            term = jnp.dot(normed[:, span], weights(c), preferred_element_type=F32)
            total = term if total is None else total + term
        return total.astype(BF16)

    prim[...] = product(lambda c: wp[c])

    @pl.when(seg == 0)
    def _():
        sec[...] = product(lambda c: ws[c][...])

    mine = pl.ds(pl.multiple_of(model * depth, depth), depth)
    own[...] = normed[:, mine]
    own_states[...] = xbuf[:, mine]
    own_gain[...] = gbuf[:, mine]


def part_kernel(c0, c1, c2, w0, w1, w2, acc):
    @pl.when(lax.axis_index("segment") == 1)
    def _():
        acc[...] = jnp.dot(c0[...], w0[...], preferred_element_type=F32)
        acc[...] += jnp.dot(c1[...], w1[...], preferred_element_type=F32)
        acc[...] += jnp.dot(c2[...], w2[...], preferred_element_type=F32)


def pack_kernel(sizes, counts, prim, sec, acc, c3, w3, *rest):
    heads = sizes[0] * sizes[1]
    second, outs = rest[0], rest[1:]
    seg, entry, _ = place(sizes)
    rows = prim.shape[0]

    @pl.when(seg == 0)
    def _():
        second[...] = sec[...]

    @pl.when(seg == 1)
    def _():
        total = acc[...] + jnp.dot(c3[...], w3[...], preferred_element_type=F32)
        line = lax.broadcasted_iota(jnp.int32, acc.shape, 0)
        second[...] = jnp.where(line < counts[0, 1], total, 0.0).astype(BF16)

    tail = jnp.full((TAIL, LANES), 1.0, F32) * counts[0, 0].astype(F32)
    for head in range(heads):
        cols = slice(head * DH, (head + 1) * DH)
        pair = jnp.concatenate([prim[:, cols], second[:, cols]], axis=1)
        for k, out in enumerate(outs):

            @pl.when(jnp.bitwise_xor(entry, k) == head)
            def _():
                out[:rows, :] = pair
                out[rows:, :] = tail.astype(BF16)


def live_keys(piece, rows):
    position = lax.broadcasted_iota(jnp.int32, (1, rows), 1).astype(F32)
    count = piece[rows : rows + 1, :].astype(F32)
    return position < jnp.concatenate([count] * (rows // LANES), axis=1)


def attend_kernel(sizes, *rest):
    heads = sizes[0] * sizes[1]
    blocks = sizes[1]
    ins, outs = rest[:heads], rest[heads : 2 * heads]
    parts, back, totals = rest[2 * heads :]
    _, entry, _ = place(sizes)
    rows = outs[0].shape[0]
    for k, piece in enumerate(ins):
        parts[jnp.bitwise_xor(entry, k)] = piece[...]
    low = lax.broadcasted_iota(jnp.int32, (rows, LANES), 1) < DH
    zero = jnp.zeros((rows, LANES), BF16)
    live = [live_keys(parts[j], rows) for j in range(blocks)]
    for i in range(blocks):
        both = parts[blocks + i, :rows, :]
        query = jnp.where(low, both * BF16(SCALE), zero)
        grad = jnp.where(low, zero, both)
        flip_query = query.astype(F32).T.astype(BF16)
        flip_grad = grad.astype(F32).T.astype(BF16)
        scores = []
        for j in range(i + 1):
            product = right_product(query, parts[j, :rows, :])
            scores.append(jnp.where(live[j], product, NEGATIVE))
        top = jnp.max(functools.reduce(jnp.maximum, scores), axis=1, keepdims=True)
        expo = [jnp.exp(s - top) for s in scores]
        total = jnp.sum(functools.reduce(jnp.add, expo), axis=1, keepdims=True)
        share = 1.0 / total
        probs = [e * share for e in expo]
        slopes = [right_product(grad, parts[j, :rows, :]) for j in range(i + 1)]
        delta = functools.reduce(jnp.add, [p * g for p, g in zip(probs, slopes)])
        delta = jnp.sum(delta, axis=1, keepdims=True)
        out = jnp.zeros((rows, LANES), F32)
        other = jnp.zeros((rows, LANES), F32)
        for j in range(i + 1):
            prob = probs[j].astype(BF16)
            slope = (probs[j] * (slopes[j] - delta)).astype(BF16)
            other += jnp.dot(slope, parts[j, :rows, :], preferred_element_type=F32)
            out += jnp.dot(prob, parts[j, :rows, :], preferred_element_type=F32)
            tall = jnp.dot(flip_query, slope, preferred_element_type=F32)
            tall += jnp.dot(flip_grad, prob, preferred_element_type=F32)
            if i == j:
                totals[j] = tall
            else:
                totals[j] += tall
        back[blocks + i] = jnp.where(low, other * SCALE, out).astype(BF16)
    for j in range(blocks):
        back[j] = totals[j].T.astype(BF16)
    for k, out in enumerate(outs):
        out[...] = back[jnp.bitwise_xor(entry, k)]


def split_rows(column):
    row = jnp.broadcast_to(column, (column.shape[0], LANES)).T[:TAIL, :]
    high = row.astype(BF16).astype(F32)
    line = lax.broadcasted_iota(jnp.int32, row.shape, 0)
    return jnp.where(line == 0, high, row - high).astype(BF16)


def regroup_kernel(sizes, counts, *rest):
    heads = sizes[0] * sizes[1]
    ins, (lp, ls, parts) = rest[:heads], rest[heads:]
    seg, entry, _ = place(sizes)
    rows = lp.shape[0]
    for k, piece in enumerate(ins):
        parts[jnp.bitwise_xor(entry, k)] = piece[...]
    low = lax.broadcasted_iota(jnp.int32, (rows, LANES), 0)
    alive = low < jnp.where(seg == 0, rows, counts[0, 1])
    for head in range(0, heads, 2):
        cols = slice(head * DH, (head + 2) * DH)
        one, two = parts[head], parts[head + 1]
        lp[:, cols] = jnp.concatenate([one[:, :DH], two[:, :DH]], axis=1)
        both = jnp.concatenate([one[:, DH:], two[:, DH:]], axis=1)
        ls[:, cols] = jnp.where(alive, both.astype(F32), 0.0).astype(BF16)


def project_block(seg, wp, ws, lp, ls, out, slot):
    rows = lp.shape[0]

    @pl.when(seg == 0)
    def _():
        total = right_product(lp[...], wp) + right_product(ls[...], ws)
        out[slot, :rows, :] = total.astype(BF16)

    @pl.when(seg == 1)
    def _():
        out[slot, :rows, :] = right_product(lp[...], wp).astype(BF16)


def send_kernel(sizes, lp, ls, prim, second, spread, wp, w3, w1, sent):
    seg, _, _ = place(sizes)
    rows, feats = prim.shape[0], sent.shape[2]
    project_block(seg, wp[3], w3[...], lp, ls, sent, 0)
    project_block(seg, wp[1], w1[...], lp, ls, sent, 1)
    term = lp[...].astype(F32) * prim[...].astype(F32)
    also = ls[...].astype(F32) * second[...].astype(F32)
    term = term + jnp.where(seg == 0, also, 0.0)
    column = jnp.sum(term, axis=1, keepdims=True) * spread[:, :1]
    sent[0, rows:, :] = jnp.zeros((TAIL, feats), BF16)
    sent[1, rows:, :] = jnp.zeros((TAIL, feats), BF16)
    sent[0, rows:, :rows] = split_rows(column)


def keep_kernel(sizes, lp, ls, wp, w2, w0, kept):
    seg, _, _ = place(sizes)
    project_block(seg, wp[2], w2[...], lp, ls, kept, 0)
    project_block(seg, wp[0], w0[...], lp, ls, kept, 1)


def layer_kernel(a0, a1, a2, a3, w0, w1, w2, w3, own, out, obuf, sem):
    seg = lax.axis_index("segment")

    @pl.when(seg == 0)
    def _():
        obuf[...] = own[...]

    @pl.when(seg == 1)
    def _():
        total = right_product(a0[...], w0[...])
        for a, w in ((a1, w1), (a2, w2), (a3, w3)):
            total += right_product(a[...], w[...])
        obuf[...] = total.astype(BF16)

    leaving = pltpu.make_async_copy(obuf, out, sem)
    leaving.start()
    leaving.wait()


def fold_kernel(kept, got, sent, out, ends):
    rows = kept.shape[1]
    out[...] = (kept[0].astype(F32) + got[0, :rows, :].astype(F32)).astype(BF16)
    mine = sent[0, rows:, :rows].astype(F32)
    theirs = got[0, rows:, :rows].astype(F32)
    total = mine[0:1] + mine[1:2] + theirs[0:1] + theirs[1:2]
    ends[...] = jnp.broadcast_to(total, ends.shape)


ANYWHERE = pl.BlockSpec(memory_space=pltpu.HBM)
INSIDE = pl.BlockSpec(memory_space=pltpu.VMEM)
SCALARS = pl.BlockSpec(memory_space=pltpu.SMEM)


def call(body, ins, specs, outs, scratch=(), limit=16, flops=0, out_specs=None):
    inside = out_specs is None
    ins = [
        pltpu.with_memory_space_constraint(x, pltpu.HBM) if spec is ANYWHERE else x
        for x, spec in zip(ins, specs)
    ]
    return pl.pallas_call(
        body,
        in_specs=list(specs),
        out_specs=[INSIDE] * len(outs) if inside else out_specs,
        out_shape=[(pltpu.VMEM if inside else jax.ShapeDtypeStruct)(s, d) for s, d in outs],
        scratch_shapes=list(scratch),
        compiler_params=pltpu.CompilerParams(vmem_limit_bytes=limit << 20),
        cost_estimate=pl.CostEstimate(flops=flops, transcendentals=0, bytes_accessed=1 << 20),
    )(*ins)


def scales_kernel(width, spread, inverse, shrink):
    root = spread[...]
    inverse[...] = 1.0 / root
    shrink[...] = 1.0 / (width * root * root * root)


def leave_kernel(kept, got, ends, far_ends, far, states, gain, inverse, shrink, grad):
    rows = states.shape[0]
    row = ends[...] + far_ends[...]
    term = jnp.broadcast_to(row[:1], (LANES, rows)).T[:, :1]
    scaled = term * shrink[:, :1]
    total = kept[1].astype(F32) + got[1, :rows, :].astype(F32) + far[...].astype(F32)
    grad[...] = (gain[...] * total * inverse[:, :1] - states[...].astype(F32) * scaled).astype(BF16)


def per_device_heads(sizes, segment_in, norm_gains, projections, live_counts, cotangent):
    n_seg, n_blk, n_mp = sizes
    heads = n_seg * n_blk
    states = segment_in[0]
    rows, width = states.shape
    feats = cotangent.shape[1]
    group = projections.shape[3]
    counts = live_counts.T

    def swap(x, over_heads, over_mp):
        pairs = [
            (e * n_mp + m, (e ^ over_heads) * n_mp + (m ^ over_mp))
            for e in range(heads)
            for m in range(n_mp)
        ]
        return lax.ppermute(x, AXES, pairs)

    def exchange(pieces):
        moved = [pieces[0]]
        for k in range(1, heads):
            moved.append(swap(pieces[k], k, 0))
        return moved

    far_cot = swap(cotangent, 0, 2)
    near_cot = swap(cotangent, 0, 1)
    tiles = group // LANES
    mixed = projections.reshape(width, 2, tiles, LANES).transpose(0, 2, 1, 3)
    mixed = mixed.reshape(width * 2 * tiles, LANES)
    made = call(
        functools.partial(enter_kernel, sizes),
        (states, norm_gains, mixed),
        [ANYWHERE] * 3,
        [((n_mp, feats, group), BF16)]
        + [((feats, group), BF16)] * n_mp
        + [
            ((rows, feats), BF16),
            ((rows, feats), BF16),
            ((1, feats), F32),
            ((rows, LANES), F32),
            ((rows, group), BF16),
            ((rows, group), BF16),
        ],
        [
            pltpu.VMEM((rows, width), BF16),
            pltpu.VMEM((1, width), F32),
            pltpu.VMEM((width * 2 * tiles, LANES), BF16),
            pltpu.VMEM((rows, width), BF16),
            pltpu.SemaphoreType.DMA((n_mp,)),
            pltpu.SemaphoreType.DMA((2,)),
        ],
        24,
        8 << 30,
    )
    wp, ws = made[0], made[1 : 1 + n_mp]
    own, own_states, own_gain, spread, prim, sec = made[1 + n_mp :]
    lent_3 = swap(ws[3], 0, 3)
    far_cot, spread = lax.optimization_barrier((far_cot, spread))
    cross_cot = swap(far_cot, 0, 1)
    acc = call(
        part_kernel,
        (cotangent, near_cot, far_cot, *ws[:3]),
        [INSIDE] * 6,
        [((rows, group), F32)],
        (),
        16,
        1 << 30,
    )[0]
    made = call(
        functools.partial(pack_kernel, sizes),
        (counts, prim, sec, acc, cross_cot, ws[3]),
        [SCALARS] + [INSIDE] * 5,
        [((rows, group), BF16)] + [((rows + TAIL, LANES), BF16)] * heads,
        (),
        16,
        1 << 30,
    )
    second, pieces = made[0], made[1:]
    pieces = exchange(pieces)
    lent_2 = swap(ws[2], 0, 2)
    inverse, shrink = call(
        functools.partial(scales_kernel, width), (spread,), [INSIDE], [((rows, LANES), F32)] * 2
    )
    pieces = call(
        functools.partial(attend_kernel, sizes),
        pieces,
        [INSIDE] * heads,
        [((rows, LANES), BF16)] * heads,
        [
            pltpu.VMEM((heads, rows + TAIL, LANES), BF16),
            pltpu.VMEM((heads, rows, LANES), BF16),
            pltpu.VMEM((n_blk, LANES, rows), F32),
        ],
        24,
        4 << 30,
    )
    pieces = exchange(pieces)
    lp, ls = call(
        functools.partial(regroup_kernel, sizes),
        (counts, *pieces),
        [SCALARS] + [INSIDE] * heads,
        [((rows, group), BF16)] * 2,
        [pltpu.VMEM((heads, rows, LANES), BF16)],
    )
    far_att = swap(ls, 0, 2)
    (sent,) = call(
        functools.partial(send_kernel, sizes),
        (lp, ls, prim, second, spread, wp, ws[3], ws[1]),
        [INSIDE] * 8,
        [((2, rows + TAIL, feats), BF16)],
        (),
        16,
        2 << 30,
    )
    got = swap(sent, 0, 1)
    (kept,) = call(
        functools.partial(keep_kernel, sizes),
        (lp, ls, wp, ws[2], ws[0]),
        [INSIDE] * 5,
        [((2, rows, feats), BF16)],
        (),
        16,
        2 << 30,
    )
    half, ends = call(
        fold_kernel, (kept, got, sent), [INSIDE] * 3, [((rows, feats), BF16), ((8, rows), F32)]
    )
    far = swap(half, 0, 2)
    far_ends = swap(ends, 0, 2)
    own_att, lent_1, ends = lax.optimization_barrier((ls, ws[1], ends))
    lent_1 = swap(lent_1, 0, 1)
    near_att = swap(own_att, 0, 1)
    cross_att = swap(far_att, 0, 1)
    (out,) = call(
        layer_kernel,
        (ls, near_att, far_att, cross_att, ws[0], lent_1, lent_2, lent_3, own),
        [INSIDE] * 9,
        [((rows, feats), BF16)],
        [pltpu.VMEM((rows, feats), BF16), pltpu.SemaphoreType.DMA],
        16,
        2 << 30,
        [ANYWHERE],
    )
    (grad,) = call(
        leave_kernel,
        (kept, got, ends, far_ends, far, own_states, own_gain, inverse, shrink),
        [INSIDE] * 9,
        [((rows, feats), BF16)],
        out_specs=[INSIDE],
    )
    return (out[None], grad[None])


def solution(mesh):
    sizes = tuple(mesh.shape[axis] for axis in AXES)
    n_seg, n_blk, n_mp = sizes
    by_heads = n_seg == 2 and n_blk <= WIN and n_blk & (n_blk - 1) == 0 and n_mp == 4

    def body(segment_in, norm_gains, projections, live_counts, cotangent):
        rows, group = segment_in.shape[1], projections.shape[3]
        if by_heads:
            assert n_seg * n_blk * DH == group and group == 4 * LANES and rows % LANES == 0
            return per_device_heads(
                sizes, segment_in, norm_gains, projections, live_counts, cotangent
            )
        return per_device_windows(segment_in, norm_gains, projections, live_counts, cotangent)

    in_specs = (
        P("segment", "blk", None),
        P("segment", None),
        P("segment", None, None, "mp"),
        P(None, "blk"),
        P("blk", "mp"),
    )
    out_specs = (P("segment", "blk", "mp"), P("segment", "blk", "mp"))
    return jax.shard_map(body, mesh=mesh, in_specs=in_specs, out_specs=out_specs, check_vma=False)
```

```python
import functools

import jax
import jax.numpy as jnp
from jax import lax
from jax.experimental import pallas as pl
from jax.experimental.pallas import tpu as pltpu
from jax.sharding import PartitionSpec as P


DH = 64
WIN = 4


EPSILON = 1e-06
SCALE = 0.125
NEGATIVE = -1e30
LANES = 128
TAIL = 16
AXES = ("segment", "blk", "mp")

F32 = jnp.float32
BF16 = jnp.bfloat16


def from_behind(x, axis, by):
    size = lax.axis_size(axis)
    pairs = [(i, i + by) for i in range(size) if 0 <= i + by < size]
    return lax.ppermute(x, axis, pairs)


def normalize(states, gain_row):
    widened = states.astype(jnp.float32)
    spread = jnp.sqrt(jnp.mean(widened * widened, axis=-1, keepdims=True) + EPSILON)
    return ((widened / spread * gain_row).astype(jnp.bfloat16), spread)


def right_product(left, right):
    return lax.dot_general(
        left, right, (((1,), (1,)), ((), ())), preferred_element_type=jnp.float32
    )


def per_device_windows(segment_in, norm_gains, projections, live_counts, cotangent):
    segment_pos = lax.axis_index("segment")
    model_index = lax.axis_index("mp")
    states = segment_in[0]
    gain_row = norm_gains[0]
    row_count, full_width = states.shape
    feature_width = cotangent.shape[1]
    w_primary = projections[0, :, 0, :]
    w_secondary = projections[0, :, 1, :]
    group_width = w_primary.shape[1]
    group_heads = group_width // DH
    normed, spread = normalize(states, gain_row)
    primary = jnp.dot(normed, w_primary, preferred_element_type=jnp.float32).astype(jnp.bfloat16)
    secondary = lax.cond(
        segment_pos == 0,
        lambda: jnp.dot(normed, w_secondary, preferred_element_type=jnp.float32).astype(
            jnp.bfloat16
        ),
        lambda: jnp.zeros_like(primary),
    )
    doc_keys, doc_values = from_behind((primary, secondary), "segment", 1)
    own_block = (doc_keys, doc_values, live_counts[0])
    window = [own_block]
    moving = own_block
    for _ in range(1, WIN):
        moving = from_behind((moving[0], moving[1], moving[2]), "blk", 1)
        window.append(moving)
    position = jnp.arange(row_count, dtype=jnp.int32)
    all_keys = jnp.concatenate([piece[0] for piece in window], 0).reshape(
        WIN * row_count, group_heads, DH
    )
    all_values = jnp.concatenate([piece[1] for piece in window], 0).reshape(
        WIN * row_count, group_heads, DH
    )
    key_live = jnp.concatenate([position < piece[2][0] for piece in window], 0)
    query_live = position < live_counts[1][0]
    query_heads = primary.reshape(row_count, group_heads, DH)
    scores = (
        jnp.einsum("qhd,khd->hqk", query_heads, all_keys, preferred_element_type=jnp.float32)
        * SCALE
    )
    scores = jnp.where(key_live[None, None, :], scores, NEGATIVE)
    row_max = jnp.max(scores, axis=-1, keepdims=True)
    expo = jnp.exp(scores - row_max)
    row_total = jnp.sum(expo, axis=-1, keepdims=True)
    softmax_out = expo / row_total
    weights_low = softmax_out.astype(jnp.bfloat16)
    attended = jnp.einsum(
        "hqk,khd->qhd", weights_low, all_values, preferred_element_type=jnp.float32
    ).astype(jnp.bfloat16)
    attended = jnp.where(query_live[:, None, None], attended, jnp.zeros_like(attended)).reshape(
        row_count, group_width
    )
    projected = lax.cond(
        segment_pos == 1,
        lambda: right_product(attended, w_secondary),
        lambda: jnp.zeros((row_count, full_width), jnp.float32),
    )
    layer_out = lax.psum_scatter(
        projected.astype(jnp.bfloat16), "mp", scatter_dimension=1, tiled=True
    )
    own_normed = lax.dynamic_slice_in_dim(normed, model_index * feature_width, feature_width, 1)
    segment_out = jnp.where(segment_pos == 0, own_normed, layer_out)[None]
    grad_out = jnp.dot(
        lax.all_gather(cotangent, "mp", axis=1, tiled=True),
        w_secondary,
        preferred_element_type=jnp.float32,
    )
    grad_out = grad_out.astype(jnp.bfloat16)
    grad_out = jnp.where(query_live[:, None], grad_out, jnp.zeros_like(grad_out))
    grad_heads = grad_out.reshape(row_count, group_heads, DH)
    grad_probs = jnp.einsum(
        "qhd,khd->hqk", grad_heads, all_values, preferred_element_type=jnp.float32
    )
    row_delta = jnp.sum(softmax_out * grad_probs, axis=-1, keepdims=True)
    grad_scores = (softmax_out * (grad_probs - row_delta)).astype(jnp.bfloat16)
    grad_queries = (
        (
            SCALE
            * jnp.einsum("hqk,khd->qhd", grad_scores, all_keys, preferred_element_type=jnp.float32)
        )
        .astype(jnp.bfloat16)
        .reshape(row_count, group_width)
    )
    key_parts = (
        SCALE
        * jnp.einsum("hqk,qhd->khd", grad_scores, query_heads, preferred_element_type=jnp.float32)
    ).reshape(WIN, row_count, group_width)
    value_parts = jnp.einsum(
        "hqk,qhd->khd", weights_low, grad_heads, preferred_element_type=jnp.float32
    ).reshape(WIN, row_count, group_width)
    key_total = key_parts[WIN - 1]
    value_total = value_parts[WIN - 1]
    for offset in range(WIN - 2, -1, -1):
        arrived = (
            from_behind(key_total.astype(jnp.bfloat16), "blk", -1).astype(key_total.dtype),
            from_behind(value_total.astype(jnp.bfloat16), "blk", -1).astype(value_total.dtype),
        )
        key_total = arrived[0] + key_parts[offset]
        value_total = arrived[1] + value_parts[offset]
    grad_keys = key_total.astype(jnp.bfloat16)
    grad_values = value_total.astype(jnp.bfloat16)
    back_keys, back_values = from_behind((grad_keys, grad_values), "segment", -1)
    partial_grad = lax.cond(
        segment_pos == 0,
        lambda: right_product(back_keys, w_primary) + right_product(back_values, w_secondary),
        lambda: right_product(grad_queries, w_primary),
    )
    widened = states.astype(jnp.float32)
    summed = lax.psum_scatter(
        partial_grad.astype(jnp.bfloat16), "mp", scatter_dimension=1, tiled=True
    ).astype(jnp.float32)
    own_states = lax.dynamic_slice_in_dim(widened, model_index * feature_width, feature_width, 1)
    own_gain = lax.dynamic_slice_in_dim(gain_row, model_index * feature_width, feature_width, 0)
    row_term = lax.psum(jnp.sum(summed * own_gain * own_states, axis=-1, keepdims=True), "mp")
    input_grad = (
        own_gain * summed / spread - own_states * row_term / (full_width * spread**3)
    ).astype(jnp.bfloat16)
    return (segment_out, input_grad[None])


def place(sizes):
    seg = lax.axis_index("segment")
    return seg, seg * sizes[1] + lax.axis_index("blk"), lax.axis_index("mp")


def enter_kernel(sizes, states, gain, w, *rest):
    n_mp = sizes[2]
    wp, ws = rest[0], rest[1 : 1 + n_mp]
    own, own_states, own_gain, spread, prim, sec = rest[1 + n_mp : 7 + n_mp]
    xbuf, gbuf, wbuf, normed, sems, ready = rest[7 + n_mp :]
    seg, _, model = place(sizes)
    rows, width = xbuf.shape
    depth = width // n_mp
    tiles = wp.shape[2] // LANES
    pack = 2 * tiles
    group = 2 * LANES // pack
    lines = depth * pack
    first_copies = [
        pltpu.make_async_copy(states, xbuf, ready.at[0]),
        pltpu.make_async_copy(gain, gbuf, ready.at[1]),
    ]
    copies = []
    for c in range(n_mp):
        start = pl.multiple_of(jnp.bitwise_xor(model, c) * lines, lines)
        copies.append(
            pltpu.make_async_copy(
                w.at[pl.ds(start, lines), :], wbuf.at[pl.ds(c * lines, lines), :], sems.at[c]
            )
        )
    for copy in first_copies + copies:
        copy.start()
    here = lax.broadcasted_iota(jnp.int32, (2 * LANES, 2 * LANES), 0)
    there = lax.broadcasted_iota(jnp.int32, (2 * LANES, 2 * LANES), 1)
    source = pack * lax.rem(here, group) + lax.div(here, group)
    mix = jnp.where(there == source, 1.0, 0.0).astype(BF16)
    part_rows = 16

    def norm_rows(first):
        line = slice(first, first + part_rows)
        wide = xbuf[line, :].astype(F32)
        mean = jnp.sum(wide * wide, axis=1, keepdims=True) * (1.0 / width)
        root = jnp.sqrt(mean + EPSILON)
        normed[line, :] = (wide * (1.0 / root) * gbuf[...]).astype(BF16)
        spread[line, :] = jnp.broadcast_to(root, (part_rows, LANES))

    for copy in first_copies:
        copy.wait()
    pairs = depth // (2 * group)
    every = n_mp * pairs * part_rows // rows
    for c in range(n_mp):
        copies[c].wait()
        for pair in range(pairs):
            if (c * pairs + pair) % every == 0:
                norm_rows((c * pairs + pair) // every * part_rows)
            base = c * lines + pair * 4 * LANES
            left = wbuf[base : base + 2 * LANES, :]
            right = wbuf[base + 2 * LANES : base + 4 * LANES, :]
            both = jnp.concatenate([left, right], axis=1)
            ordered = jnp.dot(mix, both, preferred_element_type=F32).astype(BF16)
            first = 2 * pair * group
            for slot in range(pack):
                target = (wp.at[c], ws[c])[slot % 2]
                tile = slice(slot // 2 * LANES, (slot // 2 + 1) * LANES)
                part = ordered[slot * group : (slot + 1) * group, :]
                target[first : first + group, tile] = part[:, :LANES]
                target[first + group : first + 2 * group, tile] = part[:, LANES:]

    def product(weights):
        total = None
        for c in range(n_mp):
            span = pl.ds(pl.multiple_of(jnp.bitwise_xor(model, c) * depth, depth), depth)
            term = jnp.dot(normed[:, span], weights(c), preferred_element_type=F32)
            total = term if total is None else total + term
        return total.astype(BF16)

    prim[...] = product(lambda c: wp[c])

    @pl.when(seg == 0)
    def _():
        sec[...] = product(lambda c: ws[c][...])

    mine = pl.ds(pl.multiple_of(model * depth, depth), depth)
    own[...] = normed[:, mine]
    own_states[...] = xbuf[:, mine]
    own_gain[...] = gbuf[:, mine]


def lend_kernel(w2, middle, edge):
    parity = lax.rem(lax.axis_index("blk"), 2)
    depth, quarter = w2.shape[0], edge.shape[0]
    middle[...] = w2[quarter : depth - quarter, :]
    start = pl.multiple_of(parity * (depth - quarter), quarter)
    edge[...] = w2[pl.ds(start, quarter), :]


def part_kernel(c0, c1, c2, w0, w1, w2, acc):
    @pl.when(lax.axis_index("segment") == 1)
    def _():
        acc[...] = jnp.dot(c0[...], w0[...], preferred_element_type=F32)
        acc[...] += jnp.dot(c1[...], w1[...], preferred_element_type=F32)
        acc[...] += jnp.dot(c2[...], w2[...], preferred_element_type=F32)


def pack_kernel(sizes, counts, prim, sec, acc, c3, w3, *rest):
    heads = sizes[0] * sizes[1]
    second, outs, (parts,) = rest[0], rest[1 : 1 + heads], rest[1 + heads :]
    seg, entry, _ = place(sizes)
    rows = prim.shape[0]

    @pl.when(seg == 0)
    def _():
        second[...] = sec[...]

    @pl.when(seg == 1)
    def _():
        total = acc[...] + jnp.dot(c3[...], w3[...], preferred_element_type=F32)
        line = lax.broadcasted_iota(jnp.int32, acc.shape, 0)
        second[...] = jnp.where(line < counts[0, 1], total, 0.0).astype(BF16)

    tail = jnp.full((TAIL, LANES), 1.0, F32) * counts[0, 0].astype(F32)
    for head in range(heads):
        cols = slice(head * DH, (head + 1) * DH)
        parts[head] = jnp.concatenate([prim[:, cols], second[:, cols]], axis=1)
    for k, out in enumerate(outs):
        out[:rows, :] = parts[jnp.bitwise_xor(entry, k)]
        out[rows:, :] = tail.astype(BF16)


def live_keys(piece, rows):
    position = lax.broadcasted_iota(jnp.int32, (1, rows), 1).astype(F32)
    count = piece[rows : rows + 1, :].astype(F32)
    return position < jnp.concatenate([count] * (rows // LANES), axis=1)


def attend_kernel(sizes, *rest):
    heads = sizes[0] * sizes[1]
    blocks = sizes[1]
    ins, outs = rest[:heads], rest[heads : 2 * heads]
    parts, back, totals = rest[2 * heads :]
    _, entry, _ = place(sizes)
    rows = outs[0].shape[0]
    for k, piece in enumerate(ins):
        parts[jnp.bitwise_xor(entry, k)] = piece[...]
    low = lax.broadcasted_iota(jnp.int32, (rows, LANES), 1) < DH
    zero = jnp.zeros((rows, LANES), BF16)
    live = [live_keys(parts[j], rows) for j in range(blocks)]
    for i in range(blocks):
        both = parts[blocks + i, :rows, :]
        query = jnp.where(low, both * BF16(SCALE), zero)
        grad = jnp.where(low, zero, both)
        flip_query = query.astype(F32).T.astype(BF16)
        flip_grad = grad.astype(F32).T.astype(BF16)
        scores = []
        for j in range(i + 1):
            product = right_product(query, parts[j, :rows, :])
            scores.append(jnp.where(live[j], product, NEGATIVE))
        top = jnp.max(functools.reduce(jnp.maximum, scores), axis=1, keepdims=True)
        expo = [jnp.exp(s - top) for s in scores]
        total = jnp.sum(functools.reduce(jnp.add, expo), axis=1, keepdims=True)
        share = 1.0 / total
        probs = [e * share for e in expo]
        slopes = [right_product(grad, parts[j, :rows, :]) for j in range(i + 1)]
        delta = functools.reduce(jnp.add, [p * g for p, g in zip(probs, slopes)])
        delta = jnp.sum(delta, axis=1, keepdims=True)
        out = jnp.zeros((rows, LANES), F32)
        other = jnp.zeros((rows, LANES), F32)
        for j in range(i + 1):
            prob = probs[j].astype(BF16)
            slope = (probs[j] * (slopes[j] - delta)).astype(BF16)
            other += jnp.dot(slope, parts[j, :rows, :], preferred_element_type=F32)
            out += jnp.dot(prob, parts[j, :rows, :], preferred_element_type=F32)
            tall = jnp.dot(flip_query, slope, preferred_element_type=F32)
            tall += jnp.dot(flip_grad, prob, preferred_element_type=F32)
            if i == j:
                totals[j] = tall
            else:
                totals[j] += tall
        back[blocks + i] = jnp.where(low, other * SCALE, out).astype(BF16)
    for j in range(blocks):
        back[j] = totals[j].T.astype(BF16)
    for k, out in enumerate(outs):
        out[...] = back[jnp.bitwise_xor(entry, k)]


def split_rows(column):
    row = jnp.broadcast_to(column, (column.shape[0], LANES)).T[:TAIL, :]
    high = row.astype(BF16).astype(F32)
    line = lax.broadcasted_iota(jnp.int32, row.shape, 0)
    return jnp.where(line == 0, high, row - high).astype(BF16)


def regroup(sizes, ins, parts):
    heads = sizes[0] * sizes[1]
    _, entry, _ = place(sizes)
    for k, piece in enumerate(ins):
        parts[jnp.bitwise_xor(entry, k)] = piece[...]
    for head in range(0, heads, 2):
        yield slice(head * DH, (head + 2) * DH), parts[head], parts[head + 1]


def attended_kernel(sizes, counts, *rest):
    heads = sizes[0] * sizes[1]
    ins, (ls, parts) = rest[:heads], rest[heads:]
    rows = ls.shape[0]
    line = lax.broadcasted_iota(jnp.int32, (rows, LANES), 0)
    alive = line < jnp.where(lax.axis_index("segment") == 0, rows, counts[0, 1])
    for cols, one, two in regroup(sizes, ins, parts):
        both = jnp.concatenate([one[:, DH:], two[:, DH:]], axis=1)
        ls[:, cols] = jnp.where(alive, both.astype(F32), 0.0).astype(BF16)


def project_block(seg, wp, ws, lp, ls, out, slot):
    rows = lp.shape[0]

    @pl.when(seg == 0)
    def _():
        total = right_product(lp[...], wp) + right_product(ls[...], ws)
        out[slot, :rows, :] = total.astype(BF16)

    @pl.when(seg == 1)
    def _():
        out[slot, :rows, :] = right_product(lp[...], wp).astype(BF16)


def send_kernel(sizes, ls, prim, second, spread, wp, w3, w1, *rest):
    heads = sizes[0] * sizes[1]
    ins, (sent, lp, parts) = rest[:heads], rest[heads:]
    for cols, one, two in regroup(sizes, ins, parts):
        lp[:, cols] = jnp.concatenate([one[:, :DH], two[:, :DH]], axis=1)
    seg, _, _ = place(sizes)
    rows, feats = prim.shape[0], sent.shape[2]
    project_block(seg, wp[3], w3[...], lp, ls, sent, 0)
    project_block(seg, wp[1], w1[...], lp, ls, sent, 1)
    term = lp[...].astype(F32) * prim[...].astype(F32)
    also = ls[...].astype(F32) * second[...].astype(F32)
    term = term + jnp.where(seg == 0, also, 0.0)
    column = jnp.sum(term, axis=1, keepdims=True) * spread[:, :1]
    sent[0, rows:, :] = jnp.zeros((TAIL, feats), BF16)
    sent[1, rows:, :] = jnp.zeros((TAIL, feats), BF16)
    sent[0, rows:, :rows] = split_rows(column)


def keep_kernel(sizes, lp, ls, wp, w2, w0, kept):
    seg, _, _ = place(sizes)
    project_block(seg, wp[2], w2[...], lp, ls, kept, 0)
    project_block(seg, wp[0], w0[...], lp, ls, kept, 1)


def layer_kernel(a0, a1, a2, a3, w0, w1, middle, edge, mirrored, w3, own, out, obuf, w2, sem):
    seg = lax.axis_index("segment")

    @pl.when(seg == 0)
    def _():
        obuf[...] = own[...]

    @pl.when(seg == 1)
    def _():
        parity = lax.rem(lax.axis_index("blk"), 2)
        depth, quarter = w2.shape[0], edge.shape[0]
        for lent, side in ((edge, parity), (mirrored, 1 - parity)):
            start = pl.multiple_of(side * (depth - quarter), quarter)
            w2[pl.ds(start, quarter), :] = lent[...]
        w2[quarter : depth - quarter, :] = middle[...]
        total = right_product(a0[...], w0[...])
        for a, w in ((a1, w1), (a2, w2), (a3, w3)):
            total += right_product(a[...], w[...])
        obuf[...] = total.astype(BF16)

    leaving = pltpu.make_async_copy(obuf, out, sem)
    leaving.start()
    leaving.wait()


def fold_kernel(kept, got, sent, out, ends):
    rows = kept.shape[1]
    out[...] = (kept[0].astype(F32) + got[0, :rows, :].astype(F32)).astype(BF16)
    mine = sent[0, rows:, :rows].astype(F32)
    theirs = got[0, rows:, :rows].astype(F32)
    total = mine[0:1] + mine[1:2] + theirs[0:1] + theirs[1:2]
    ends[...] = jnp.broadcast_to(total, ends.shape)


ANYWHERE = pl.BlockSpec(memory_space=pltpu.HBM)
INSIDE = pl.BlockSpec(memory_space=pltpu.VMEM)
SCALARS = pl.BlockSpec(memory_space=pltpu.SMEM)


def call(body, ins, specs, outs, scratch=(), limit=16, flops=0, out_specs=None):
    inside = out_specs is None
    ins = [
        pltpu.with_memory_space_constraint(x, pltpu.HBM) if spec is ANYWHERE else x
        for x, spec in zip(ins, specs)
    ]
    return pl.pallas_call(
        body,
        in_specs=list(specs),
        out_specs=[INSIDE] * len(outs) if inside else out_specs,
        out_shape=[(pltpu.VMEM if inside else jax.ShapeDtypeStruct)(s, d) for s, d in outs],
        scratch_shapes=list(scratch),
        compiler_params=pltpu.CompilerParams(vmem_limit_bytes=limit << 20),
        cost_estimate=pl.CostEstimate(flops=flops, transcendentals=0, bytes_accessed=1 << 20),
    )(*ins)


def scales_kernel(width, spread, inverse, shrink):
    root = spread[...]
    inverse[...] = 1.0 / root
    shrink[...] = 1.0 / (width * root * root * root)


def leave_kernel(kept, got, ends, far_ends, far, states, gain, inverse, shrink, grad):
    rows = states.shape[0]
    row = ends[...] + far_ends[...]
    term = jnp.broadcast_to(row[:1], (LANES, rows)).T[:, :1]
    scaled = term * shrink[:, :1]
    total = kept[1].astype(F32) + got[1, :rows, :].astype(F32) + far[...].astype(F32)
    grad[...] = (gain[...] * total * inverse[:, :1] - states[...].astype(F32) * scaled).astype(BF16)


def per_device_heads(sizes, segment_in, norm_gains, projections, live_counts, cotangent):
    n_seg, n_blk, n_mp = sizes
    heads = n_seg * n_blk
    states = segment_in[0]
    rows, width = states.shape
    feats = cotangent.shape[1]
    group = projections.shape[3]
    counts = live_counts.T

    def swap(x, over_heads, over_mp):
        pairs = [
            (e * n_mp + m, (e ^ over_heads) * n_mp + (m ^ over_mp))
            for e in range(heads)
            for m in range(n_mp)
        ]
        return lax.ppermute(x, AXES, pairs)

    def exchange(pieces):
        moved = [pieces[0]]
        for k in range(1, heads):
            moved.append(swap(pieces[k], k, 0))
        return moved

    far_cot = swap(cotangent, 0, 2)
    near_cot = swap(cotangent, 0, 1)
    tiles = group // LANES
    mixed = projections.reshape(width, 2, tiles, LANES).transpose(0, 2, 1, 3)
    mixed = mixed.reshape(width * 2 * tiles, LANES)
    made = call(
        functools.partial(enter_kernel, sizes),
        (states, norm_gains, mixed),
        [ANYWHERE] * 3,
        [((n_mp, feats, group), BF16)]
        + [((feats, group), BF16)] * n_mp
        + [
            ((rows, feats), BF16),
            ((rows, feats), BF16),
            ((1, feats), F32),
            ((rows, LANES), F32),
            ((rows, group), BF16),
            ((rows, group), BF16),
        ],
        [
            pltpu.VMEM((rows, width), BF16),
            pltpu.VMEM((1, width), F32),
            pltpu.VMEM((width * 2 * tiles, LANES), BF16),
            pltpu.VMEM((rows, width), BF16),
            pltpu.SemaphoreType.DMA((n_mp,)),
            pltpu.SemaphoreType.DMA((2,)),
        ],
        24,
        8 << 30,
    )
    wp, ws = made[0], made[1 : 1 + n_mp]
    own, own_states, own_gain, spread, prim, sec = made[1 + n_mp :]
    quarter = feats // 4
    middle, edge = call(
        lend_kernel,
        (ws[2],),
        [INSIDE],
        [((feats - 2 * quarter, group), BF16), ((quarter, group), BF16)],
    )
    lent_3 = swap(ws[3], 0, 3)
    far_cot, spread = lax.optimization_barrier((far_cot, spread))
    cross_cot = swap(far_cot, 0, 1)
    acc = call(
        part_kernel,
        (cotangent, near_cot, far_cot, *ws[:3]),
        [INSIDE] * 6,
        [((rows, group), F32)],
        (),
        16,
        1 << 30,
    )[0]
    made = call(
        functools.partial(pack_kernel, sizes),
        (counts, prim, sec, acc, cross_cot, ws[3]),
        [SCALARS] + [INSIDE] * 5,
        [((rows, group), BF16)] + [((rows + TAIL, LANES), BF16)] * heads,
        [pltpu.VMEM((heads, rows, LANES), BF16)],
        16,
        1 << 30,
    )
    second, pieces = made[0], made[1:]
    pieces = exchange(pieces)
    lent_2 = swap(middle, 0, 2)
    lent_edge = swap(edge, 0, 2)
    inverse, shrink = call(
        functools.partial(scales_kernel, width), (spread,), [INSIDE], [((rows, LANES), F32)] * 2
    )
    pieces = call(
        functools.partial(attend_kernel, sizes),
        pieces,
        [INSIDE] * heads,
        [((rows, LANES), BF16)] * heads,
        [
            pltpu.VMEM((heads, rows + TAIL, LANES), BF16),
            pltpu.VMEM((heads, rows, LANES), BF16),
            pltpu.VMEM((n_blk, LANES, rows), F32),
        ],
        24,
        4 << 30,
    )
    pieces = exchange(pieces)
    (ls,) = call(
        functools.partial(attended_kernel, sizes),
        (counts, *pieces),
        [SCALARS] + [INSIDE] * heads,
        [((rows, group), BF16)],
        [pltpu.VMEM((heads, rows, LANES), BF16)],
    )
    far_att = swap(ls, 0, 2)
    sent, lp = call(
        functools.partial(send_kernel, sizes),
        (ls, prim, second, spread, wp, ws[3], ws[1], *pieces),
        [INSIDE] * (7 + heads),
        [((2, rows + TAIL, feats), BF16), ((rows, group), BF16)],
        [pltpu.VMEM((heads, rows, LANES), BF16)],
        16,
        2 << 30,
    )
    got = swap(sent, 0, 1)
    mirrored = swap(lent_edge, 1, 0)
    (kept,) = call(
        functools.partial(keep_kernel, sizes),
        (lp, ls, wp, ws[2], ws[0]),
        [INSIDE] * 5,
        [((2, rows, feats), BF16)],
        (),
        16,
        2 << 30,
    )
    half, ends = call(
        fold_kernel, (kept, got, sent), [INSIDE] * 3, [((rows, feats), BF16), ((8, rows), F32)]
    )
    far = swap(half, 0, 2)
    far_ends = swap(ends, 0, 2)
    own_att, lent_1, ends = lax.optimization_barrier((ls, ws[1], ends))
    lent_1 = swap(lent_1, 0, 1)
    near_att = swap(own_att, 0, 1)
    cross_att = swap(far_att, 0, 1)
    (out,) = call(
        layer_kernel,
        (
            *(ls, near_att, far_att, cross_att),
            *(ws[0], lent_1, lent_2, lent_edge, mirrored, lent_3, own),
        ),
        [INSIDE] * 11,
        [((rows, feats), BF16)],
        [
            pltpu.VMEM((rows, feats), BF16),
            pltpu.VMEM((feats, group), BF16),
            pltpu.SemaphoreType.DMA,
        ],
        16,
        2 << 30,
        [ANYWHERE],
    )
    (grad,) = call(
        leave_kernel,
        (kept, got, ends, far_ends, far, own_states, own_gain, inverse, shrink),
        [INSIDE] * 9,
        [((rows, feats), BF16)],
        out_specs=[INSIDE],
    )
    return (out[None], grad[None])


def solution(mesh):
    sizes = tuple(mesh.shape[axis] for axis in AXES)
    n_seg, n_blk, n_mp = sizes
    by_heads = n_seg == 2 and n_blk <= WIN and n_blk & (n_blk - 1) == 0 and n_blk > 1 and n_mp == 4

    def body(segment_in, norm_gains, projections, live_counts, cotangent):
        rows, group = segment_in.shape[1], projections.shape[3]
        if by_heads:
            assert n_seg * n_blk * DH == group and group == 4 * LANES and rows % LANES == 0
            return per_device_heads(
                sizes, segment_in, norm_gains, projections, live_counts, cotangent
            )
        return per_device_windows(segment_in, norm_gains, projections, live_counts, cotangent)

    in_specs = (
        P("segment", "blk", None),
        P("segment", None),
        P("segment", None, None, "mp"),
        P(None, "blk"),
        P("blk", "mp"),
    )
    out_specs = (P("segment", "blk", "mp"), P("segment", "blk", "mp"))
    return jax.shard_map(body, mesh=mesh, in_specs=in_specs, out_specs=out_specs, check_vma=False)
```

```python
import functools

import jax
import jax.numpy as jnp
from jax import lax
from jax.experimental import pallas as pl
from jax.experimental.pallas import tpu as pltpu
from jax.sharding import PartitionSpec as P


DH = 64
WIN = 4


EPSILON = 1e-06
SCALE = 0.125
NEGATIVE = -1e30
LANES = 128
TAIL = 16
AXES = ("segment", "blk", "mp")

F32 = jnp.float32
BF16 = jnp.bfloat16


def from_behind(x, axis, by):
    size = lax.axis_size(axis)
    pairs = [(i, i + by) for i in range(size) if 0 <= i + by < size]
    return lax.ppermute(x, axis, pairs)


def normalize(states, gain_row):
    widened = states.astype(jnp.float32)
    spread = jnp.sqrt(jnp.mean(widened * widened, axis=-1, keepdims=True) + EPSILON)
    return ((widened / spread * gain_row).astype(jnp.bfloat16), spread)


def right_product(left, right):
    return lax.dot_general(
        left, right, (((1,), (1,)), ((), ())), preferred_element_type=jnp.float32
    )


def per_device_windows(segment_in, norm_gains, projections, live_counts, cotangent):
    segment_pos = lax.axis_index("segment")
    model_index = lax.axis_index("mp")
    states = segment_in[0]
    gain_row = norm_gains[0]
    row_count, full_width = states.shape
    feature_width = cotangent.shape[1]
    w_primary = projections[0, :, 0, :]
    w_secondary = projections[0, :, 1, :]
    group_width = w_primary.shape[1]
    group_heads = group_width // DH
    normed, spread = normalize(states, gain_row)
    primary = jnp.dot(normed, w_primary, preferred_element_type=jnp.float32).astype(jnp.bfloat16)
    secondary = lax.cond(
        segment_pos == 0,
        lambda: jnp.dot(normed, w_secondary, preferred_element_type=jnp.float32).astype(
            jnp.bfloat16
        ),
        lambda: jnp.zeros_like(primary),
    )
    doc_keys, doc_values = from_behind((primary, secondary), "segment", 1)
    own_block = (doc_keys, doc_values, live_counts[0])
    window = [own_block]
    moving = own_block
    for _ in range(1, WIN):
        moving = from_behind((moving[0], moving[1], moving[2]), "blk", 1)
        window.append(moving)
    position = jnp.arange(row_count, dtype=jnp.int32)
    all_keys = jnp.concatenate([piece[0] for piece in window], 0).reshape(
        WIN * row_count, group_heads, DH
    )
    all_values = jnp.concatenate([piece[1] for piece in window], 0).reshape(
        WIN * row_count, group_heads, DH
    )
    key_live = jnp.concatenate([position < piece[2][0] for piece in window], 0)
    query_live = position < live_counts[1][0]
    query_heads = primary.reshape(row_count, group_heads, DH)
    scores = (
        jnp.einsum("qhd,khd->hqk", query_heads, all_keys, preferred_element_type=jnp.float32)
        * SCALE
    )
    scores = jnp.where(key_live[None, None, :], scores, NEGATIVE)
    row_max = jnp.max(scores, axis=-1, keepdims=True)
    expo = jnp.exp(scores - row_max)
    row_total = jnp.sum(expo, axis=-1, keepdims=True)
    softmax_out = expo / row_total
    weights_low = softmax_out.astype(jnp.bfloat16)
    attended = jnp.einsum(
        "hqk,khd->qhd", weights_low, all_values, preferred_element_type=jnp.float32
    ).astype(jnp.bfloat16)
    attended = jnp.where(query_live[:, None, None], attended, jnp.zeros_like(attended)).reshape(
        row_count, group_width
    )
    projected = lax.cond(
        segment_pos == 1,
        lambda: right_product(attended, w_secondary),
        lambda: jnp.zeros((row_count, full_width), jnp.float32),
    )
    layer_out = lax.psum_scatter(
        projected.astype(jnp.bfloat16), "mp", scatter_dimension=1, tiled=True
    )
    own_normed = lax.dynamic_slice_in_dim(normed, model_index * feature_width, feature_width, 1)
    segment_out = jnp.where(segment_pos == 0, own_normed, layer_out)[None]
    grad_out = jnp.dot(
        lax.all_gather(cotangent, "mp", axis=1, tiled=True),
        w_secondary,
        preferred_element_type=jnp.float32,
    )
    grad_out = grad_out.astype(jnp.bfloat16)
    grad_out = jnp.where(query_live[:, None], grad_out, jnp.zeros_like(grad_out))
    grad_heads = grad_out.reshape(row_count, group_heads, DH)
    grad_probs = jnp.einsum(
        "qhd,khd->hqk", grad_heads, all_values, preferred_element_type=jnp.float32
    )
    row_delta = jnp.sum(softmax_out * grad_probs, axis=-1, keepdims=True)
    grad_scores = (softmax_out * (grad_probs - row_delta)).astype(jnp.bfloat16)
    grad_queries = (
        (
            SCALE
            * jnp.einsum("hqk,khd->qhd", grad_scores, all_keys, preferred_element_type=jnp.float32)
        )
        .astype(jnp.bfloat16)
        .reshape(row_count, group_width)
    )
    key_parts = (
        SCALE
        * jnp.einsum("hqk,qhd->khd", grad_scores, query_heads, preferred_element_type=jnp.float32)
    ).reshape(WIN, row_count, group_width)
    value_parts = jnp.einsum(
        "hqk,qhd->khd", weights_low, grad_heads, preferred_element_type=jnp.float32
    ).reshape(WIN, row_count, group_width)
    key_total = key_parts[WIN - 1]
    value_total = value_parts[WIN - 1]
    for offset in range(WIN - 2, -1, -1):
        arrived = (
            from_behind(key_total.astype(jnp.bfloat16), "blk", -1).astype(key_total.dtype),
            from_behind(value_total.astype(jnp.bfloat16), "blk", -1).astype(value_total.dtype),
        )
        key_total = arrived[0] + key_parts[offset]
        value_total = arrived[1] + value_parts[offset]
    grad_keys = key_total.astype(jnp.bfloat16)
    grad_values = value_total.astype(jnp.bfloat16)
    back_keys, back_values = from_behind((grad_keys, grad_values), "segment", -1)
    partial_grad = lax.cond(
        segment_pos == 0,
        lambda: right_product(back_keys, w_primary) + right_product(back_values, w_secondary),
        lambda: right_product(grad_queries, w_primary),
    )
    widened = states.astype(jnp.float32)
    summed = lax.psum_scatter(
        partial_grad.astype(jnp.bfloat16), "mp", scatter_dimension=1, tiled=True
    ).astype(jnp.float32)
    own_states = lax.dynamic_slice_in_dim(widened, model_index * feature_width, feature_width, 1)
    own_gain = lax.dynamic_slice_in_dim(gain_row, model_index * feature_width, feature_width, 0)
    row_term = lax.psum(jnp.sum(summed * own_gain * own_states, axis=-1, keepdims=True), "mp")
    input_grad = (
        own_gain * summed / spread - own_states * row_term / (full_width * spread**3)
    ).astype(jnp.bfloat16)
    return (segment_out, input_grad[None])


def place(sizes):
    seg = lax.axis_index("segment")
    return seg, seg * sizes[1] + lax.axis_index("blk"), lax.axis_index("mp")


def enter_kernel(sizes, states, gain, w, counts, *rest):
    n_mp = sizes[2]
    wp, ws = rest[0], rest[1 : 1 + n_mp]
    own, own_states, own_gain, spread, prim, sec, alive, tail = rest[1 + n_mp : 9 + n_mp]
    xbuf, gbuf, wbuf, normed, sems, ready = rest[9 + n_mp :]
    seg, _, model = place(sizes)
    rows, width = xbuf.shape
    depth = width // n_mp
    tiles = wp.shape[2] // LANES
    pack = 2 * tiles
    group = 2 * LANES // pack
    lines = depth * pack
    first_copies = [
        pltpu.make_async_copy(states, xbuf, ready.at[0]),
        pltpu.make_async_copy(gain, gbuf, ready.at[1]),
    ]
    copies = []
    for c in range(n_mp):
        start = pl.multiple_of(jnp.bitwise_xor(model, c) * lines, lines)
        copies.append(
            pltpu.make_async_copy(
                w.at[pl.ds(start, lines), :], wbuf.at[pl.ds(c * lines, lines), :], sems.at[c]
            )
        )
    for copy in first_copies + copies:
        copy.start()
    here = lax.broadcasted_iota(jnp.int32, (2 * LANES, 2 * LANES), 0)
    there = lax.broadcasted_iota(jnp.int32, (2 * LANES, 2 * LANES), 1)
    source = pack * lax.rem(here, group) + lax.div(here, group)
    mix = jnp.where(there == source, 1.0, 0.0).astype(BF16)
    part_rows = 16

    def norm_rows(first):
        line = slice(first, first + part_rows)
        wide = xbuf[line, :].astype(F32)
        mean = jnp.sum(wide * wide, axis=1, keepdims=True) * (1.0 / width)
        root = jnp.sqrt(mean + EPSILON)
        normed[line, :] = (wide * (1.0 / root) * gbuf[...]).astype(BF16)
        spread[line, :] = jnp.broadcast_to(root, (part_rows, LANES))

    for copy in first_copies:
        copy.wait()
    pairs = depth // (2 * group)
    every = n_mp * pairs * part_rows // rows
    for c in range(n_mp):
        copies[c].wait()
        for pair in range(pairs):
            if (c * pairs + pair) % every == 0:
                norm_rows((c * pairs + pair) // every * part_rows)
            base = c * lines + pair * 4 * LANES
            left = wbuf[base : base + 2 * LANES, :]
            right = wbuf[base + 2 * LANES : base + 4 * LANES, :]
            both = jnp.concatenate([left, right], axis=1)
            ordered = jnp.dot(mix, both, preferred_element_type=F32).astype(BF16)
            first = 2 * pair * group
            for slot in range(pack):
                target = (wp.at[c], ws[c])[slot % 2]
                tile = slice(slot // 2 * LANES, (slot // 2 + 1) * LANES)
                part = ordered[slot * group : (slot + 1) * group, :]
                target[first : first + group, tile] = part[:, :LANES]
                target[first + group : first + 2 * group, tile] = part[:, LANES:]

    def product(weights):
        total = None
        for c in range(n_mp):
            span = pl.ds(pl.multiple_of(jnp.bitwise_xor(model, c) * depth, depth), depth)
            term = jnp.dot(normed[:, span], weights(c), preferred_element_type=F32)
            total = term if total is None else total + term
        return total.astype(BF16)

    prim[...] = product(lambda c: wp[c])

    @pl.when(seg == 0)
    def _():
        sec[...] = product(lambda c: ws[c][...])

    @pl.when(seg == 1)
    def _():
        sec[...] = jnp.zeros_like(sec)

    line = lax.broadcasted_iota(jnp.int32, alive.shape, 0)
    last = jnp.where(seg == 0, rows, counts[0, 1])
    alive[...] = jnp.where(line < last, 1.0, 0.0)
    tail[...] = (jnp.full(tail.shape, 1.0, F32) * counts[0, 0].astype(F32)).astype(BF16)

    mine = pl.ds(pl.multiple_of(model * depth, depth), depth)
    own[...] = normed[:, mine]
    own_states[...] = xbuf[:, mine]
    own_gain[...] = gbuf[:, mine]


def lend_kernel(w2, middle, edge):
    parity = lax.rem(lax.axis_index("blk"), 2)
    depth, quarter = w2.shape[0], edge.shape[0]
    middle[...] = w2[quarter : depth - quarter, :]
    start = pl.multiple_of(parity * (depth - quarter), quarter)
    edge[...] = w2[pl.ds(start, quarter), :]


def part_kernel(c0, c1, c2, w0, w1, w2, acc):
    @pl.when(lax.axis_index("segment") == 1)
    def _():
        acc[...] = jnp.dot(c0[...], w0[...], preferred_element_type=F32)
        acc[...] += jnp.dot(c1[...], w1[...], preferred_element_type=F32)
        acc[...] += jnp.dot(c2[...], w2[...], preferred_element_type=F32)


def prepare_kernel(sizes, prim, sec, tail, *rest):
    heads = sizes[0] * sizes[1]
    outs, (parts,) = rest[:heads], rest[heads:]
    _, entry, _ = place(sizes)
    rows = prim.shape[0]
    for head in range(heads):
        cols = slice(head * DH, (head + 1) * DH)
        parts[head] = jnp.concatenate([prim[:, cols], sec[:, cols]], axis=1)
    for k, out in enumerate(outs):
        out[:rows, :] = parts[jnp.bitwise_xor(entry, k)]
        out[rows:, :] = tail[...]


def pack_kernel(acc, alive, c3, w3, *halves):
    @pl.when(lax.axis_index("segment") == 1)
    def _():
        total = acc[...] + jnp.dot(c3[...], w3[...], preferred_element_type=F32)
        for tile in range(total.shape[1] // LANES):
            part = total[:, tile * LANES : (tile + 1) * LANES]
            part = jnp.where(alive[...] > 0.0, part, 0.0).astype(BF16)
            width = halves[0].shape[1]
            at = tile * LANES % width
            halves[tile * LANES // width][:, at : at + LANES] = part


def deal_kernel(sizes, here, turned, *rest):
    blocks = sizes[1]
    outs, (parts,) = rest[:blocks], rest[blocks:]
    half_rows = here.shape[0] // 2

    def split(source):
        for head in range(blocks):
            cols = slice(head * DH, (head + 1) * DH)
            parts[head] = jnp.concatenate([source[:half_rows, cols], source[half_rows:, cols]], axis=1)

    @pl.when(lax.axis_index("segment") == 0)
    def _():
        split(turned)

    @pl.when(lax.axis_index("segment") == 1)
    def _():
        split(here)

    for k, out in enumerate(outs):
        out[...] = parts[jnp.bitwise_xor(lax.axis_index("blk"), k)]


def live_keys(piece, rows):
    position = lax.broadcasted_iota(jnp.int32, (1, rows), 1).astype(F32)
    count = piece[rows : rows + 1, :].astype(F32)
    return position < jnp.concatenate([count] * (rows // LANES), axis=1)


def attend_kernel(sizes, *rest):
    heads = sizes[0] * sizes[1]
    blocks = sizes[1]
    ins, grads = rest[:heads], rest[heads : heads + blocks]
    outs, (parts, slots, back, totals) = rest[heads + blocks : -4], rest[-4:]
    _, entry, _ = place(sizes)
    rows = outs[0].shape[0]
    for k, piece in enumerate(ins):
        parts[jnp.bitwise_xor(entry, k)] = piece[...]
    for k, piece in enumerate(grads):
        slots[jnp.bitwise_xor(lax.axis_index("blk"), k)] = piece[...]
    low = lax.broadcasted_iota(jnp.int32, (rows, LANES), 1) < DH
    zero = jnp.zeros((rows, LANES), BF16)
    live = [live_keys(parts[j], rows) for j in range(blocks)]
    for i in range(blocks):
        both = parts[blocks + i, :rows, :]
        query = jnp.where(low, both * BF16(SCALE), zero)
        half = slots[i]
        turned = jnp.concatenate([half[:, DH:], half[:, :DH]], axis=1)
        grad = jnp.where(low, zero, jnp.concatenate([turned, half], axis=0))
        flip_query = query.astype(F32).T.astype(BF16)
        flip_grad = grad.astype(F32).T.astype(BF16)
        scores = []
        for j in range(i + 1):
            product = right_product(query, parts[j, :rows, :])
            scores.append(jnp.where(live[j], product, NEGATIVE))
        top = jnp.max(functools.reduce(jnp.maximum, scores), axis=1, keepdims=True)
        expo = [jnp.exp(s - top) for s in scores]
        total = jnp.sum(functools.reduce(jnp.add, expo), axis=1, keepdims=True)
        share = 1.0 / total
        probs = [e * share for e in expo]
        slopes = [right_product(grad, parts[j, :rows, :]) for j in range(i + 1)]
        delta = functools.reduce(jnp.add, [p * g for p, g in zip(probs, slopes)])
        delta = jnp.sum(delta, axis=1, keepdims=True)
        out = jnp.zeros((rows, LANES), F32)
        other = jnp.zeros((rows, LANES), F32)
        for j in range(i + 1):
            prob = probs[j].astype(BF16)
            slope = (probs[j] * (slopes[j] - delta)).astype(BF16)
            other += jnp.dot(slope, parts[j, :rows, :], preferred_element_type=F32)
            out += jnp.dot(prob, parts[j, :rows, :], preferred_element_type=F32)
            tall = jnp.dot(flip_query, slope, preferred_element_type=F32)
            tall += jnp.dot(flip_grad, prob, preferred_element_type=F32)
            if i == j:
                totals[j] = tall
            else:
                totals[j] += tall
        back[blocks + i] = jnp.where(low, other * SCALE, out).astype(BF16)
    for j in range(blocks):
        back[j] = totals[j].T.astype(BF16)
    for k, out in enumerate(outs):
        out[...] = back[jnp.bitwise_xor(entry, k)]


def split_rows(column):
    row = jnp.broadcast_to(column, (column.shape[0], LANES)).T[:TAIL, :]
    high = row.astype(BF16).astype(F32)
    line = lax.broadcasted_iota(jnp.int32, row.shape, 0)
    return jnp.where(line == 0, high, row - high).astype(BF16)


def regroup(sizes, ins, parts):
    heads = sizes[0] * sizes[1]
    _, entry, _ = place(sizes)
    for k, piece in enumerate(ins):
        parts[jnp.bitwise_xor(entry, k)] = piece[...]
    for head in range(0, heads, 2):
        yield slice(head * DH, (head + 2) * DH), parts[head], parts[head + 1]


def attended_kernel(sizes, alive, *rest):
    heads = sizes[0] * sizes[1]
    ins, (ls, parts) = rest[:heads], rest[heads:]
    for cols, one, two in regroup(sizes, ins, parts):
        both = jnp.concatenate([one[:, DH:], two[:, DH:]], axis=1)
        ls[:, cols] = jnp.where(alive[...] > 0.0, both.astype(F32), 0.0).astype(BF16)


def project_block(seg, wp, ws, lp, ls, out, slot):
    rows = lp.shape[0]

    @pl.when(seg == 0)
    def _():
        total = right_product(lp[...], wp) + right_product(ls[...], ws)
        out[slot, :rows, :] = total.astype(BF16)

    @pl.when(seg == 1)
    def _():
        out[slot, :rows, :] = right_product(lp[...], wp).astype(BF16)


def send_kernel(sizes, ls, prim, second, spread, wp, w3, w1, *rest):
    heads = sizes[0] * sizes[1]
    ins, (sent, lp, parts) = rest[:heads], rest[heads:]
    for cols, one, two in regroup(sizes, ins, parts):
        lp[:, cols] = jnp.concatenate([one[:, :DH], two[:, :DH]], axis=1)
    seg, _, _ = place(sizes)
    rows, feats = prim.shape[0], sent.shape[2]
    project_block(seg, wp[3], w3[...], lp, ls, sent, 0)
    project_block(seg, wp[1], w1[...], lp, ls, sent, 1)
    term = lp[...].astype(F32) * prim[...].astype(F32)
    also = ls[...].astype(F32) * second[...].astype(F32)
    term = term + jnp.where(seg == 0, also, 0.0)
    column = jnp.sum(term, axis=1, keepdims=True) * spread[:, :1]
    sent[0, rows:, :] = jnp.zeros((TAIL, feats), BF16)
    sent[1, rows:, :] = jnp.zeros((TAIL, feats), BF16)
    sent[0, rows:, :rows] = split_rows(column)


def keep_kernel(sizes, lp, ls, wp, w2, w0, kept):
    seg, _, _ = place(sizes)
    project_block(seg, wp[2], w2[...], lp, ls, kept, 0)
    project_block(seg, wp[0], w0[...], lp, ls, kept, 1)


def layer_kernel(a0, a1, a2, a3, w0, w1, middle, edge, mirrored, w3, own, out, obuf, w2, sem):
    seg = lax.axis_index("segment")

    @pl.when(seg == 0)
    def _():
        obuf[...] = own[...]

    @pl.when(seg == 1)
    def _():
        parity = lax.rem(lax.axis_index("blk"), 2)
        depth, quarter = w2.shape[0], edge.shape[0]
        for lent, side in ((edge, parity), (mirrored, 1 - parity)):
            start = pl.multiple_of(side * (depth - quarter), quarter)
            w2[pl.ds(start, quarter), :] = lent[...]
        w2[quarter : depth - quarter, :] = middle[...]
        total = right_product(a0[...], w0[...])
        for a, w in ((a1, w1), (a2, w2), (a3, w3)):
            total += right_product(a[...], w[...])
        obuf[...] = total.astype(BF16)

    leaving = pltpu.make_async_copy(obuf, out, sem)
    leaving.start()
    leaving.wait()


def fold_kernel(kept, got, sent, out, ends):
    rows = kept.shape[1]
    out[...] = (kept[0].astype(F32) + got[0, :rows, :].astype(F32)).astype(BF16)
    mine = sent[0, rows:, :rows].astype(F32)
    theirs = got[0, rows:, :rows].astype(F32)
    total = mine[0:1] + mine[1:2] + theirs[0:1] + theirs[1:2]
    ends[...] = jnp.broadcast_to(total, ends.shape)


ANYWHERE = pl.BlockSpec(memory_space=pltpu.HBM)
INSIDE = pl.BlockSpec(memory_space=pltpu.VMEM)
SCALARS = pl.BlockSpec(memory_space=pltpu.SMEM)


def call(body, ins, specs, outs, scratch=(), limit=16, flops=0, out_specs=None):
    inside = out_specs is None
    ins = [
        pltpu.with_memory_space_constraint(x, pltpu.HBM) if spec is ANYWHERE else x
        for x, spec in zip(ins, specs)
    ]
    return pl.pallas_call(
        body,
        in_specs=list(specs),
        out_specs=[INSIDE] * len(outs) if inside else out_specs,
        out_shape=[(pltpu.VMEM if inside else jax.ShapeDtypeStruct)(s, d) for s, d in outs],
        scratch_shapes=list(scratch),
        compiler_params=pltpu.CompilerParams(vmem_limit_bytes=limit << 20),
        cost_estimate=pl.CostEstimate(flops=flops, transcendentals=0, bytes_accessed=1 << 20),
    )(*ins)


def scales_kernel(width, spread, inverse, shrink):
    root = spread[...]
    inverse[...] = 1.0 / root
    shrink[...] = 1.0 / (width * root * root * root)


def leave_kernel(kept, got, ends, far_ends, far, states, gain, inverse, shrink, grad):
    rows = states.shape[0]
    row = ends[...] + far_ends[...]
    term = jnp.broadcast_to(row[:1], (LANES, rows)).T[:, :1]
    scaled = term * shrink[:, :1]
    total = kept[1].astype(F32) + got[1, :rows, :].astype(F32) + far[...].astype(F32)
    grad[...] = (gain[...] * total * inverse[:, :1] - states[...].astype(F32) * scaled).astype(BF16)


def per_device_heads(sizes, segment_in, norm_gains, projections, live_counts, cotangent):
    n_seg, n_blk, n_mp = sizes
    heads = n_seg * n_blk
    states = segment_in[0]
    rows, width = states.shape
    feats = cotangent.shape[1]
    group = projections.shape[3]
    counts = live_counts.T

    def swap(x, over_heads, over_mp):
        pairs = [
            (e * n_mp + m, (e ^ over_heads) * n_mp + (m ^ over_mp))
            for e in range(heads)
            for m in range(n_mp)
        ]
        return lax.ppermute(x, AXES, pairs)

    def exchange(pieces, among=heads):
        moved = [pieces[0]]
        for k in range(1, among):
            moved.append(swap(pieces[k], k, 0))
        return moved

    far_cot = swap(cotangent, 0, 2)
    near_cot = swap(cotangent, 0, 1)
    tiles = group // LANES
    mixed = projections.reshape(width, 2, tiles, LANES).transpose(0, 2, 1, 3)
    mixed = mixed.reshape(width * 2 * tiles, LANES)
    made = call(
        functools.partial(enter_kernel, sizes),
        (states, norm_gains, mixed, counts),
        [ANYWHERE] * 3 + [SCALARS],
        [((n_mp, feats, group), BF16)]
        + [((feats, group), BF16)] * n_mp
        + [
            ((rows, feats), BF16),
            ((rows, feats), BF16),
            ((1, feats), F32),
            ((rows, LANES), F32),
            ((rows, group), BF16),
            ((rows, group), BF16),
            ((rows, LANES), F32),
            ((TAIL, LANES), BF16),
        ],
        [
            pltpu.VMEM((rows, width), BF16),
            pltpu.VMEM((1, width), F32),
            pltpu.VMEM((width * 2 * tiles, LANES), BF16),
            pltpu.VMEM((rows, width), BF16),
            pltpu.SemaphoreType.DMA((n_mp,)),
            pltpu.SemaphoreType.DMA((2,)),
        ],
        24,
        8 << 30,
    )
    wp, ws = made[0], made[1 : 1 + n_mp]
    own, own_states, own_gain, spread, prim, sec, alive, tail = made[1 + n_mp :]
    pieces = call(
        functools.partial(prepare_kernel, sizes),
        (prim, sec, tail),
        [INSIDE] * 3,
        [((rows + TAIL, LANES), BF16)] * heads,
        [pltpu.VMEM((heads, rows, LANES), BF16)],
    )
    pieces = exchange(pieces)
    quarter = feats // 4
    middle, edge = call(
        lend_kernel,
        (ws[2],),
        [INSIDE],
        [((feats - 2 * quarter, group), BF16), ((quarter, group), BF16)],
    )
    lent_3 = swap(ws[3], 0, 3)
    far_cot, spread = lax.optimization_barrier((far_cot, spread))
    cross_cot = swap(far_cot, 0, 1)
    acc = call(
        part_kernel,
        (cotangent, near_cot, far_cot, *ws[:3]),
        [INSIDE] * 6,
        [((rows, group), F32)],
        (),
        16,
        1 << 30,
    )[0]
    here, turning = call(
        pack_kernel,
        (acc, alive, cross_cot, ws[3]),
        [INSIDE] * 4,
        [((rows, group // n_seg), BF16)] * n_seg,
        (),
        16,
        1 << 30,
    )[::-1]
    turned = swap(turning, n_blk, 0)
    grads = call(
        functools.partial(deal_kernel, sizes),
        (here, turned),
        [INSIDE] * 2,
        [((rows // 2, LANES), BF16)] * n_blk,
        [pltpu.VMEM((n_blk, rows // 2, LANES), BF16)],
    )
    grads = exchange(grads, n_blk)
    lent_2 = swap(middle, 0, 2)
    lent_edge = swap(edge, 0, 2)
    inverse, shrink = call(
        functools.partial(scales_kernel, width), (spread,), [INSIDE], [((rows, LANES), F32)] * 2
    )
    pieces = call(
        functools.partial(attend_kernel, sizes),
        (*pieces, *grads),
        [INSIDE] * (heads + n_blk),
        [((rows, LANES), BF16)] * heads,
        [
            pltpu.VMEM((heads, rows + TAIL, LANES), BF16),
            pltpu.VMEM((n_blk, rows // 2, LANES), BF16),
            pltpu.VMEM((heads, rows, LANES), BF16),
            pltpu.VMEM((n_blk, LANES, rows), F32),
        ],
        24,
        4 << 30,
    )
    pieces = exchange(pieces)
    (ls,) = call(
        functools.partial(attended_kernel, sizes),
        (alive, *pieces),
        [INSIDE] * (1 + heads),
        [((rows, group), BF16)],
        [pltpu.VMEM((heads, rows, LANES), BF16)],
    )
    far_att = swap(ls, 0, 2)
    sent, lp = call(
        functools.partial(send_kernel, sizes),
        (ls, prim, sec, spread, wp, ws[3], ws[1], *pieces),
        [INSIDE] * (7 + heads),
        [((2, rows + TAIL, feats), BF16), ((rows, group), BF16)],
        [pltpu.VMEM((heads, rows, LANES), BF16)],
        16,
        2 << 30,
    )
    got = swap(sent, 0, 1)
    mirrored = swap(lent_edge, 1, 0)
    (kept,) = call(
        functools.partial(keep_kernel, sizes),
        (lp, ls, wp, ws[2], ws[0]),
        [INSIDE] * 5,
        [((2, rows, feats), BF16)],
        (),
        16,
        2 << 30,
    )
    half, ends = call(
        fold_kernel, (kept, got, sent), [INSIDE] * 3, [((rows, feats), BF16), ((8, rows), F32)]
    )
    far = swap(half, 0, 2)
    far_ends = swap(ends, 0, 2)
    own_att, lent_1, ends = lax.optimization_barrier((ls, ws[1], ends))
    lent_1 = swap(lent_1, 0, 1)
    near_att = swap(own_att, 0, 1)
    cross_att = swap(far_att, 0, 1)
    (out,) = call(
        layer_kernel,
        (
            *(ls, near_att, far_att, cross_att),
            *(ws[0], lent_1, lent_2, lent_edge, mirrored, lent_3, own),
        ),
        [INSIDE] * 11,
        [((rows, feats), BF16)],
        [
            pltpu.VMEM((rows, feats), BF16),
            pltpu.VMEM((feats, group), BF16),
            pltpu.SemaphoreType.DMA,
        ],
        16,
        2 << 30,
        [ANYWHERE],
    )
    (grad,) = call(
        leave_kernel,
        (kept, got, ends, far_ends, far, own_states, own_gain, inverse, shrink),
        [INSIDE] * 9,
        [((rows, feats), BF16)],
        out_specs=[INSIDE],
    )
    return (out[None], grad[None])


def solution(mesh):
    sizes = tuple(mesh.shape[axis] for axis in AXES)
    n_seg, n_blk, n_mp = sizes
    by_heads = n_seg == 2 and n_blk <= WIN and n_blk & (n_blk - 1) == 0 and n_blk > 1 and n_mp == 4

    def body(segment_in, norm_gains, projections, live_counts, cotangent):
        rows, group = segment_in.shape[1], projections.shape[3]
        if by_heads:
            assert n_seg * n_blk * DH == group and group == 4 * LANES and rows % LANES == 0
            return per_device_heads(
                sizes, segment_in, norm_gains, projections, live_counts, cotangent
            )
        return per_device_windows(segment_in, norm_gains, projections, live_counts, cotangent)

    in_specs = (
        P("segment", "blk", None),
        P("segment", None),
        P("segment", None, None, "mp"),
        P(None, "blk"),
        P("blk", "mp"),
    )
    out_specs = (P("segment", "blk", "mp"), P("segment", "blk", "mp"))
    return jax.shard_map(body, mesh=mesh, in_specs=in_specs, out_specs=out_specs, check_vma=False)
```

```python
import functools

import jax
import jax.numpy as jnp
from jax import lax
from jax.experimental import pallas as pl
from jax.experimental.pallas import tpu as pltpu
from jax.sharding import PartitionSpec as P


DH = 64
WIN = 4


EPSILON = 1e-06
SCALE = 0.125
NEGATIVE = -1e30
LANES = 128
TAIL = 16
AXES = ("segment", "blk", "mp")

F32 = jnp.float32
BF16 = jnp.bfloat16


def from_behind(x, axis, by):
    size = lax.axis_size(axis)
    pairs = [(i, i + by) for i in range(size) if 0 <= i + by < size]
    return lax.ppermute(x, axis, pairs)


def normalize(states, gain_row):
    widened = states.astype(jnp.float32)
    spread = jnp.sqrt(jnp.mean(widened * widened, axis=-1, keepdims=True) + EPSILON)
    return ((widened / spread * gain_row).astype(jnp.bfloat16), spread)


def right_product(left, right):
    return lax.dot_general(
        left, right, (((1,), (1,)), ((), ())), preferred_element_type=jnp.float32
    )


def per_device_windows(segment_in, norm_gains, projections, live_counts, cotangent):
    segment_pos = lax.axis_index("segment")
    model_index = lax.axis_index("mp")
    states = segment_in[0]
    gain_row = norm_gains[0]
    row_count, full_width = states.shape
    feature_width = cotangent.shape[1]
    w_primary = projections[0, :, 0, :]
    w_secondary = projections[0, :, 1, :]
    group_width = w_primary.shape[1]
    group_heads = group_width // DH
    normed, spread = normalize(states, gain_row)
    primary = jnp.dot(normed, w_primary, preferred_element_type=jnp.float32).astype(jnp.bfloat16)
    secondary = lax.cond(
        segment_pos == 0,
        lambda: jnp.dot(normed, w_secondary, preferred_element_type=jnp.float32).astype(
            jnp.bfloat16
        ),
        lambda: jnp.zeros_like(primary),
    )
    doc_keys, doc_values = from_behind((primary, secondary), "segment", 1)
    own_block = (doc_keys, doc_values, live_counts[0])
    window = [own_block]
    moving = own_block
    for _ in range(1, WIN):
        moving = from_behind((moving[0], moving[1], moving[2]), "blk", 1)
        window.append(moving)
    position = jnp.arange(row_count, dtype=jnp.int32)
    all_keys = jnp.concatenate([piece[0] for piece in window], 0).reshape(
        WIN * row_count, group_heads, DH
    )
    all_values = jnp.concatenate([piece[1] for piece in window], 0).reshape(
        WIN * row_count, group_heads, DH
    )
    key_live = jnp.concatenate([position < piece[2][0] for piece in window], 0)
    query_live = position < live_counts[1][0]
    query_heads = primary.reshape(row_count, group_heads, DH)
    scores = (
        jnp.einsum("qhd,khd->hqk", query_heads, all_keys, preferred_element_type=jnp.float32)
        * SCALE
    )
    scores = jnp.where(key_live[None, None, :], scores, NEGATIVE)
    row_max = jnp.max(scores, axis=-1, keepdims=True)
    expo = jnp.exp(scores - row_max)
    row_total = jnp.sum(expo, axis=-1, keepdims=True)
    softmax_out = expo / row_total
    weights_low = softmax_out.astype(jnp.bfloat16)
    attended = jnp.einsum(
        "hqk,khd->qhd", weights_low, all_values, preferred_element_type=jnp.float32
    ).astype(jnp.bfloat16)
    attended = jnp.where(query_live[:, None, None], attended, jnp.zeros_like(attended)).reshape(
        row_count, group_width
    )
    projected = lax.cond(
        segment_pos == 1,
        lambda: right_product(attended, w_secondary),
        lambda: jnp.zeros((row_count, full_width), jnp.float32),
    )
    layer_out = lax.psum_scatter(
        projected.astype(jnp.bfloat16), "mp", scatter_dimension=1, tiled=True
    )
    own_normed = lax.dynamic_slice_in_dim(normed, model_index * feature_width, feature_width, 1)
    segment_out = jnp.where(segment_pos == 0, own_normed, layer_out)[None]
    grad_out = jnp.dot(
        lax.all_gather(cotangent, "mp", axis=1, tiled=True),
        w_secondary,
        preferred_element_type=jnp.float32,
    )
    grad_out = grad_out.astype(jnp.bfloat16)
    grad_out = jnp.where(query_live[:, None], grad_out, jnp.zeros_like(grad_out))
    grad_heads = grad_out.reshape(row_count, group_heads, DH)
    grad_probs = jnp.einsum(
        "qhd,khd->hqk", grad_heads, all_values, preferred_element_type=jnp.float32
    )
    row_delta = jnp.sum(softmax_out * grad_probs, axis=-1, keepdims=True)
    grad_scores = (softmax_out * (grad_probs - row_delta)).astype(jnp.bfloat16)
    grad_queries = (
        (
            SCALE
            * jnp.einsum("hqk,khd->qhd", grad_scores, all_keys, preferred_element_type=jnp.float32)
        )
        .astype(jnp.bfloat16)
        .reshape(row_count, group_width)
    )
    key_parts = (
        SCALE
        * jnp.einsum("hqk,qhd->khd", grad_scores, query_heads, preferred_element_type=jnp.float32)
    ).reshape(WIN, row_count, group_width)
    value_parts = jnp.einsum(
        "hqk,qhd->khd", weights_low, grad_heads, preferred_element_type=jnp.float32
    ).reshape(WIN, row_count, group_width)
    key_total = key_parts[WIN - 1]
    value_total = value_parts[WIN - 1]
    for offset in range(WIN - 2, -1, -1):
        arrived = (
            from_behind(key_total.astype(jnp.bfloat16), "blk", -1).astype(key_total.dtype),
            from_behind(value_total.astype(jnp.bfloat16), "blk", -1).astype(value_total.dtype),
        )
        key_total = arrived[0] + key_parts[offset]
        value_total = arrived[1] + value_parts[offset]
    grad_keys = key_total.astype(jnp.bfloat16)
    grad_values = value_total.astype(jnp.bfloat16)
    back_keys, back_values = from_behind((grad_keys, grad_values), "segment", -1)
    partial_grad = lax.cond(
        segment_pos == 0,
        lambda: right_product(back_keys, w_primary) + right_product(back_values, w_secondary),
        lambda: right_product(grad_queries, w_primary),
    )
    widened = states.astype(jnp.float32)
    summed = lax.psum_scatter(
        partial_grad.astype(jnp.bfloat16), "mp", scatter_dimension=1, tiled=True
    ).astype(jnp.float32)
    own_states = lax.dynamic_slice_in_dim(widened, model_index * feature_width, feature_width, 1)
    own_gain = lax.dynamic_slice_in_dim(gain_row, model_index * feature_width, feature_width, 0)
    row_term = lax.psum(jnp.sum(summed * own_gain * own_states, axis=-1, keepdims=True), "mp")
    input_grad = (
        own_gain * summed / spread - own_states * row_term / (full_width * spread**3)
    ).astype(jnp.bfloat16)
    return (segment_out, input_grad[None])


def place(sizes):
    seg = lax.axis_index("segment")
    return seg, seg * sizes[1] + lax.axis_index("blk"), lax.axis_index("mp")


def enter_kernel(sizes, states, gain, w, *rest):
    n_mp = sizes[2]
    wp, ws = rest[0], rest[1 : 1 + n_mp]
    own, own_states, own_gain, spread, prim, sec = rest[1 + n_mp : 7 + n_mp]
    xbuf, gbuf, wbuf, normed, sems, ready = rest[7 + n_mp :]
    seg, _, model = place(sizes)
    rows, width = xbuf.shape
    depth = width // n_mp
    tiles = wp.shape[2] // LANES
    pack = 2 * tiles
    group = 2 * LANES // pack
    lines = depth * pack
    first_copies = [
        pltpu.make_async_copy(states, xbuf, ready.at[0]),
        pltpu.make_async_copy(gain, gbuf, ready.at[1]),
    ]
    copies = []
    for c in range(n_mp):
        start = pl.multiple_of(jnp.bitwise_xor(model, c) * lines, lines)
        copies.append(
            pltpu.make_async_copy(
                w.at[pl.ds(start, lines), :], wbuf.at[pl.ds(c * lines, lines), :], sems.at[c]
            )
        )
    for copy in first_copies + copies:
        copy.start()
    here = lax.broadcasted_iota(jnp.int32, (2 * LANES, 2 * LANES), 0)
    there = lax.broadcasted_iota(jnp.int32, (2 * LANES, 2 * LANES), 1)
    source = pack * lax.rem(here, group) + lax.div(here, group)
    mix = jnp.where(there == source, 1.0, 0.0).astype(BF16)
    part_rows = 16

    def norm_rows(first):
        line = slice(first, first + part_rows)
        wide = xbuf[line, :].astype(F32)
        mean = jnp.sum(wide * wide, axis=1, keepdims=True) * (1.0 / width)
        root = jnp.sqrt(mean + EPSILON)
        normed[line, :] = (wide * (1.0 / root) * gbuf[...]).astype(BF16)
        spread[line, :] = jnp.broadcast_to(root, (part_rows, LANES))

    for copy in first_copies:
        copy.wait()
    pairs = depth // (2 * group)
    every = n_mp * pairs * part_rows // rows
    for c in range(n_mp):
        copies[c].wait()
        for pair in range(pairs):
            if (c * pairs + pair) % every == 0:
                norm_rows((c * pairs + pair) // every * part_rows)
            base = c * lines + pair * 4 * LANES
            left = wbuf[base : base + 2 * LANES, :]
            right = wbuf[base + 2 * LANES : base + 4 * LANES, :]
            both = jnp.concatenate([left, right], axis=1)
            ordered = jnp.dot(mix, both, preferred_element_type=F32).astype(BF16)
            first = 2 * pair * group
            for slot in range(pack):
                target = (wp.at[c], ws[c])[slot % 2]
                tile = slice(slot // 2 * LANES, (slot // 2 + 1) * LANES)
                part = ordered[slot * group : (slot + 1) * group, :]
                target[first : first + group, tile] = part[:, :LANES]
                target[first + group : first + 2 * group, tile] = part[:, LANES:]

    def product(weights):
        total = None
        for c in range(n_mp):
            span = pl.ds(pl.multiple_of(jnp.bitwise_xor(model, c) * depth, depth), depth)
            term = jnp.dot(normed[:, span], weights(c), preferred_element_type=F32)
            total = term if total is None else total + term
        return total.astype(BF16)

    prim[...] = product(lambda c: wp[c])

    @pl.when(seg == 0)
    def _():
        sec[...] = product(lambda c: ws[c][...])

    mine = pl.ds(pl.multiple_of(model * depth, depth), depth)
    own[...] = normed[:, mine]
    own_states[...] = xbuf[:, mine]
    own_gain[...] = gbuf[:, mine]


def marks_kernel(counts, alive, tail):
    line = lax.broadcasted_iota(jnp.int32, alive.shape, 0)
    last = jnp.where(lax.axis_index("segment") == 0, alive.shape[0], counts[0, 1])
    alive[...] = jnp.where(line < last, 1.0, 0.0)
    tail[...] = (jnp.full(tail.shape, 1.0, F32) * counts[0, 0].astype(F32)).astype(BF16)


def lend_kernel(w2, middle, edge):
    parity = lax.rem(lax.axis_index("blk"), 2)
    depth, quarter = w2.shape[0], edge.shape[0]
    middle[...] = w2[quarter : depth - quarter, :]
    start = pl.multiple_of(parity * (depth - quarter), quarter)
    edge[...] = w2[pl.ds(start, quarter), :]


def part_kernel(c0, c1, c2, w0, w1, w2, acc):
    @pl.when(lax.axis_index("segment") == 1)
    def _():
        acc[...] = jnp.dot(c0[...], w0[...], preferred_element_type=F32)
        acc[...] += jnp.dot(c1[...], w1[...], preferred_element_type=F32)
        acc[...] += jnp.dot(c2[...], w2[...], preferred_element_type=F32)


def pack_kernel(sizes, prim, sec, acc, alive, tail, c3, w3, *rest):
    heads = sizes[0] * sizes[1]
    second, outs, (parts,) = rest[0], rest[1 : 1 + heads], rest[1 + heads :]
    seg, entry, _ = place(sizes)
    rows = prim.shape[0]

    @pl.when(seg == 0)
    def _():
        second[...] = sec[...]

    @pl.when(seg == 1)
    def _():
        total = acc[...] + jnp.dot(c3[...], w3[...], preferred_element_type=F32)
        for tile in range(total.shape[1] // LANES):
            cols = slice(tile * LANES, (tile + 1) * LANES)
            second[:, cols] = jnp.where(alive[...] > 0.0, total[:, cols], 0.0).astype(BF16)

    for head in range(heads):
        cols = slice(head * DH, (head + 1) * DH)
        parts[head] = jnp.concatenate([prim[:, cols], second[:, cols]], axis=1)
    for k, out in enumerate(outs):
        out[:rows, :] = parts[jnp.bitwise_xor(entry, k)]
        out[rows:, :] = tail[...]


def live_keys(piece, rows):
    position = lax.broadcasted_iota(jnp.int32, (1, rows), 1).astype(F32)
    count = piece[rows : rows + 1, :].astype(F32)
    return position < jnp.concatenate([count] * (rows // LANES), axis=1)


def attend_kernel(sizes, *rest):
    heads = sizes[0] * sizes[1]
    blocks = sizes[1]
    ins, outs = rest[:heads], rest[heads : 2 * heads]
    parts, back, totals = rest[2 * heads :]
    _, entry, _ = place(sizes)
    rows = outs[0].shape[0]
    for k, piece in enumerate(ins):
        parts[jnp.bitwise_xor(entry, k)] = piece[...]
    low = lax.broadcasted_iota(jnp.int32, (rows, LANES), 1) < DH
    zero = jnp.zeros((rows, LANES), BF16)
    live = [live_keys(parts[j], rows) for j in range(blocks)]
    for i in range(blocks):
        both = parts[blocks + i, :rows, :]
        query = jnp.where(low, both * BF16(SCALE), zero)
        grad = jnp.where(low, zero, both)
        flip_query = query.astype(F32).T.astype(BF16)
        flip_grad = grad.astype(F32).T.astype(BF16)
        scores = []
        for j in range(i + 1):
            product = right_product(query, parts[j, :rows, :])
            scores.append(jnp.where(live[j], product, NEGATIVE))
        top = jnp.max(functools.reduce(jnp.maximum, scores), axis=1, keepdims=True)
        expo = [jnp.exp(s - top) for s in scores]
        total = jnp.sum(functools.reduce(jnp.add, expo), axis=1, keepdims=True)
        share = 1.0 / total
        probs = [e * share for e in expo]
        slopes = [right_product(grad, parts[j, :rows, :]) for j in range(i + 1)]
        delta = functools.reduce(jnp.add, [p * g for p, g in zip(probs, slopes)])
        delta = jnp.sum(delta, axis=1, keepdims=True)
        out = jnp.zeros((rows, LANES), F32)
        other = jnp.zeros((rows, LANES), F32)
        for j in range(i + 1):
            prob = probs[j].astype(BF16)
            slope = (probs[j] * (slopes[j] - delta)).astype(BF16)
            other += jnp.dot(slope, parts[j, :rows, :], preferred_element_type=F32)
            out += jnp.dot(prob, parts[j, :rows, :], preferred_element_type=F32)
            tall = jnp.dot(flip_query, slope, preferred_element_type=F32)
            tall += jnp.dot(flip_grad, prob, preferred_element_type=F32)
            if i == j:
                totals[j] = tall
            else:
                totals[j] += tall
        back[blocks + i] = jnp.where(low, other * SCALE, out).astype(BF16)
    for j in range(blocks):
        back[j] = totals[j].T.astype(BF16)
    for k, out in enumerate(outs):
        out[...] = back[jnp.bitwise_xor(entry, k)]


def split_rows(column):
    row = jnp.broadcast_to(column, (column.shape[0], LANES)).T[:TAIL, :]
    high = row.astype(BF16).astype(F32)
    line = lax.broadcasted_iota(jnp.int32, row.shape, 0)
    return jnp.where(line == 0, high, row - high).astype(BF16)


def regroup(sizes, ins, parts):
    heads = sizes[0] * sizes[1]
    _, entry, _ = place(sizes)
    for k, piece in enumerate(ins):
        parts[jnp.bitwise_xor(entry, k)] = piece[...]
    for head in range(0, heads, 2):
        yield slice(head * DH, (head + 2) * DH), parts[head], parts[head + 1]


def attended_kernel(sizes, alive, *rest):
    heads = sizes[0] * sizes[1]
    ins, (ls, parts) = rest[:heads], rest[heads:]
    for cols, one, two in regroup(sizes, ins, parts):
        both = jnp.concatenate([one[:, DH:], two[:, DH:]], axis=1)
        ls[:, cols] = jnp.where(alive[...] > 0.0, both.astype(F32), 0.0).astype(BF16)


def project_block(seg, wp, ws, lp, ls, out, slot):
    rows = lp.shape[0]

    @pl.when(seg == 0)
    def _():
        total = right_product(lp[...], wp) + right_product(ls[...], ws)
        out[slot, :rows, :] = total.astype(BF16)

    @pl.when(seg == 1)
    def _():
        out[slot, :rows, :] = right_product(lp[...], wp).astype(BF16)


def send_kernel(sizes, ls, prim, second, spread, wp, w3, w1, *rest):
    heads = sizes[0] * sizes[1]
    ins, (sent, lp, parts) = rest[:heads], rest[heads:]
    for cols, one, two in regroup(sizes, ins, parts):
        lp[:, cols] = jnp.concatenate([one[:, :DH], two[:, :DH]], axis=1)
    seg, _, _ = place(sizes)
    rows, feats = prim.shape[0], sent.shape[2]
    project_block(seg, wp[3], w3[...], lp, ls, sent, 0)
    project_block(seg, wp[1], w1[...], lp, ls, sent, 1)
    term = lp[...].astype(F32) * prim[...].astype(F32)
    also = ls[...].astype(F32) * second[...].astype(F32)
    term = term + jnp.where(seg == 0, also, 0.0)
    column = jnp.sum(term, axis=1, keepdims=True) * spread[:, :1]
    sent[0, rows:, :] = jnp.zeros((TAIL, feats), BF16)
    sent[1, rows:, :] = jnp.zeros((TAIL, feats), BF16)
    sent[0, rows:, :rows] = split_rows(column)


def keep_kernel(sizes, lp, ls, wp, w2, w0, kept):
    seg, _, _ = place(sizes)
    project_block(seg, wp[2], w2[...], lp, ls, kept, 0)
    project_block(seg, wp[0], w0[...], lp, ls, kept, 1)


def layer_kernel(a0, a1, a2, a3, w0, w1, middle, edge, mirrored, w3, own, out, obuf, w2, sem):
    seg = lax.axis_index("segment")

    @pl.when(seg == 0)
    def _():
        obuf[...] = own[...]

    @pl.when(seg == 1)
    def _():
        parity = lax.rem(lax.axis_index("blk"), 2)
        depth, quarter = w2.shape[0], edge.shape[0]
        for lent, side in ((edge, parity), (mirrored, 1 - parity)):
            start = pl.multiple_of(side * (depth - quarter), quarter)
            w2[pl.ds(start, quarter), :] = lent[...]
        w2[quarter : depth - quarter, :] = middle[...]
        total = right_product(a0[...], w0[...])
        for a, w in ((a1, w1), (a2, w2), (a3, w3)):
            total += right_product(a[...], w[...])
        obuf[...] = total.astype(BF16)

    leaving = pltpu.make_async_copy(obuf, out, sem)
    leaving.start()
    leaving.wait()


def fold_kernel(kept, got, sent, out, ends):
    rows = kept.shape[1]
    out[...] = (kept[0].astype(F32) + got[0, :rows, :].astype(F32)).astype(BF16)
    mine = sent[0, rows:, :rows].astype(F32)
    theirs = got[0, rows:, :rows].astype(F32)
    total = mine[0:1] + mine[1:2] + theirs[0:1] + theirs[1:2]
    ends[...] = jnp.broadcast_to(total, ends.shape)


ANYWHERE = pl.BlockSpec(memory_space=pltpu.HBM)
INSIDE = pl.BlockSpec(memory_space=pltpu.VMEM)
SCALARS = pl.BlockSpec(memory_space=pltpu.SMEM)


def call(body, ins, specs, outs, scratch=(), limit=16, flops=0, out_specs=None):
    inside = out_specs is None
    ins = [
        pltpu.with_memory_space_constraint(x, pltpu.HBM) if spec is ANYWHERE else x
        for x, spec in zip(ins, specs)
    ]
    return pl.pallas_call(
        body,
        in_specs=list(specs),
        out_specs=[INSIDE] * len(outs) if inside else out_specs,
        out_shape=[(pltpu.VMEM if inside else jax.ShapeDtypeStruct)(s, d) for s, d in outs],
        scratch_shapes=list(scratch),
        compiler_params=pltpu.CompilerParams(vmem_limit_bytes=limit << 20),
        cost_estimate=pl.CostEstimate(flops=flops, transcendentals=0, bytes_accessed=1 << 20),
    )(*ins)


def scales_kernel(width, spread, inverse, shrink):
    root = spread[...]
    inverse[...] = 1.0 / root
    shrink[...] = 1.0 / (width * root * root * root)


def leave_kernel(kept, got, ends, far_ends, far, states, gain, inverse, shrink, grad):
    rows = states.shape[0]
    row = ends[...] + far_ends[...]
    term = jnp.broadcast_to(row[:1], (LANES, rows)).T[:, :1]
    scaled = term * shrink[:, :1]
    total = kept[1].astype(F32) + got[1, :rows, :].astype(F32) + far[...].astype(F32)
    grad[...] = (gain[...] * total * inverse[:, :1] - states[...].astype(F32) * scaled).astype(BF16)


def per_device_heads(sizes, segment_in, norm_gains, projections, live_counts, cotangent):
    n_seg, n_blk, n_mp = sizes
    heads = n_seg * n_blk
    states = segment_in[0]
    rows, width = states.shape
    feats = cotangent.shape[1]
    group = projections.shape[3]
    counts = live_counts.T

    def swap(x, over_heads, over_mp):
        pairs = [
            (e * n_mp + m, (e ^ over_heads) * n_mp + (m ^ over_mp))
            for e in range(heads)
            for m in range(n_mp)
        ]
        return lax.ppermute(x, AXES, pairs)

    def exchange(pieces):
        moved = [pieces[0]]
        for k in range(1, heads):
            moved.append(swap(pieces[k], k, 0))
        return moved

    far_cot = swap(cotangent, 0, 2)
    near_cot = swap(cotangent, 0, 1)
    tiles = group // LANES
    mixed = projections.reshape(width, 2, tiles, LANES).transpose(0, 2, 1, 3)
    mixed = mixed.reshape(width * 2 * tiles, LANES)
    made = call(
        functools.partial(enter_kernel, sizes),
        (states, norm_gains, mixed),
        [ANYWHERE] * 3,
        [((n_mp, feats, group), BF16)]
        + [((feats, group), BF16)] * n_mp
        + [
            ((rows, feats), BF16),
            ((rows, feats), BF16),
            ((1, feats), F32),
            ((rows, LANES), F32),
            ((rows, group), BF16),
            ((rows, group), BF16),
        ],
        [
            pltpu.VMEM((rows, width), BF16),
            pltpu.VMEM((1, width), F32),
            pltpu.VMEM((width * 2 * tiles, LANES), BF16),
            pltpu.VMEM((rows, width), BF16),
            pltpu.SemaphoreType.DMA((n_mp,)),
            pltpu.SemaphoreType.DMA((2,)),
        ],
        24,
        8 << 30,
    )
    wp, ws = made[0], made[1 : 1 + n_mp]
    own, own_states, own_gain, spread, prim, sec = made[1 + n_mp :]
    alive, tail = call(
        marks_kernel, (counts,), [SCALARS], [((rows, LANES), F32), ((TAIL, LANES), BF16)]
    )
    quarter = feats // 4
    middle, edge = call(
        lend_kernel,
        (ws[2],),
        [INSIDE],
        [((feats - 2 * quarter, group), BF16), ((quarter, group), BF16)],
    )
    lent_3 = swap(ws[3], 0, 3)
    far_cot, spread = lax.optimization_barrier((far_cot, spread))
    cross_cot = swap(far_cot, 0, 1)
    acc = call(
        part_kernel,
        (cotangent, near_cot, far_cot, *ws[:3]),
        [INSIDE] * 6,
        [((rows, group), F32)],
        (),
        16,
        1 << 30,
    )[0]
    made = call(
        functools.partial(pack_kernel, sizes),
        (prim, sec, acc, alive, tail, cross_cot, ws[3]),
        [INSIDE] * 7,
        [((rows, group), BF16)] + [((rows + TAIL, LANES), BF16)] * heads,
        [pltpu.VMEM((heads, rows, LANES), BF16)],
        16,
        1 << 30,
    )
    second, pieces = made[0], made[1:]
    pieces = exchange(pieces)
    lent_2 = swap(middle, 0, 2)
    lent_edge = swap(edge, 0, 2)
    inverse, shrink = call(
        functools.partial(scales_kernel, width), (spread,), [INSIDE], [((rows, LANES), F32)] * 2
    )
    pieces = call(
        functools.partial(attend_kernel, sizes),
        pieces,
        [INSIDE] * heads,
        [((rows, LANES), BF16)] * heads,
        [
            pltpu.VMEM((heads, rows + TAIL, LANES), BF16),
            pltpu.VMEM((heads, rows, LANES), BF16),
            pltpu.VMEM((n_blk, LANES, rows), F32),
        ],
        24,
        4 << 30,
    )
    pieces = exchange(pieces)
    (ls,) = call(
        functools.partial(attended_kernel, sizes),
        (alive, *pieces),
        [INSIDE] * (1 + heads),
        [((rows, group), BF16)],
        [pltpu.VMEM((heads, rows, LANES), BF16)],
    )
    far_att = swap(ls, 0, 2)
    sent, lp = call(
        functools.partial(send_kernel, sizes),
        (ls, prim, second, spread, wp, ws[3], ws[1], *pieces),
        [INSIDE] * (7 + heads),
        [((2, rows + TAIL, feats), BF16), ((rows, group), BF16)],
        [pltpu.VMEM((heads, rows, LANES), BF16)],
        16,
        2 << 30,
    )
    got = swap(sent, 0, 1)
    mirrored = swap(lent_edge, 1, 0)
    (kept,) = call(
        functools.partial(keep_kernel, sizes),
        (lp, ls, wp, ws[2], ws[0]),
        [INSIDE] * 5,
        [((2, rows, feats), BF16)],
        (),
        16,
        2 << 30,
    )
    half, ends = call(
        fold_kernel, (kept, got, sent), [INSIDE] * 3, [((rows, feats), BF16), ((8, rows), F32)]
    )
    far = swap(half, 0, 2)
    far_ends = swap(ends, 0, 2)
    own_att, lent_1, ends = lax.optimization_barrier((ls, ws[1], ends))
    lent_1 = swap(lent_1, 0, 1)
    near_att = swap(own_att, 0, 1)
    cross_att = swap(far_att, 0, 1)
    (out,) = call(
        layer_kernel,
        (
            *(ls, near_att, far_att, cross_att),
            *(ws[0], lent_1, lent_2, lent_edge, mirrored, lent_3, own),
        ),
        [INSIDE] * 11,
        [((rows, feats), BF16)],
        [
            pltpu.VMEM((rows, feats), BF16),
            pltpu.VMEM((feats, group), BF16),
            pltpu.SemaphoreType.DMA,
        ],
        16,
        2 << 30,
        [ANYWHERE],
    )
    (grad,) = call(
        leave_kernel,
        (kept, got, ends, far_ends, far, own_states, own_gain, inverse, shrink),
        [INSIDE] * 9,
        [((rows, feats), BF16)],
        out_specs=[INSIDE],
    )
    return (out[None], grad[None])


def solution(mesh):
    sizes = tuple(mesh.shape[axis] for axis in AXES)
    n_seg, n_blk, n_mp = sizes
    by_heads = n_seg == 2 and n_blk <= WIN and n_blk & (n_blk - 1) == 0 and n_blk > 1 and n_mp == 4

    def body(segment_in, norm_gains, projections, live_counts, cotangent):
        rows, group = segment_in.shape[1], projections.shape[3]
        if by_heads:
            assert n_seg * n_blk * DH == group and group == 4 * LANES and rows % LANES == 0
            return per_device_heads(
                sizes, segment_in, norm_gains, projections, live_counts, cotangent
            )
        return per_device_windows(segment_in, norm_gains, projections, live_counts, cotangent)

    in_specs = (
        P("segment", "blk", None),
        P("segment", None),
        P("segment", None, None, "mp"),
        P(None, "blk"),
        P("blk", "mp"),
    )
    out_specs = (P("segment", "blk", "mp"), P("segment", "blk", "mp"))
    return jax.shard_map(body, mesh=mesh, in_specs=in_specs, out_specs=out_specs, check_vma=False)
```

```python
import functools

import jax
import jax.numpy as jnp
from jax import lax
from jax.experimental import pallas as pl
from jax.experimental.pallas import tpu as pltpu
from jax.sharding import PartitionSpec as P


DH = 64
WIN = 4


EPSILON = 1e-06
SCALE = 0.125
NEGATIVE = -1e30
LANES = 128
TAIL = 16
AXES = ("segment", "blk", "mp")

F32 = jnp.float32
BF16 = jnp.bfloat16


def from_behind(x, axis, by):
    size = lax.axis_size(axis)
    pairs = [(i, i + by) for i in range(size) if 0 <= i + by < size]
    return lax.ppermute(x, axis, pairs)


def normalize(states, gain_row):
    widened = states.astype(jnp.float32)
    spread = jnp.sqrt(jnp.mean(widened * widened, axis=-1, keepdims=True) + EPSILON)
    return ((widened / spread * gain_row).astype(jnp.bfloat16), spread)


def right_product(left, right):
    return lax.dot_general(
        left, right, (((1,), (1,)), ((), ())), preferred_element_type=jnp.float32
    )


def per_device_windows(segment_in, norm_gains, projections, live_counts, cotangent):
    segment_pos = lax.axis_index("segment")
    model_index = lax.axis_index("mp")
    states = segment_in[0]
    gain_row = norm_gains[0]
    row_count, full_width = states.shape
    feature_width = cotangent.shape[1]
    w_primary = projections[0, :, 0, :]
    w_secondary = projections[0, :, 1, :]
    group_width = w_primary.shape[1]
    group_heads = group_width // DH
    normed, spread = normalize(states, gain_row)
    primary = jnp.dot(normed, w_primary, preferred_element_type=jnp.float32).astype(jnp.bfloat16)
    secondary = lax.cond(
        segment_pos == 0,
        lambda: jnp.dot(normed, w_secondary, preferred_element_type=jnp.float32).astype(
            jnp.bfloat16
        ),
        lambda: jnp.zeros_like(primary),
    )
    doc_keys, doc_values = from_behind((primary, secondary), "segment", 1)
    own_block = (doc_keys, doc_values, live_counts[0])
    window = [own_block]
    moving = own_block
    for _ in range(1, WIN):
        moving = from_behind((moving[0], moving[1], moving[2]), "blk", 1)
        window.append(moving)
    position = jnp.arange(row_count, dtype=jnp.int32)
    all_keys = jnp.concatenate([piece[0] for piece in window], 0).reshape(
        WIN * row_count, group_heads, DH
    )
    all_values = jnp.concatenate([piece[1] for piece in window], 0).reshape(
        WIN * row_count, group_heads, DH
    )
    key_live = jnp.concatenate([position < piece[2][0] for piece in window], 0)
    query_live = position < live_counts[1][0]
    query_heads = primary.reshape(row_count, group_heads, DH)
    scores = (
        jnp.einsum("qhd,khd->hqk", query_heads, all_keys, preferred_element_type=jnp.float32)
        * SCALE
    )
    scores = jnp.where(key_live[None, None, :], scores, NEGATIVE)
    row_max = jnp.max(scores, axis=-1, keepdims=True)
    expo = jnp.exp(scores - row_max)
    row_total = jnp.sum(expo, axis=-1, keepdims=True)
    softmax_out = expo / row_total
    weights_low = softmax_out.astype(jnp.bfloat16)
    attended = jnp.einsum(
        "hqk,khd->qhd", weights_low, all_values, preferred_element_type=jnp.float32
    ).astype(jnp.bfloat16)
    attended = jnp.where(query_live[:, None, None], attended, jnp.zeros_like(attended)).reshape(
        row_count, group_width
    )
    projected = lax.cond(
        segment_pos == 1,
        lambda: right_product(attended, w_secondary),
        lambda: jnp.zeros((row_count, full_width), jnp.float32),
    )
    layer_out = lax.psum_scatter(
        projected.astype(jnp.bfloat16), "mp", scatter_dimension=1, tiled=True
    )
    own_normed = lax.dynamic_slice_in_dim(normed, model_index * feature_width, feature_width, 1)
    segment_out = jnp.where(segment_pos == 0, own_normed, layer_out)[None]
    grad_out = jnp.dot(
        lax.all_gather(cotangent, "mp", axis=1, tiled=True),
        w_secondary,
        preferred_element_type=jnp.float32,
    )
    grad_out = grad_out.astype(jnp.bfloat16)
    grad_out = jnp.where(query_live[:, None], grad_out, jnp.zeros_like(grad_out))
    grad_heads = grad_out.reshape(row_count, group_heads, DH)
    grad_probs = jnp.einsum(
        "qhd,khd->hqk", grad_heads, all_values, preferred_element_type=jnp.float32
    )
    row_delta = jnp.sum(softmax_out * grad_probs, axis=-1, keepdims=True)
    grad_scores = (softmax_out * (grad_probs - row_delta)).astype(jnp.bfloat16)
    grad_queries = (
        (
            SCALE
            * jnp.einsum("hqk,khd->qhd", grad_scores, all_keys, preferred_element_type=jnp.float32)
        )
        .astype(jnp.bfloat16)
        .reshape(row_count, group_width)
    )
    key_parts = (
        SCALE
        * jnp.einsum("hqk,qhd->khd", grad_scores, query_heads, preferred_element_type=jnp.float32)
    ).reshape(WIN, row_count, group_width)
    value_parts = jnp.einsum(
        "hqk,qhd->khd", weights_low, grad_heads, preferred_element_type=jnp.float32
    ).reshape(WIN, row_count, group_width)
    key_total = key_parts[WIN - 1]
    value_total = value_parts[WIN - 1]
    for offset in range(WIN - 2, -1, -1):
        arrived = (
            from_behind(key_total.astype(jnp.bfloat16), "blk", -1).astype(key_total.dtype),
            from_behind(value_total.astype(jnp.bfloat16), "blk", -1).astype(value_total.dtype),
        )
        key_total = arrived[0] + key_parts[offset]
        value_total = arrived[1] + value_parts[offset]
    grad_keys = key_total.astype(jnp.bfloat16)
    grad_values = value_total.astype(jnp.bfloat16)
    back_keys, back_values = from_behind((grad_keys, grad_values), "segment", -1)
    partial_grad = lax.cond(
        segment_pos == 0,
        lambda: right_product(back_keys, w_primary) + right_product(back_values, w_secondary),
        lambda: right_product(grad_queries, w_primary),
    )
    widened = states.astype(jnp.float32)
    summed = lax.psum_scatter(
        partial_grad.astype(jnp.bfloat16), "mp", scatter_dimension=1, tiled=True
    ).astype(jnp.float32)
    own_states = lax.dynamic_slice_in_dim(widened, model_index * feature_width, feature_width, 1)
    own_gain = lax.dynamic_slice_in_dim(gain_row, model_index * feature_width, feature_width, 0)
    row_term = lax.psum(jnp.sum(summed * own_gain * own_states, axis=-1, keepdims=True), "mp")
    input_grad = (
        own_gain * summed / spread - own_states * row_term / (full_width * spread**3)
    ).astype(jnp.bfloat16)
    return (segment_out, input_grad[None])


def place(sizes):
    seg = lax.axis_index("segment")
    return seg, seg * sizes[1] + lax.axis_index("blk"), lax.axis_index("mp")


def enter_kernel(sizes, states, gain, w, *rest):
    n_mp = sizes[2]
    wp, ws = rest[0], rest[1 : 1 + n_mp]
    own, own_states, own_gain, spread, prim, sec = rest[1 + n_mp : 7 + n_mp]
    xbuf, gbuf, wbuf, normed, sems, ready = rest[7 + n_mp :]
    seg, _, model = place(sizes)
    rows, width = xbuf.shape
    depth = width // n_mp
    tiles = wp.shape[2] // LANES
    pack = 2 * tiles
    group = 2 * LANES // pack
    lines = depth * pack
    first_copies = [
        pltpu.make_async_copy(states, xbuf, ready.at[0]),
        pltpu.make_async_copy(gain, gbuf, ready.at[1]),
    ]
    copies = []
    for c in range(n_mp):
        start = pl.multiple_of(jnp.bitwise_xor(model, c) * lines, lines)
        copies.append(
            pltpu.make_async_copy(
                w.at[pl.ds(start, lines), :], wbuf.at[pl.ds(c * lines, lines), :], sems.at[c]
            )
        )
    for copy in first_copies + copies:
        copy.start()
    here = lax.broadcasted_iota(jnp.int32, (2 * LANES, 2 * LANES), 0)
    there = lax.broadcasted_iota(jnp.int32, (2 * LANES, 2 * LANES), 1)
    source = pack * lax.rem(here, group) + lax.div(here, group)
    mix = jnp.where(there == source, 1.0, 0.0).astype(BF16)
    part_rows = 16

    def norm_rows(first):
        line = slice(first, first + part_rows)
        wide = xbuf[line, :].astype(F32)
        mean = jnp.sum(wide * wide, axis=1, keepdims=True) * (1.0 / width)
        root = jnp.sqrt(mean + EPSILON)
        normed[line, :] = (wide * (1.0 / root) * gbuf[...]).astype(BF16)
        spread[line, :] = jnp.broadcast_to(root, (part_rows, LANES))

    for copy in first_copies:
        copy.wait()
    pairs = depth // (2 * group)
    every = n_mp * pairs * part_rows // rows
    for c in range(n_mp):
        copies[c].wait()
        for pair in range(pairs):
            if (c * pairs + pair) % every == 0:
                norm_rows((c * pairs + pair) // every * part_rows)
            base = c * lines + pair * 4 * LANES
            left = wbuf[base : base + 2 * LANES, :]
            right = wbuf[base + 2 * LANES : base + 4 * LANES, :]
            both = jnp.concatenate([left, right], axis=1)
            ordered = jnp.dot(mix, both, preferred_element_type=F32).astype(BF16)
            first = 2 * pair * group
            for slot in range(pack):
                target = (wp.at[c], ws[c])[slot % 2]
                tile = slice(slot // 2 * LANES, (slot // 2 + 1) * LANES)
                part = ordered[slot * group : (slot + 1) * group, :]
                target[first : first + group, tile] = part[:, :LANES]
                target[first + group : first + 2 * group, tile] = part[:, LANES:]

    def product(weights):
        total = None
        for c in range(n_mp):
            span = pl.ds(pl.multiple_of(jnp.bitwise_xor(model, c) * depth, depth), depth)
            term = jnp.dot(normed[:, span], weights(c), preferred_element_type=F32)
            total = term if total is None else total + term
        return total.astype(BF16)

    prim[...] = product(lambda c: wp[c])

    @pl.when(seg == 0)
    def _():
        sec[...] = product(lambda c: ws[c][...])

    mine = pl.ds(pl.multiple_of(model * depth, depth), depth)
    own[...] = normed[:, mine]
    own_states[...] = xbuf[:, mine]
    own_gain[...] = gbuf[:, mine]


def marks_kernel(counts, alive, tail):
    line = lax.broadcasted_iota(jnp.int32, alive.shape, 0)
    last = jnp.where(lax.axis_index("segment") == 0, alive.shape[0], counts[0, 1])
    alive[...] = jnp.where(line < last, 1.0, 0.0)
    tail[...] = (jnp.full(tail.shape, 1.0, F32) * counts[0, 0].astype(F32)).astype(BF16)


def lend_kernel(w2, middle, edge):
    parity = lax.rem(lax.axis_index("blk"), 2)
    depth, quarter = w2.shape[0], edge.shape[0]
    middle[...] = w2[quarter : depth - quarter, :]
    start = pl.multiple_of(parity * (depth - quarter), quarter)
    edge[...] = w2[pl.ds(start, quarter), :]


def part_kernel(c0, c1, c2, w0, w1, w2, acc):
    @pl.when(lax.axis_index("segment") == 1)
    def _():
        acc[...] = jnp.dot(c0[...], w0[...], preferred_element_type=F32)
        acc[...] += jnp.dot(c1[...], w1[...], preferred_element_type=F32)
        acc[...] += jnp.dot(c2[...], w2[...], preferred_element_type=F32)


def pack_kernel(sizes, prim, sec, acc, alive, tail, c3, w3, *rest):
    heads = sizes[0] * sizes[1]
    second, outs, (parts,) = rest[0], rest[1 : 1 + heads], rest[1 + heads :]
    seg, entry, _ = place(sizes)
    rows = prim.shape[0]

    @pl.when(seg == 0)
    def _():
        second[...] = sec[...]

    @pl.when(seg == 1)
    def _():
        total = acc[...] + jnp.dot(c3[...], w3[...], preferred_element_type=F32)
        for tile in range(total.shape[1] // LANES):
            cols = slice(tile * LANES, (tile + 1) * LANES)
            second[:, cols] = jnp.where(alive[...] > 0.0, total[:, cols], 0.0).astype(BF16)

    for head in range(heads):
        cols = slice(head * DH, (head + 1) * DH)
        parts[head] = jnp.concatenate([prim[:, cols], second[:, cols]], axis=1)
    for k, out in enumerate(outs):
        out[:rows, :] = parts[jnp.bitwise_xor(entry, k)]
        out[rows:, :] = tail[...]


def live_keys(piece, rows):
    position = lax.broadcasted_iota(jnp.int32, (1, rows), 1).astype(F32)
    count = piece[rows : rows + 1, :].astype(F32)
    return position < jnp.concatenate([count] * (rows // LANES), axis=1)


def attend_kernel(sizes, *rest):
    heads = sizes[0] * sizes[1]
    blocks = sizes[1]
    ins, outs = rest[:heads], rest[heads : 2 * heads]
    parts, back, totals = rest[2 * heads :]
    _, entry, _ = place(sizes)
    rows = outs[0].shape[0]
    for k, piece in enumerate(ins):
        parts[jnp.bitwise_xor(entry, k)] = piece[...]
    low = lax.broadcasted_iota(jnp.int32, (rows, LANES), 1) < DH
    zero = jnp.zeros((rows, LANES), BF16)
    live = [live_keys(parts[j], rows) for j in range(blocks)]
    for i in range(blocks):
        both = parts[blocks + i, :rows, :]
        query = jnp.where(low, both * BF16(SCALE), zero)
        grad = jnp.where(low, zero, both)
        flip_query = query.astype(F32).T.astype(BF16)
        flip_grad = grad.astype(F32).T.astype(BF16)
        scores = []
        for j in range(i + 1):
            product = right_product(query, parts[j, :rows, :])
            scores.append(jnp.where(live[j], product, NEGATIVE))
        top = jnp.max(functools.reduce(jnp.maximum, scores), axis=1, keepdims=True)
        expo = [jnp.exp(s - top) for s in scores]
        total = jnp.sum(functools.reduce(jnp.add, expo), axis=1, keepdims=True)
        share = 1.0 / total
        probs = [e * share for e in expo]
        slopes = [right_product(grad, parts[j, :rows, :]) for j in range(i + 1)]
        delta = functools.reduce(jnp.add, [p * g for p, g in zip(probs, slopes)])
        delta = jnp.sum(delta, axis=1, keepdims=True)
        out = jnp.zeros((rows, LANES), F32)
        other = jnp.zeros((rows, LANES), F32)
        for j in range(i + 1):
            prob = probs[j].astype(BF16)
            slope = (probs[j] * (slopes[j] - delta)).astype(BF16)
            other += jnp.dot(slope, parts[j, :rows, :], preferred_element_type=F32)
            out += jnp.dot(prob, parts[j, :rows, :], preferred_element_type=F32)
            tall = jnp.dot(flip_query, slope, preferred_element_type=F32)
            tall += jnp.dot(flip_grad, prob, preferred_element_type=F32)
            if i == j:
                totals[j] = tall
            else:
                totals[j] += tall
        back[blocks + i] = jnp.where(low, other * SCALE, out).astype(BF16)
    for j in range(blocks):
        back[j] = totals[j].T.astype(BF16)
    for k, out in enumerate(outs):
        out[...] = back[jnp.bitwise_xor(entry, k)]


def split_rows(column):
    row = jnp.broadcast_to(column, (column.shape[0], LANES)).T[:TAIL, :]
    high = row.astype(BF16).astype(F32)
    line = lax.broadcasted_iota(jnp.int32, row.shape, 0)
    return jnp.where(line == 0, high, row - high).astype(BF16)


def regroup(sizes, ins, parts):
    heads = sizes[0] * sizes[1]
    _, entry, _ = place(sizes)
    for k, piece in enumerate(ins):
        parts[jnp.bitwise_xor(entry, k)] = piece[...]
    for head in range(0, heads, 2):
        yield slice(head * DH, (head + 2) * DH), parts[head], parts[head + 1]


def attended_kernel(sizes, alive, *rest):
    heads = sizes[0] * sizes[1]
    ins, (ls, parts) = rest[:heads], rest[heads:]
    for cols, one, two in regroup(sizes, ins, parts):
        both = jnp.concatenate([one[:, DH:], two[:, DH:]], axis=1)
        ls[:, cols] = jnp.where(alive[...] > 0.0, both.astype(F32), 0.0).astype(BF16)


def project_block(seg, wp, ws, lp, ls, out, slot):
    rows = lp.shape[0]

    @pl.when(seg == 0)
    def _():
        total = right_product(lp[...], wp) + right_product(ls[...], ws)
        out[slot, :rows, :] = total.astype(BF16)

    @pl.when(seg == 1)
    def _():
        out[slot, :rows, :] = right_product(lp[...], wp).astype(BF16)


def send_kernel(sizes, ls, prim, second, spread, wp, w3, w1, *rest):
    heads = sizes[0] * sizes[1]
    ins, (sent, lp, parts) = rest[:heads], rest[heads:]
    for cols, one, two in regroup(sizes, ins, parts):
        lp[:, cols] = jnp.concatenate([one[:, :DH], two[:, :DH]], axis=1)
    seg, _, _ = place(sizes)
    rows, feats = prim.shape[0], sent.shape[2]
    project_block(seg, wp[3], w3[...], lp, ls, sent, 0)
    project_block(seg, wp[1], w1[...], lp, ls, sent, 1)
    term = lp[...].astype(F32) * prim[...].astype(F32)
    also = ls[...].astype(F32) * second[...].astype(F32)
    term = term + jnp.where(seg == 0, also, 0.0)
    column = jnp.sum(term, axis=1, keepdims=True) * spread[:, :1]
    sent[0, rows:, :] = jnp.zeros((TAIL, feats), BF16)
    sent[1, rows:, :] = jnp.zeros((TAIL, feats), BF16)
    sent[0, rows:, :rows] = split_rows(column)


def keep_kernel(sizes, lp, ls, wp, w2, w0, kept):
    seg, _, _ = place(sizes)
    project_block(seg, wp[2], w2[...], lp, ls, kept, 0)
    project_block(seg, wp[0], w0[...], lp, ls, kept, 1)


def layer_kernel(a0, a1, a2, a3, w0, w1, middle, edge, mirrored, w3, own, out, obuf, w2, sem):
    seg = lax.axis_index("segment")

    @pl.when(seg == 0)
    def _():
        obuf[...] = own[...]

    @pl.when(seg == 1)
    def _():
        parity = lax.rem(lax.axis_index("blk"), 2)
        depth, quarter = w2.shape[0], edge.shape[0]
        for lent, side in ((edge, parity), (mirrored, 1 - parity)):
            start = pl.multiple_of(side * (depth - quarter), quarter)
            w2[pl.ds(start, quarter), :] = lent[...]
        w2[quarter : depth - quarter, :] = middle[...]
        total = right_product(a0[...], w0[...])
        for a, w in ((a1, w1), (a2, w2), (a3, w3)):
            total += right_product(a[...], w[...])
        obuf[...] = total.astype(BF16)

    leaving = pltpu.make_async_copy(obuf, out, sem)
    leaving.start()
    leaving.wait()


def fold_kernel(kept, got, sent, top, bottom, ends):
    rows = kept.shape[1]
    for out, line in ((top, slice(0, rows // 2)), (bottom, slice(rows // 2, rows))):
        out[...] = (kept[0, line, :].astype(F32) + got[0, line, :].astype(F32)).astype(BF16)
    mine = sent[0, rows:, :rows].astype(F32)
    theirs = got[0, rows:, :rows].astype(F32)
    total = mine[0:1] + mine[1:2] + theirs[0:1] + theirs[1:2]
    ends[...] = jnp.broadcast_to(total, ends.shape)


ANYWHERE = pl.BlockSpec(memory_space=pltpu.HBM)
INSIDE = pl.BlockSpec(memory_space=pltpu.VMEM)
SCALARS = pl.BlockSpec(memory_space=pltpu.SMEM)


def call(body, ins, specs, outs, scratch=(), limit=16, flops=0, out_specs=None):
    inside = out_specs is None
    ins = [
        pltpu.with_memory_space_constraint(x, pltpu.HBM) if spec is ANYWHERE else x
        for x, spec in zip(ins, specs)
    ]
    return pl.pallas_call(
        body,
        in_specs=list(specs),
        out_specs=[INSIDE] * len(outs) if inside else out_specs,
        out_shape=[(pltpu.VMEM if inside else jax.ShapeDtypeStruct)(s, d) for s, d in outs],
        scratch_shapes=list(scratch),
        compiler_params=pltpu.CompilerParams(vmem_limit_bytes=limit << 20),
        cost_estimate=pl.CostEstimate(flops=flops, transcendentals=0, bytes_accessed=1 << 20),
    )(*ins)


def scales_kernel(width, spread, inverse, shrink):
    root = spread[...]
    inverse[...] = 1.0 / root
    shrink[...] = 1.0 / (width * root * root * root)


def leave_rows(first, kept, got, ends, far_ends, far, states, gain, inverse, shrink):
    rows, size = states.shape[0], far.shape[0]
    line = slice(first, first + size)
    row = ends[...] + far_ends[...]
    term = jnp.broadcast_to(row[:1], (LANES, rows)).T[line, :1]
    scaled = term * shrink[line, :1]
    total = kept[1, line, :].astype(F32) + got[1, line, :].astype(F32) + far[...].astype(F32)
    direct = gain[...] * total * inverse[line, :1]
    return (direct - states[line, :].astype(F32) * scaled).astype(BF16)


def leave_top_kernel(*refs):
    refs[-1][...] = leave_rows(0, *refs[:-1])


def leave_kernel(top, *refs):
    ins, (grad, obuf, sems) = refs[:-3], refs[-3:]
    size = top.shape[0]
    early = pltpu.make_async_copy(top, grad.at[:size, :], sems.at[0])
    early.start()
    obuf[...] = leave_rows(size, *ins)
    late = pltpu.make_async_copy(obuf, grad.at[size:, :], sems.at[1])
    late.start()
    early.wait()
    late.wait()


def per_device_heads(sizes, segment_in, norm_gains, projections, live_counts, cotangent):
    n_seg, n_blk, n_mp = sizes
    heads = n_seg * n_blk
    states = segment_in[0]
    rows, width = states.shape
    feats = cotangent.shape[1]
    group = projections.shape[3]
    counts = live_counts.T

    def swap(x, over_heads, over_mp):
        pairs = [
            (e * n_mp + m, (e ^ over_heads) * n_mp + (m ^ over_mp))
            for e in range(heads)
            for m in range(n_mp)
        ]
        return lax.ppermute(x, AXES, pairs)

    def exchange(pieces):
        moved = [pieces[0]]
        for k in range(1, heads):
            moved.append(swap(pieces[k], k, 0))
        return moved

    far_cot = swap(cotangent, 0, 2)
    near_cot = swap(cotangent, 0, 1)
    tiles = group // LANES
    mixed = projections.reshape(width, 2, tiles, LANES).transpose(0, 2, 1, 3)
    mixed = mixed.reshape(width * 2 * tiles, LANES)
    made = call(
        functools.partial(enter_kernel, sizes),
        (states, norm_gains, mixed),
        [ANYWHERE] * 3,
        [((n_mp, feats, group), BF16)]
        + [((feats, group), BF16)] * n_mp
        + [
            ((rows, feats), BF16),
            ((rows, feats), BF16),
            ((1, feats), F32),
            ((rows, LANES), F32),
            ((rows, group), BF16),
            ((rows, group), BF16),
        ],
        [
            pltpu.VMEM((rows, width), BF16),
            pltpu.VMEM((1, width), F32),
            pltpu.VMEM((width * 2 * tiles, LANES), BF16),
            pltpu.VMEM((rows, width), BF16),
            pltpu.SemaphoreType.DMA((n_mp,)),
            pltpu.SemaphoreType.DMA((2,)),
        ],
        24,
        8 << 30,
    )
    wp, ws = made[0], made[1 : 1 + n_mp]
    own, own_states, own_gain, spread, prim, sec = made[1 + n_mp :]
    alive, tail = call(
        marks_kernel, (counts,), [SCALARS], [((rows, LANES), F32), ((TAIL, LANES), BF16)]
    )
    quarter = feats // 4
    middle, edge = call(
        lend_kernel,
        (ws[2],),
        [INSIDE],
        [((feats - 2 * quarter, group), BF16), ((quarter, group), BF16)],
    )
    lent_3 = swap(ws[3], 0, 3)
    far_cot, spread = lax.optimization_barrier((far_cot, spread))
    cross_cot = swap(far_cot, 0, 1)
    acc = call(
        part_kernel,
        (cotangent, near_cot, far_cot, *ws[:3]),
        [INSIDE] * 6,
        [((rows, group), F32)],
        (),
        16,
        1 << 30,
    )[0]
    made = call(
        functools.partial(pack_kernel, sizes),
        (prim, sec, acc, alive, tail, cross_cot, ws[3]),
        [INSIDE] * 7,
        [((rows, group), BF16)] + [((rows + TAIL, LANES), BF16)] * heads,
        [pltpu.VMEM((heads, rows, LANES), BF16)],
        16,
        1 << 30,
    )
    second, pieces = made[0], made[1:]
    pieces = exchange(pieces)
    lent_2 = swap(middle, 0, 2)
    lent_edge = swap(edge, 0, 2)
    inverse, shrink = call(
        functools.partial(scales_kernel, width), (spread,), [INSIDE], [((rows, LANES), F32)] * 2
    )
    pieces = call(
        functools.partial(attend_kernel, sizes),
        pieces,
        [INSIDE] * heads,
        [((rows, LANES), BF16)] * heads,
        [
            pltpu.VMEM((heads, rows + TAIL, LANES), BF16),
            pltpu.VMEM((heads, rows, LANES), BF16),
            pltpu.VMEM((n_blk, LANES, rows), F32),
        ],
        24,
        4 << 30,
    )
    pieces = exchange(pieces)
    (ls,) = call(
        functools.partial(attended_kernel, sizes),
        (alive, *pieces),
        [INSIDE] * (1 + heads),
        [((rows, group), BF16)],
        [pltpu.VMEM((heads, rows, LANES), BF16)],
    )
    far_att = swap(ls, 0, 2)
    sent, lp = call(
        functools.partial(send_kernel, sizes),
        (ls, prim, second, spread, wp, ws[3], ws[1], *pieces),
        [INSIDE] * (7 + heads),
        [((2, rows + TAIL, feats), BF16), ((rows, group), BF16)],
        [pltpu.VMEM((heads, rows, LANES), BF16)],
        16,
        2 << 30,
    )
    got = swap(sent, 0, 1)
    mirrored = swap(lent_edge, 1, 0)
    (kept,) = call(
        functools.partial(keep_kernel, sizes),
        (lp, ls, wp, ws[2], ws[0]),
        [INSIDE] * 5,
        [((2, rows, feats), BF16)],
        (),
        16,
        2 << 30,
    )
    top, bottom, ends = call(
        fold_kernel,
        (kept, got, sent),
        [INSIDE] * 3,
        [((rows // 2, feats), BF16)] * 2 + [((8, rows), F32)],
    )
    far_top = swap(top, 0, 2)
    far_bottom = swap(bottom, 0, 2)
    far_ends = swap(ends, 0, 2)
    own_att, lent_1, ends = lax.optimization_barrier((ls, ws[1], ends))
    lent_1 = swap(lent_1, 0, 1)
    near_att = swap(own_att, 0, 1)
    cross_att = swap(far_att, 0, 1)
    (out,) = call(
        layer_kernel,
        (
            *(ls, near_att, far_att, cross_att),
            *(ws[0], lent_1, lent_2, lent_edge, mirrored, lent_3, own),
        ),
        [INSIDE] * 11,
        [((rows, feats), BF16)],
        [
            pltpu.VMEM((rows, feats), BF16),
            pltpu.VMEM((feats, group), BF16),
            pltpu.SemaphoreType.DMA,
        ],
        16,
        2 << 30,
        [ANYWHERE],
    )
    (leave_top,) = call(
        leave_top_kernel,
        (kept, got, ends, far_ends, far_top, own_states, own_gain, inverse, shrink),
        [INSIDE] * 9,
        [((rows // 2, feats), BF16)],
    )
    (grad,) = call(
        leave_kernel,
        (
            *(leave_top, kept, got, ends, far_ends, far_bottom),
            *(own_states, own_gain, inverse, shrink),
        ),
        [INSIDE] * 10,
        [((rows, feats), BF16)],
        [pltpu.VMEM((rows // 2, feats), BF16), pltpu.SemaphoreType.DMA((2,))],
        out_specs=[ANYWHERE],
    )
    return (out[None], grad[None])


def solution(mesh):
    sizes = tuple(mesh.shape[axis] for axis in AXES)
    n_seg, n_blk, n_mp = sizes
    by_heads = n_seg == 2 and n_blk <= WIN and n_blk & (n_blk - 1) == 0 and n_blk > 1 and n_mp == 4

    def body(segment_in, norm_gains, projections, live_counts, cotangent):
        rows, group = segment_in.shape[1], projections.shape[3]
        if by_heads:
            assert n_seg * n_blk * DH == group and group == 4 * LANES and rows % LANES == 0
            return per_device_heads(
                sizes, segment_in, norm_gains, projections, live_counts, cotangent
            )
        return per_device_windows(segment_in, norm_gains, projections, live_counts, cotangent)

    in_specs = (
        P("segment", "blk", None),
        P("segment", None),
        P("segment", None, None, "mp"),
        P(None, "blk"),
        P("blk", "mp"),
    )
    out_specs = (P("segment", "blk", "mp"), P("segment", "blk", "mp"))
    return jax.shard_map(body, mesh=mesh, in_specs=in_specs, out_specs=out_specs, check_vma=False)
```
